32 devices in a mesh: clus: 8 (over z, core), lvl: 4 (over y, x).
Axes of the slice: x: 2, y: 2, z: 4, core: 2. Of those that a mesh axis runs over, the one named last changes fastest.
Arguments:
- krylov_basis: float32 [8, 4, 2048], P(None, 'lvl', 'clus'), may hold values from -90 to 90
- near_block: bfloat16 [4, 8, 4, 256, 256], P('lvl', 'clus'), may hold values from -1 to 2.5
- near_col: int32 [4, 8, 4], P('lvl', 'clus'), may hold values from 0 to 7, as said below
- near_count: int32 [4, 8], P('lvl', 'clus'), may hold values from 1 to 4, as said below
- far_col: int32 [4, 8, 6], P('lvl', 'clus'), may hold values from 0 to 7, as said below
- v_basis: bfloat16 [4, 8, 32, 256], P('lvl', 'clus'), may hold values from -0.375 to 0.375
- u_basis: bfloat16 [4, 8, 32, 256], P('lvl', 'clus'), may hold values from -1 to 1
- far_coupling: float32 [4, 8, 6, 32, 32], P('lvl', 'clus'), may hold values from -0.4375 to 0.4375
- transfer: float32 [4, 8, 32, 32], P('lvl', 'clus'), may hold values from -1 to 1
- top_coupling: float32 [4, 8, 4, 32, 32], P('lvl', 'clus'), may hold values from -0.5 to 0.5
Outputs:
- q_next: float32 [4, 4, 2048], P(None, 'lvl', 'clus')
- coeffs: float32 [2, 12, 4], replicated
The draws below stay inside these ranges and needn't reach their ends.
Inputs may be any that keep to these rules, and one draw needn't show every extreme that they name: `near_col`: slot 0 of every leaf names the leaf itself; every other slot names leaf i - 1 or leaf i + 1 of the same subtree. Slots at or beyond the leaf's near_count name such leaves too, and their blocks are ignored. `near_count`: in some aligned run of 1 leaves every leaf has 4. `far_col`: A partner lies in the same subtree, in an aligned run of 1 leaves other than the leaf's own. Slot 0 names a leaf of the run just before the leaf's own, runs counted cyclically within the subtree.
All inputs are finite; a program needn't handle non-finite values.
Results may differ from the reference program's by a relative error of at most 0.00037.
Values may be sent and summed in bfloat16 or wider, within the bound.
No kernel may reach another device: no remote copies, remote signals or barrier semaphores. Data moves between devices by JAX's collectives and lax.ppermute only.
A program may use at most 64 MiB of HBM per device.

```python
import jax
import jax.numpy as jnp
from jax import lax

LEAF = 256
RANK = 32
VECS = 4
NEAR_SLOTS = 4
FAR_SLOTS = 6
STEPS = 2
LEAVES_DEV = 1
BASIS = 8
SUBTREES = 4
CLUSTERS = 8
SUB_LEAVES = 8
SUB_ROWS = 2048
ROWS = 8192


def draw_krylov_basis(key, part):
    noise_key, scale_key = jax.random.split(key, 2)
    leaf_total = SUBTREES * SUB_LEAVES
    position = jnp.arange(leaf_total, dtype=jnp.float32) / leaf_total
    jitter = jnp.exp(jax.random.uniform(scale_key, (leaf_total,), minval=0.0, maxval=jnp.log(3.0)))
    random_part = jnp.clip(jax.random.normal(noise_key, (BASIS, leaf_total, LEAF)), -6.0, 6.0)
    row_scale = jnp.exp(position * jnp.log(3.0)) * jitter
    values = random_part * row_scale[None, :, None]
    return values.reshape(BASIS, SUBTREES, SUB_ROWS).astype(jnp.float32)


def draw_near_block(key, part):
    spread = (LEAF * NEAR_SLOTS) ** (-0.5)
    identity = jnp.eye(LEAF, dtype=jnp.float32)
    first_slot = (jnp.arange(NEAR_SLOTS) == 0).astype(jnp.float32)

    def one_tree(tree_index):
        tree_key = jax.random.fold_in(key, tree_index)
        full_shape = (SUB_LEAVES, NEAR_SLOTS, LEAF, LEAF)
        random_part = jnp.clip(jax.random.normal(tree_key, full_shape), -6.0, 6.0)
        values = random_part * spread + 1.5 * first_slot[None, :, None, None] * identity
        return values.astype(jnp.bfloat16)
    return lax.map(one_tree, jnp.arange(SUBTREES, dtype=jnp.int32))


def near_tables(key):
    pick_key = jax.random.fold_in(key, 11)
    heavy_key = jax.random.fold_in(key, 12)
    forced_key = jax.random.fold_in(key, 13)
    light_key = jax.random.fold_in(key, 14)
    leaf_ids = jnp.arange(SUB_LEAVES, dtype=jnp.int32)
    run_start = leaf_ids // LEAVES_DEV * LEAVES_DEV
    window_low = jnp.maximum(run_start - LEAVES_DEV, 0)
    window_high = jnp.minimum(run_start + 2 * LEAVES_DEV, SUB_LEAVES)
    window_size = window_high - window_low
    chosen = jax.random.randint(pick_key, (SUBTREES, SUB_LEAVES, NEAR_SLOTS), 0, (window_size - 1)[None, :, None])
    candidate = window_low[None, :, None] + chosen
    candidate = candidate + (candidate >= leaf_ids[None, :, None]).astype(jnp.int32)
    self_slot = (jnp.arange(NEAR_SLOTS, dtype=jnp.int32) == 0)[None, None, :]
    partner_cols = jnp.where(self_slot, leaf_ids[None, :, None], candidate).astype(jnp.int32)
    run_count = SUBTREES * (SUB_LEAVES // LEAVES_DEV)
    heavy_run = jax.random.randint(heavy_key, (run_count,), 0, 8) == 0
    forced = jax.random.randint(forced_key, (), 0, run_count)
    heavy_run = heavy_run | (jnp.arange(run_count, dtype=jnp.int32) == forced)
    light_count = jax.random.randint(light_key, (SUBTREES, SUB_LEAVES), 1, NEAR_SLOTS + 1)
    heavy_leaf = jnp.repeat(heavy_run, LEAVES_DEV).reshape(SUBTREES, SUB_LEAVES)
    live_count = jnp.where(heavy_leaf, NEAR_SLOTS, light_count).astype(jnp.int32)
    return (partner_cols, live_count)


def draw_near_col(key, part):
    return near_tables(key)[0]


def draw_near_count(key, part):
    return near_tables(key)[1]


def draw_far_col(key, part):
    hop_key, inside_key = jax.random.split(key)
    run_total = SUB_LEAVES // LEAVES_DEV
    leaf_ids = jnp.arange(SUB_LEAVES, dtype=jnp.int32)
    home_run = leaf_ids // LEAVES_DEV
    full_shape = (SUBTREES, SUB_LEAVES, FAR_SLOTS)
    run_hop = jax.random.randint(hop_key, full_shape, 1, run_total)
    first_slot = (jnp.arange(FAR_SLOTS, dtype=jnp.int32) == 0)[None, None, :]
    run_hop = jnp.where(first_slot, run_total - 1, run_hop)
    target = (home_run[None, :, None] + run_hop) % run_total
    inside = jax.random.randint(inside_key, full_shape, 0, LEAVES_DEV)
    return (target * LEAVES_DEV + inside).astype(jnp.int32)


def shard_levels(key, extent, cuts, low, high):
    gain, own = 1.0, jax.random.fold_in(key, 6)
    for axis_at, shards_of in cuts:
        heights = jnp.exp(jax.random.uniform(jax.random.fold_in(own, axis_at), (shards_of,), jnp.float32, low / len(cuts), high / len(cuts)))
        gain = gain * jnp.repeat(heights, extent[axis_at] // shards_of).reshape([-1 if axis == axis_at else 1 for axis in range(len(extent))])
    return gain


def centred(stream_key, extent, scale, reach, cuts=(), kind=jnp.bfloat16):
    factor_of = shard_levels(stream_key, extent, cuts, -0.22, 0.18) if cuts else 1.0
    values = jax.random.normal(stream_key, extent, jnp.float32) * scale * factor_of
    return jnp.minimum(jnp.maximum(values, -reach), reach).astype(kind)


def setup_inputs(seed: int = 0) -> dict:
    keys = jax.random.split(jax.random.key(seed), 11)
    return {
        "krylov_basis": draw_krylov_basis(jax.random.fold_in(keys[10], 71), 0),
        "near_block": draw_near_block(jax.random.fold_in(keys[10], 71), 0),
        "near_col": draw_near_col(jax.random.fold_in(keys[10], 71), 0),
        "near_count": draw_near_count(jax.random.fold_in(keys[10], 71), 0),
        "far_col": draw_far_col(jax.random.fold_in(keys[10], 71), 0),
        "v_basis": centred(keys[5], (SUBTREES, SUB_LEAVES, RANK, LEAF), LEAF ** -0.5, 0.375, ((0, 4), (1, 8))),
        "u_basis": centred(keys[6], (SUBTREES, SUB_LEAVES, RANK, LEAF), RANK ** -0.5, 1.0, ((0, 4), (1, 8))),
        "far_coupling": centred(keys[7], (SUBTREES, SUB_LEAVES, FAR_SLOTS, RANK, RANK), (RANK * FAR_SLOTS) ** -0.5, 0.4375, ((0, 4), (1, 8)), jnp.float32),
        "transfer": centred(keys[8], (SUBTREES, SUB_LEAVES, RANK, RANK), (RANK * LEAVES_DEV) ** -0.5, 1.0, ((0, 4), (1, 8)), jnp.float32),
        "top_coupling": centred(keys[9], (SUBTREES, CLUSTERS, SUBTREES, RANK, RANK), (RANK * SUBTREES) ** -0.5, 0.5, ((0, 4), (1, 8)), jnp.float32),
    }


PRECISE = lax.Precision.HIGHEST

def apply_operator(current, near_block, near_col, near_count, far_col, v_basis, u_basis, far_coupling, transfer, top_coupling):
    lowered = current.astype(jnp.bfloat16)
    leaves = jnp.transpose(lowered.reshape(VECS, SUBTREES, SUB_LEAVES, LEAF), (1, 2, 0, 3))
    slot_ids = jnp.arange(NEAR_SLOTS, dtype=jnp.int32)

    def near_subtree(bundle):
        blocks, partner_cols, live_count, tree_leaves = bundle
        picked = tree_leaves[partner_cols]
        is_live = slot_ids[None, :] < live_count[:, None]
        picked = jnp.where(is_live[:, :, None, None], picked, jnp.zeros_like(picked))
        return jnp.einsum('lkpq,lkvq->lvp', blocks.astype(jnp.float32), picked.astype(jnp.float32), precision=PRECISE)
    near_part = lax.map(near_subtree, (near_block, near_col, near_count, leaves))
    skeleton = jnp.einsum('slrp,slvp->slvr', v_basis.astype(jnp.float32), leaves.astype(jnp.float32), precision=PRECISE)
    partners = jax.vmap(lambda tree_skel, tree_cols: tree_skel[tree_cols])(skeleton, far_col)
    coupled = jnp.einsum('slkqr,slkvr->slvq', far_coupling, partners, precision=PRECISE)
    clusters = SUB_LEAVES // LEAVES_DEV
    grouped = skeleton.reshape(SUBTREES, clusters, LEAVES_DEV, VECS, RANK)
    transfer_runs = transfer.reshape(SUBTREES, clusters, LEAVES_DEV, RANK, RANK)
    coarse = jnp.einsum('scuvr,scurq->scvq', grouped, transfer_runs, precision=PRECISE)
    tree_ids = jnp.arange(SUBTREES, dtype=jnp.int32)
    distinct = (tree_ids[:, None] != tree_ids[None, :])[:, None, :, None, None]
    masked_top = jnp.where(distinct, top_coupling, jnp.zeros_like(top_coupling))
    upper = jnp.einsum('sctqr,tcvr->scvq', masked_top, coarse, precision=PRECISE)
    downward = jnp.einsum('scuqr,scvr->scuvq', transfer_runs, upper, precision=PRECISE)
    coupled = coupled + downward.reshape(SUBTREES, SUB_LEAVES, VECS, RANK)
    coupled_low = coupled.astype(jnp.bfloat16)
    far_part = jnp.einsum('slvq,slqp->slvp', coupled_low.astype(jnp.float32), u_basis.astype(jnp.float32), precision=PRECISE)
    image_block = jnp.transpose(near_part + far_part, (2, 0, 1, 3))
    return image_block.reshape(VECS, SUBTREES, SUB_ROWS)

def orthogonalize(window, image_block):
    flat_window = window.reshape(BASIS, ROWS)
    flat_image = image_block.reshape(VECS, ROWS)
    projection = jnp.dot(flat_window, flat_image.T, precision=PRECISE) / ROWS
    remainder = flat_image - jnp.dot(projection.T, flat_window, precision=PRECISE)
    gram = jnp.dot(remainder, remainder.T, precision=PRECISE) / ROWS
    lower_factor = jnp.linalg.cholesky(gram)
    inverse = lax.linalg.triangular_solve(lower_factor, jnp.eye(VECS, dtype=jnp.float32), left_side=True, lower=True)
    new_block = jnp.dot(inverse, remainder, precision=PRECISE)
    record = jnp.concatenate([projection, lower_factor.T], axis=0)
    return (new_block.reshape(VECS, SUBTREES, SUB_ROWS), record)

def reference(krylov_basis, near_block, near_col, near_count, far_col, v_basis, u_basis, far_coupling, transfer, top_coupling):
    window = krylov_basis
    current = krylov_basis[VECS:]
    records = []
    for step_index in range(STEPS):
        image_block = apply_operator(current, near_block, near_col, near_count, far_col, v_basis, u_basis, far_coupling, transfer, top_coupling)
        current, record = orthogonalize(window, image_block)
        records.append(record)
        window = jnp.concatenate([window[VECS:], current], axis=0)
    return (current, jnp.stack(records))
```

```python
import jax
import jax.numpy as jnp
from jax import lax
from jax.sharding import PartitionSpec as P

LEAF = 256
RANK = 32
VECS = 4
NEAR_SLOTS = 4
FAR_SLOTS = 6
STEPS = 2
LEAVES_DEV = 1
BASIS = 8


PRECISE = lax.Precision.HIGHEST


AXES = ("clus", "lvl")


def row_products(left_rows, right_rows):
    return jnp.dot(left_rows, right_rows.T, precision=PRECISE)


def exchange(slots):
    return lax.all_to_all(slots, AXES, 0, 0, tiled=True)


def three_parts(values):
    high = lax.reduce_precision(values, 8, 7)
    rest = values - high
    middle = lax.reduce_precision(rest, 8, 7)
    low = rest - middle
    return jnp.concatenate([high, middle, low]).astype(jnp.bfloat16)


def joined_parts(parts):
    wide = parts.astype(jnp.float32)
    count = wide.shape[-1] // 3
    return wide[..., :count] + wide[..., count : 2 * count] + wide[..., 2 * count :]


def operator(
    lowered, near_block, near_col, near_count, far_col, v_basis, u_basis, far_coupling, transfer, top_coupling
):
    trees, leaves = lax.axis_size("lvl"), lax.axis_size("clus")
    own_tree, own_leaf = lax.axis_index("lvl"), lax.axis_index("clus")
    skeleton = jnp.einsum("rp,vp->vr", v_basis[0, 0], lowered, preferred_element_type=jnp.float32)
    coarse = jnp.dot(skeleton, transfer[0, 0], precision=PRECISE)
    flat = lowered.reshape(-1)
    same_tree = jnp.concatenate([flat, three_parts(skeleton.reshape(-1))])
    other_tree = jnp.concatenate([flat, three_parts(coarse.reshape(-1))])
    peers = lax.broadcasted_iota(jnp.int32, (leaves * trees, 1, 1), 0)
    slots = jnp.where(peers % trees == own_tree, same_tree[None, None], other_tree[None, None])
    arrived = exchange(slots).reshape(leaves, trees, -1)
    in_tree = lax.dynamic_index_in_dim(arrived, own_tree, 1, keepdims=False)
    across = lax.dynamic_index_in_dim(arrived, own_leaf, 0, keepdims=False)
    size = flat.shape[0]
    skeletons = joined_parts(in_tree[:, size:])
    coarses = joined_parts(across[:, size:]).reshape(trees, VECS, RANK)
    wanted = far_col[0, 0]
    matches = (wanted[:, None] == lax.broadcasted_iota(jnp.int32, (1, leaves), 1)).astype(jnp.float32)
    partners = jnp.dot(matches, skeletons, precision=PRECISE).reshape(FAR_SLOTS, VECS, RANK)
    coupled = jnp.einsum("kqr,kvr->vq", far_coupling[0, 0], partners, precision=PRECISE)
    couplings = top_coupling[0, 0]
    others = lax.broadcasted_iota(jnp.int32, (trees, 1, 1), 0) != own_tree
    couplings = jnp.where(others, couplings, jnp.zeros_like(couplings))
    upper = jnp.einsum("tqr,tvr->vq", couplings, coarses, precision=PRECISE)
    coupled = coupled + jnp.einsum("qr,vr->vq", transfer[0, 0], upper, precision=PRECISE)
    coupled_low = coupled.astype(jnp.bfloat16)
    far_part = jnp.einsum("vq,qp->vp", coupled_low, u_basis[0, 0], preferred_element_type=jnp.float32)
    blocks = in_tree[:, :size].reshape(leaves, VECS, LEAF)
    picked = jnp.take(blocks, near_col[0, 0], axis=0)
    is_live = lax.broadcasted_iota(jnp.int32, (NEAR_SLOTS, 1, 1), 0) < near_count[0, 0]
    picked = jnp.where(is_live, picked, jnp.zeros_like(picked))
    near_part = jnp.einsum("kpq,kvq->vp", near_block[0, 0], picked, preferred_element_type=jnp.float32)
    return near_part + far_part


def orthogonalize(window, image_block):
    devices = lax.axis_size("clus") * lax.axis_size("lvl")
    rows_all = float(devices * image_block.shape[1])
    pieces = (
        row_products(window, window),
        row_products(window, image_block),
        row_products(image_block, image_block),
    )
    flat = jnp.concatenate([piece.reshape(-1) for piece in pieces])
    flat = jnp.pad(flat, (0, -flat.shape[0] % 128))
    total = exchange(jnp.broadcast_to(flat, (devices, 1, flat.shape[0]))).sum((0, 1)) / rows_all
    metric = total[: BASIS * BASIS].reshape(BASIS, BASIS)
    at = BASIS * BASIS
    projection = total[at : at + BASIS * VECS].reshape(BASIS, VECS)
    at = at + BASIS * VECS
    square = total[at : at + VECS * VECS].reshape(VECS, VECS)
    remainder = image_block - jnp.dot(projection.T, window, precision=PRECISE)
    coef_cross = jnp.dot(projection.T, projection, precision=PRECISE)
    weighted = jnp.dot(
        projection.T, jnp.dot(metric, projection, precision=PRECISE), precision=PRECISE
    )
    gram = square - 2.0 * coef_cross + weighted
    lower_factor = jnp.linalg.cholesky(gram)
    inverse = lax.linalg.triangular_solve(
        lower_factor, jnp.eye(VECS, dtype=jnp.float32), left_side=True, lower=True
    )
    new_block = jnp.dot(inverse, remainder, precision=PRECISE)
    return (new_block, jnp.concatenate([projection, lower_factor.T], axis=0))


def local(
    krylov_basis,
    near_block,
    near_col,
    near_count,
    far_col,
    v_basis,
    u_basis,
    far_coupling,
    transfer,
    top_coupling,
):
    row_count = krylov_basis.shape[2]
    window = krylov_basis.reshape(BASIS, row_count)
    current = window[VECS:]
    records = []
    for step_index in range(STEPS):
        lowered = current.astype(jnp.bfloat16)
        image_block = operator(
            lowered, near_block, near_col, near_count, far_col, v_basis, u_basis, far_coupling, transfer, top_coupling
        )
        current, record = orthogonalize(window, image_block)
        records.append(record)
        window = jnp.concatenate([window[VECS:], current], axis=0)
    return (current.reshape(VECS, 1, row_count), jnp.stack(records))


def solution(mesh):
    return jax.shard_map(
        local,
        mesh=mesh,
        in_specs=(
            P(None, "lvl", "clus"),
            P("lvl", "clus", None, None, None),
            P("lvl", "clus", None),
            P("lvl", "clus"),
            P("lvl", "clus", None),
            P("lvl", "clus", None, None),
            P("lvl", "clus", None, None),
            P("lvl", "clus", None, None, None),
            P("lvl", "clus", None, None),
            P("lvl", "clus", None, None, None),
        ),
        out_specs=(P(None, "lvl", "clus"), P()),
        check_vma=False,
    )
```

```python
import functools

import jax
import jax.numpy as jnp
from jax import lax
from jax.experimental import pallas as pl
from jax.experimental.pallas import tpu as pltpu
from jax.sharding import PartitionSpec as P

VECS = 4
STEPS = 2
LANES = 128
AXES = ("clus", "lvl")

PRECISE = lax.Precision.HIGHEST
ROWS_DIMS = (((1,), (1,)), ((), ()))


def rows_dot(left, right, precision=None):
    return lax.dot_general(
        left, right, ROWS_DIMS, precision=precision, preferred_element_type=jnp.float32
    )


def three_parts(values):
    high = values.astype(jnp.bfloat16)
    rest = values - high.astype(jnp.float32)
    middle = rest.astype(jnp.bfloat16)
    low = (rest - middle.astype(jnp.float32)).astype(jnp.bfloat16)
    return high, middle, low


def tail_of(values):
    high, middle, low = three_parts(values)
    empty = jnp.zeros((VECS, LANES - 3 * values.shape[1]), jnp.float32)
    wide = [part.astype(jnp.float32) for part in (high, middle, low)]
    return jnp.concatenate(wide + [empty], axis=1).astype(jnp.bfloat16)


def over_slots(count, store):
    step = min(count, 32)
    if count == step:
        for slot in range(count):
            store(slot)
        return

    def body(at, carry):
        for inner in range(step):
            store(at * step + inner)
        return carry

    lax.fori_loop(0, count // step, body, 0)


def fill_operator_slots(slots_ref, lowered, v_basis, transfer, trees):
    size = lowered.shape[1]
    skeleton = rows_dot(lowered, v_basis)
    coarse = jnp.dot(skeleton, transfer, precision=PRECISE, preferred_element_type=jnp.float32)
    own_tree = lax.axis_index("lvl")
    tree_tail = tail_of(skeleton)
    level_tail = tail_of(coarse)

    def store(slot):
        slots_ref[slot, :, :size] = lowered
        slots_ref[slot, :, size:] = level_tail

    over_slots(slots_ref.shape[0], store)

    def store_tree(leaf):
        slots_ref[leaf * trees + own_tree, :, size:] = tree_tail

    over_slots(slots_ref.shape[0] // trees, store_tree)


def split_rows(flat_ref, rows):
    halves = flat_ref.shape[0] // rows
    return jnp.concatenate(
        [flat_ref[pl.ds(half, rows, stride=halves), :] for half in range(halves)], axis=1
    )


def store_rows(flat_ref, values):
    rows = values.shape[0]
    halves = flat_ref.shape[0] // rows
    for half in range(halves):
        flat_ref[pl.ds(half, rows, stride=halves), :] = values[:, half * LANES : (half + 1) * LANES]


def begin_kernel(trees, basis_ref, v_ref, transfer_ref, slots_ref, window_ref):
    basis = basis_ref.shape[0] * LANES // v_ref.shape[1]
    window = split_rows(basis_ref, basis)
    window_ref[...] = window
    lowered = window[basis - VECS :].astype(jnp.bfloat16)
    fill_operator_slots(slots_ref, lowered, v_ref[...], transfer_ref[...], trees)


def pack_couplings(weights_ref, far_coupling_ref, transfer_ref, top_ref):
    own_tree = lax.axis_index("lvl")
    far_slots = far_coupling_ref.shape[0]
    trees, rank = top_ref.shape[0], top_ref.shape[1]
    transfer = transfer_ref[...]
    for slot in range(far_slots + trees):
        if slot < far_slots:
            block = far_coupling_ref[slot]
        else:
            tree = slot - far_slots
            block = jnp.where(tree != own_tree, top_ref[tree], 0.0)
            block = jnp.dot(
                transfer, block, precision=PRECISE, preferred_element_type=jnp.float32
            )
        wide = jnp.concatenate(
            [block] * 3 + [jnp.zeros((rank, LANES - 3 * rank), jnp.float32)], axis=1
        )
        for part, piece in enumerate(three_parts(wide)):
            weights_ref[part, :, slot * LANES : (slot + 1) * LANES] = piece


def apply_kernel(
    trees,
    first,
    near_col_ref,
    near_count_ref,
    far_col_ref,
    arrived_ref,
    window_ref,
    near_ref,
    u_ref,
    *refs,
):
    if first:
        far_coupling_ref, transfer_ref, top_ref, image_ref, slots_ref, weights_ref = refs
        pack_couplings(weights_ref, far_coupling_ref, transfer_ref, top_ref)
    else:
        weights_ref, image_ref, slots_ref = refs
    own_tree = lax.axis_index("lvl")
    own_leaf = lax.axis_index("clus")
    size = near_ref.shape[1]
    far_slots = far_col_ref.shape[2]
    tails = []
    for slot in range(far_slots):
        tails.append(arrived_ref[far_col_ref[0, 0, slot] * trees + own_tree, :, size:])
    for tree in range(trees):
        tails.append(arrived_ref[own_leaf * trees + tree, :, size:])
    tails = jnp.concatenate(tails, axis=1)
    coupled = sum(rows_dot(tails, weights_ref[part]) for part in range(3))
    image = jnp.dot(
        coupled.astype(jnp.bfloat16), u_ref[...], preferred_element_type=jnp.float32
    )
    count = near_count_ref[0, 0]
    for slot in range(near_ref.shape[0]):
        source = arrived_ref[near_col_ref[0, 0, slot] * trees + own_tree, :, :size]
        source = jnp.where(slot < count, source, jnp.zeros_like(source))
        image = image + rows_dot(source, near_ref[slot])
    image_ref[...] = image
    window = window_ref[...]
    basis = window.shape[0]
    stacked = jnp.concatenate([window, image], axis=0)
    products = rows_dot(stacked, stacked, PRECISE)
    pieces = [products[basis:]]
    for at in range(0, basis, VECS):
        pieces.append(products[at : at + VECS, :basis])
    used = sum(piece.shape[1] for piece in pieces)
    pieces.append(jnp.zeros((VECS, LANES - used), jnp.float32))
    packed = jnp.concatenate(pieces, axis=1)

    def store(slot):
        slots_ref[slot] = packed

    over_slots(slots_ref.shape[0], store)


def orthogonalized(arrived_ref, window, image, rows_all):
    basis = window.shape[0]
    total = arrived_ref[0:8]
    for at in range(8, arrived_ref.shape[0], 8):
        total = total + arrived_ref[at : at + 8]
    total = (total[:VECS] + total[VECS:]) * (1.0 / rows_all)
    projection = total[:, :basis]
    square = total[:, basis : basis + VECS]
    inner = jnp.zeros((VECS, basis), jnp.float32)
    remainder = image
    at = basis + VECS
    lane = lax.broadcasted_iota(jnp.int32, (1, basis), 1)
    for b in range(basis):
        column = projection[:, b : b + 1]
        group = at + basis * (b // VECS)
        metric_row = total[b % VECS : b % VECS + 1, group : group + basis]
        metric_row = metric_row - jnp.where(lane == b, 2.0, 0.0)
        inner = inner + column * metric_row
        remainder = remainder - column * window[b : b + 1]
    columns = []
    for u in range(VECS):
        cross = jnp.sum(inner * projection[u : u + 1], axis=1, keepdims=True)
        columns.append(square[:, u : u + 1] + cross)
    row = lax.broadcasted_iota(jnp.int32, (VECS, 1), 0)
    factor = []
    for j in range(VECS):
        pivot = columns[j][j : j + 1]
        root = jnp.sqrt(pivot)
        scale = 1.0 / root
        lower = jnp.where(row > j, columns[j] * scale, 0.0)
        factor.append(jnp.where(row == j, root, lower))
        for u in range(j + 1, VECS):
            columns[u] = columns[u] - lower * lower[u : u + 1]
        solved = remainder[j : j + 1] * scale
        remainder = jnp.where(row == j, solved, remainder - lower * solved)
    record = jnp.concatenate([projection] + factor, axis=1)
    return remainder, record


def middle_kernel(
    trees,
    rows_all,
    arrived_ref,
    window_ref,
    image_ref,
    v_ref,
    transfer_ref,
    slots_ref,
    next_window_ref,
    record_ref,
):
    window = window_ref[...]
    new_block, record = orthogonalized(arrived_ref, window, image_ref[...], rows_all)
    record_ref[...] = record
    next_window_ref[:-VECS] = window[VECS:]
    next_window_ref[-VECS:] = new_block
    lowered = new_block.astype(jnp.bfloat16)
    fill_operator_slots(slots_ref, lowered, v_ref[...], transfer_ref[...], trees)


def end_kernel(rows_all, arrived_ref, window_ref, image_ref, first_ref, block_ref, records_ref):
    new_block, record = orthogonalized(arrived_ref, window_ref[...], image_ref[...], rows_all)
    store_rows(block_ref, new_block)
    records_ref[0] = first_ref[...]
    records_ref[1] = record


def call(kernel, name, outs, ins, scalars=0):
    specs = [pl.BlockSpec(memory_space=pltpu.SMEM)] * scalars
    specs += [pl.BlockSpec(memory_space=pltpu.VMEM)] * (len(ins) - scalars)
    return pl.pallas_call(
        kernel,
        name=name,
        out_shape=[jax.ShapeDtypeStruct(shape, dtype) for shape, dtype in outs],
        in_specs=specs,
        out_specs=[pl.BlockSpec(memory_space=pltpu.VMEM)] * len(outs),
        compiler_params=pltpu.CompilerParams(vmem_limit_bytes=16 << 20),
    )(*ins)


def exchange(slots):
    return lax.all_to_all(slots, AXES, 0, 0, tiled=True)


def local(
    krylov_basis,
    near_block,
    near_col,
    near_count,
    far_col,
    v_basis,
    u_basis,
    far_coupling,
    transfer,
    top_coupling,
):
    basis, _, size = krylov_basis.shape
    trees = lax.axis_size("lvl")
    devices = lax.axis_size("clus") * trees
    rows_all = float(devices * size)
    v_own, u_own, transfer_own = v_basis[0, 0], u_basis[0, 0], transfer[0, 0]
    rank = v_own.shape[0]
    far_own, top_own, near_own = far_coupling[0, 0], top_coupling[0, 0], near_block[0, 0]
    f32, bf16 = jnp.float32, jnp.bfloat16
    operator_slots = ((devices, VECS, size + LANES), bf16)
    product_slots = ((devices, VECS, LANES), f32)
    image_like = ((VECS, size), f32)
    window_like = ((basis, size), f32)
    record_like = ((VECS, basis + VECS), f32)
    weights_like = ((3, rank, (far_own.shape[0] + trees) * LANES), bf16)
    scalars = (near_col, near_count, far_col)
    slots, window = call(
        functools.partial(begin_kernel, trees),
        "begin",
        [operator_slots, window_like],
        [krylov_basis.reshape(-1, LANES), v_own, transfer_own],
    )
    arrived = exchange(slots)
    image, slots, weights = call(
        functools.partial(apply_kernel, trees, True),
        "apply_first",
        [image_like, product_slots, weights_like],
        [*scalars, arrived, window, near_own, u_own, far_own, transfer_own, top_own],
        scalars=3,
    )
    arrived = exchange(slots).reshape(-1, LANES)
    slots, window, record = call(
        functools.partial(middle_kernel, trees, rows_all),
        "middle",
        [operator_slots, window_like, record_like],
        [arrived, window, image, v_own, transfer_own],
    )
    arrived = exchange(slots)
    image, slots = call(
        functools.partial(apply_kernel, trees, False),
        "apply_second",
        [image_like, product_slots],
        [*scalars, arrived, window, near_own, u_own, weights],
        scalars=3,
    )
    arrived = exchange(slots).reshape(-1, LANES)
    block, records = call(
        functools.partial(end_kernel, rows_all),
        "end",
        [((VECS * size // LANES, LANES), f32), ((STEPS,) + record_like[0], f32)],
        [arrived, window, image, record],
    )
    return (block.reshape(VECS, 1, size), jnp.transpose(records, (0, 2, 1)))


def solution(mesh):
    return jax.shard_map(
        local,
        mesh=mesh,
        in_specs=(
            P(None, "lvl", "clus"),
            P("lvl", "clus", None, None, None),
            P("lvl", "clus", None),
            P("lvl", "clus"),
            P("lvl", "clus", None),
            P("lvl", "clus", None, None),
            P("lvl", "clus", None, None),
            P("lvl", "clus", None, None, None),
            P("lvl", "clus", None, None),
            P("lvl", "clus", None, None, None),
        ),
        out_specs=(P(None, "lvl", "clus"), P()),
        check_vma=False,
    )
```

```python
import functools

import jax
import jax.numpy as jnp
from jax import lax
from jax.experimental import pallas as pl
from jax.experimental.pallas import tpu as pltpu
from jax.sharding import PartitionSpec as P

VECS = 4
STEPS = 2
LANES = 128
PIECE = 16
UNROLL = 32
AXES = ("clus", "lvl")

PRECISE = lax.Precision.HIGHEST
ROWS_DIMS = (((1,), (1,)), ((), ()))
F32, BF16 = jnp.float32, jnp.bfloat16


def rows_dot(left, right, precision=None):
    return lax.dot_general(
        left, right, ROWS_DIMS, precision=precision, preferred_element_type=F32
    )


def precise_dot(left, right):
    return jnp.dot(left, right, precision=PRECISE, preferred_element_type=F32)


def three_parts(values):
    high = values.astype(BF16)
    rest = values - high.astype(F32)
    middle = rest.astype(BF16)
    low = (rest - middle.astype(F32)).astype(BF16)
    return high, middle, low


def lane_parts(values, part):
    high = values.astype(BF16).astype(F32)
    rest = values - high
    middle = rest.astype(BF16).astype(F32)
    low = rest - middle
    return jnp.where(part == 0, high, jnp.where(part == 1, middle, jnp.where(part == 2, low, 0.0)))


def wide_parts(values, count):
    return [part.astype(F32) for part in three_parts(values)[:count]]


def lanes_of(shape):
    return lax.broadcasted_iota(jnp.int32, shape, len(shape) - 1)


def over_slots(count, store):
    step = min(count, UNROLL)
    if count == step:
        for slot in range(count):
            store(slot, slot)
        return

    def body(at, carry):
        for inner in range(step):
            store(at * step + inner, inner)
        return carry

    lax.fori_loop(0, count // step, body, 0)


def split_rows(flat, rows):
    halves = flat.shape[0] // rows
    return jnp.concatenate(
        [flat[pl.ds(half, rows, stride=halves), :] for half in range(halves)], axis=1
    )


def store_rows(flat_ref, values):
    rows = values.shape[0]
    halves = flat_ref.shape[0] // rows
    for half in range(halves):
        flat_ref[pl.ds(half, rows, stride=halves), :] = values[:, half * LANES : (half + 1) * LANES]


def skeleton_of(parts, v_basis):
    rows = rows_dot(jnp.concatenate(parts, axis=0), v_basis)
    return [rows[at : at + VECS] for at in range(0, rows.shape[0], VECS)]


def begin_kernel(trees, basis_hbm, v_hbm, transfer_hbm, slots_ref, window_ref, *scratch):
    basis_ref, v_ref, transfer_ref, sems = scratch
    copies = [
        pltpu.make_async_copy(source, target, sems.at[at])
        for at, (source, target) in enumerate(
            ((basis_hbm, basis_ref), (v_hbm, v_ref), (transfer_hbm, transfer_ref))
        )
    ]
    for copy in copies:
        copy.start()
    for copy in copies:
        copy.wait()
    basis, size = window_ref.shape
    rank = v_ref.shape[0]
    window = split_rows(basis_ref, basis)
    window_ref[...] = window
    current = window[basis - VECS :]
    lowered = current.astype(BF16)
    rest = current - lowered.astype(F32)
    parts = [lowered, *three_parts(window[: basis - VECS]), *three_parts(rest)[:2]]
    rows = skeleton_of([part.astype(F32) for part in parts], v_ref[...].astype(F32))
    skeletons = jnp.concatenate([rows[0], rows[1] + rows[2] + rows[3], rows[4] + rows[5]], axis=0)
    coarse = precise_dot(skeletons, transfer_ref[...])
    own_tree = lax.axis_index("lvl")

    def tails(values):
        exact, old, extra = (values[at : at + VECS] for at in range(0, 3 * VECS, VECS))
        first = jnp.concatenate(wide_parts(exact, 3) + [extra], axis=1)
        blank = jnp.zeros((VECS, LANES - 2 * rank), F32)
        second = jnp.concatenate([blank] + wide_parts(old, 2), axis=1)
        return first.astype(BF16), second

    tree_first, tree_second = tails(skeletons)
    level_first, level_second = tails(coarse)
    lane = lanes_of((VECS, LANES))
    turns = LANES // PIECE
    tiles = [
        window[row : row + VECS, at : at + LANES]
        for row in range(0, basis, VECS)
        for at in range(0, size, LANES)
    ]
    turned = [
        [pltpu.roll(tile, (LANES - PIECE * c) % LANES, 1) if c else tile for c in range(turns)]
        for tile in tiles
    ]
    part = lane // PIECE

    def store(slot, at):
        tile = turned[at // turns % len(tiles)]
        c = at % turns
        copies_of = jnp.where(
            part == 0, tile[c], jnp.where(part == 1, tile[(c - 1) % turns], tile[(c - 2) % turns])
        )
        piece = lane_parts(copies_of, part)
        same = lax.rem(jnp.int32(slot), jnp.int32(trees)) == own_tree
        second = jnp.where(same, tree_second, level_second)
        slots_ref[slot, :, :size] = lowered
        slots_ref[slot, :, size : size + LANES] = level_first
        slots_ref[slot, :, size + LANES :] = (piece + second).astype(BF16)

    over_slots(slots_ref.shape[0], store)

    def store_tree(leaf, at):
        slots_ref[leaf * trees + own_tree, :, size : size + LANES] = tree_first

    over_slots(slots_ref.shape[0] // trees, store_tree)


def prepare_kernel(
    near_col_ref,
    near_count_ref,
    far_col_ref,
    near_hbm,
    far_coupling_ref,
    transfer_ref,
    top_ref,
    weights_ref,
    near_ref,
    sem,
):
    copy = pltpu.make_async_copy(near_hbm, near_ref, sem)
    copy.start()
    own_tree = lax.axis_index("lvl")
    far_slots = far_coupling_ref.shape[0]
    trees, rank = top_ref.shape[0], top_ref.shape[1]
    transfer = transfer_ref[...]
    for slot in range(far_slots + trees):
        if slot < far_slots:
            block = far_coupling_ref[slot]
        else:
            tree = slot - far_slots
            block = precise_dot(transfer, jnp.where(tree != own_tree, top_ref[tree], 0.0))
        wide = jnp.concatenate([block] * (LANES // rank), axis=1)
        for part, piece in enumerate(three_parts(wide)):
            weights_ref[part, :, slot * LANES : (slot + 1) * LANES] = piece
    copy.wait()


def sources_of(far_col_ref, trees):
    own_tree = lax.axis_index("lvl")
    own_leaf = lax.axis_index("clus")
    places = [far_col_ref[0, 0, slot] * trees + own_tree for slot in range(far_col_ref.shape[2])]
    return places + [own_leaf * trees + tree for tree in range(trees)]


def couple(values, weights_ref):
    lowered = values.astype(BF16)
    return sum(rows_dot(lowered, weights_ref[part]) for part in range(3))


def product_lanes(window, image):
    basis = window.shape[0]
    stacked = jnp.concatenate([window, image], axis=0)
    products = rows_dot(stacked, stacked, PRECISE)
    pieces = [products[basis:]]
    for at in range(0, basis, VECS):
        pieces.append(products[at : at + VECS, :basis])
    return jnp.concatenate(pieces, axis=1)


def framed(before, values, after):
    rows = values.shape[0]
    pieces = [jnp.zeros((rows, before), F32)] if before else []
    pieces.append(values)
    if after:
        pieces.append(jnp.zeros((rows, after), F32))
    return jnp.concatenate(pieces, axis=1)


def first_kernel(
    trees,
    near_col_ref,
    near_count_ref,
    far_col_ref,
    arrived_ref,
    window_ref,
    weights_ref,
    near_ref,
    u_ref,
    v_ref,
    transfer_ref,
    image_ref,
    slots_ref,
    window_coupled_ref,
):
    own_tree = lax.axis_index("lvl")
    size = near_ref.shape[1]
    rank = v_ref.shape[0]
    places = sources_of(far_col_ref, trees)
    first = [arrived_ref[place, :, size : size + LANES] for place in places]
    second = [arrived_ref[place, :, size + LANES :] for place in places]
    first = jnp.concatenate(first, axis=1).astype(F32)
    second = jnp.concatenate(second, axis=1).astype(F32)
    lane = lanes_of(first.shape) % LANES
    exact = jnp.where(lane < 3 * rank, first, 0.0)
    old = jnp.where(lane >= LANES - 2 * rank, second, 0.0)
    rows = couple(jnp.concatenate([exact, first, old], axis=0), weights_ref)
    window_coupled_ref[:VECS] = rows[2 * VECS :]
    window_coupled_ref[VECS:] = rows[VECS : 2 * VECS]
    image = jnp.dot(rows[:VECS].astype(BF16), u_ref[...], preferred_element_type=F32)
    count = near_count_ref[0, 0]
    for slot in range(near_ref.shape[0]):
        source = arrived_ref[near_col_ref[0, 0, slot] * trees + own_tree, :, :size]
        source = jnp.where(slot < count, source, jnp.zeros_like(source))
        image = image + rows_dot(source, near_ref[slot])
    image_ref[...] = image
    packed = product_lanes(window_ref[...], image)
    parts = [part.astype(F32) for part in three_parts(image)]
    pieces = skeleton_of(parts, v_ref[...].astype(F32))
    skeleton = pieces[0] + pieces[1] + pieces[2]
    coarse = precise_dot(skeleton, transfer_ref[...])
    room = LANES - 2 * rank
    packed = framed(PIECE, packed, room - PIECE - packed.shape[1])
    tree_tail = jnp.concatenate([packed, skeleton, skeleton], axis=1)
    level_tail = jnp.concatenate([packed, coarse, coarse], axis=1)
    narrow = lanes_of((VECS, LANES))
    from_low = narrow < PIECE
    from_high = (narrow >= 3 * PIECE) & (narrow < 4 * PIECE)
    total = slots_ref.shape[0]

    def store(slot, at):
        if isinstance(slot, int):
            low, high = max(slot - trees, 0), min(slot + trees, total - 1)
        else:
            low, high = jnp.maximum(slot - trees, 0), jnp.minimum(slot + trees, total - 1)
        low = arrived_ref[low, :, size + LANES :].astype(F32)
        high = arrived_ref[high, :, size + LANES :].astype(F32)
        both = jnp.where(narrow < 3 * PIECE, low, pltpu.roll(high, 3 * PIECE, 1))
        both = both + pltpu.roll(both, LANES - PIECE, 1) + pltpu.roll(both, LANES - 2 * PIECE, 1)
        same = lax.rem(jnp.int32(slot), jnp.int32(trees)) == own_tree
        tail = jnp.where(same, tree_tail, level_tail)
        slots_ref[slot, :, :size] = image
        slots_ref[slot, :, size:] = jnp.where(from_low | from_high, both, tail)

    over_slots(total, store)


def orthogonalized(total, window, image):
    basis = window.shape[0]
    projection = total[:, :basis]
    square = total[:, basis : basis + VECS]
    inner = jnp.zeros((VECS, basis), F32)
    remainder = image
    at = basis + VECS
    lane = lanes_of((1, basis))
    for b in range(basis):
        column = projection[:, b : b + 1]
        group = at + basis * (b // VECS)
        metric_row = total[b % VECS : b % VECS + 1, group : group + basis]
        metric_row = metric_row - jnp.where(lane == b, 2.0, 0.0)
        inner = inner + column * metric_row
        remainder = remainder - column * window[b : b + 1]
    columns = []
    for u in range(VECS):
        cross = jnp.sum(inner * projection[u : u + 1], axis=1, keepdims=True)
        columns.append(square[:, u : u + 1] + cross)
    row = lax.broadcasted_iota(jnp.int32, (VECS, 1), 0)
    factor = []
    for j in range(VECS):
        root = jnp.sqrt(columns[j][j : j + 1])
        scale = 1.0 / root
        lower = jnp.where(row > j, columns[j] * scale, 0.0)
        factor.append(jnp.where(row == j, root, lower))
        for u in range(j + 1, VECS):
            columns[u] = columns[u] - lower * lower[u : u + 1]
        solved = remainder[j : j + 1] * scale
        remainder = jnp.where(row == j, solved, remainder - lower * solved)
    record = jnp.concatenate([projection] + factor, axis=1)
    return remainder, record


def middle_kernel(
    trees,
    rows_all,
    near_col_ref,
    near_count_ref,
    far_col_ref,
    arrived_ref,
    window_ref,
    image_ref,
    window_coupled_ref,
    weights_ref,
    near_ref,
    u_ref,
    v_ref,
    transfer_ref,
    slots_ref,
    next_window_ref,
    near_part_ref,
    record_ref,
):
    own_tree = lax.axis_index("lvl")
    own_leaf = lax.axis_index("clus")
    window = window_ref[...]
    basis, size = window.shape
    rank = v_ref.shape[0]
    lane = lanes_of((VECS, LANES))
    group = lane // PIECE
    turns = LANES // PIECE
    tile_count = basis // VECS * (size // LANES)
    low_tiles, high_tiles = [], []
    total = jnp.zeros((VECS, LANES), F32)
    for slot in range(tile_count * turns):
        tail = arrived_ref[slot, :, size:]
        total = total + tail
        c = slot % turns
        turned = pltpu.roll(tail, PIECE * c, 1) if c else tail
        if c == 0:
            low_tiles.append(turned)
            high_tiles.append(turned)
        else:
            low_tiles[-1] = jnp.where(group == c, turned, low_tiles[-1])
            high_tiles[-1] = jnp.where(group == (c + 3) % turns, turned, high_tiles[-1])
    slots = arrived_ref.shape[0]
    if slots > tile_count * turns:
        total = lax.fori_loop(
            tile_count * turns, slots, lambda at, held: held + arrived_ref[at, :, size:], total
        )
    high_tiles = [pltpu.roll(tile, LANES - 3 * PIECE, 1) for tile in high_tiles]
    total = total[:, PIECE : LANES - 2 * rank] * (1.0 / rows_all)

    def rows_from(tiles):
        per_row = size // LANES
        rows = [
            jnp.concatenate(tiles[at : at + per_row], axis=1)
            for at in range(0, tile_count, per_row)
        ]
        return jnp.concatenate(rows, axis=0)

    leaves = slots // trees
    low_place = jnp.maximum(own_leaf - 1, 0) * trees + own_tree
    high_place = jnp.minimum(own_leaf + 1, leaves - 1) * trees + own_tree
    tails = jnp.concatenate(
        [arrived_ref[place, :, size:] for place in sources_of(far_col_ref, trees)], axis=1
    )
    tails = lane_parts(tails, lanes_of(tails.shape) % LANES // rank - (LANES // rank - 2))
    wide_lane = lanes_of(tails.shape) % LANES
    tails = jnp.where(wide_lane >= LANES - 2 * rank, tails, 0.0)
    coupled = couple(tails, weights_ref)
    images = jnp.concatenate(
        [
            arrived_ref[low_place, :, :size],
            image_ref[...],
            arrived_ref[high_place, :, :size],
            coupled,
        ],
        axis=1,
    )
    windows = jnp.concatenate(
        [rows_from(low_tiles), window, rows_from(high_tiles), window_coupled_ref[...]], axis=1
    )
    solved, record = orthogonalized(total, windows, images)
    record_ref[...] = record
    low_block, new_block, high_block = (solved[:, at : at + size] for at in range(0, 3 * size, size))
    next_window = jnp.concatenate([window[VECS:], new_block], axis=0)
    next_window_ref[...] = next_window
    count = near_count_ref[0, 0]
    near_part = jnp.zeros((VECS, size), F32)
    for slot in range(near_ref.shape[0]):
        leaf = near_col_ref[0, 0, slot]
        source = jnp.where(leaf < own_leaf, low_block, jnp.where(leaf > own_leaf, high_block, new_block))
        source = jnp.where(slot < count, source, 0.0).astype(BF16)
        near_part = near_part + rows_dot(source, near_ref[slot])
    near_part_ref[...] = near_part
    far_part = jnp.dot(
        solved[:, 3 * size :].astype(BF16), u_ref[...], preferred_element_type=F32
    )
    skeleton = rows_dot(new_block.astype(BF16), v_ref[...])
    coarse = precise_dot(skeleton, transfer_ref[...])
    packed = product_lanes(next_window, near_part + far_part)
    packed = framed(0, packed, rank - packed.shape[1])
    copies = LANES // rank - 1
    tree_tail = jnp.concatenate([packed] + [skeleton] * copies, axis=1)
    level_tail = jnp.concatenate([packed] + [coarse] * copies, axis=1)

    def store(slot, at):
        slots_ref[slot] = level_tail

    over_slots(slots, store)

    def store_tree(leaf, at):
        slots_ref[leaf * trees + own_tree] = tree_tail

    over_slots(leaves, store_tree)


def end_kernel(
    trees,
    rows_all,
    far_col_ref,
    arrived_ref,
    window_ref,
    near_part_ref,
    weights_ref,
    u_ref,
    first_ref,
    block_ref,
    records_ref,
):
    rank = u_ref.shape[0]
    tails = jnp.concatenate(
        [arrived_ref[place] for place in sources_of(far_col_ref, trees)], axis=1
    )
    part = lanes_of(tails.shape) % LANES // rank - 1
    coupled = couple(jnp.where(part >= 0, lane_parts(tails, part), 0.0), weights_ref)
    far_part = jnp.dot(coupled.astype(BF16), u_ref[...], preferred_element_type=F32)
    slots = arrived_ref.shape[0]
    near = min(slots, UNROLL)
    total = arrived_ref[0]
    for slot in range(1, near):
        total = total + arrived_ref[slot]
    if slots > near:
        total = lax.fori_loop(near, slots, lambda at, held: held + arrived_ref[at], total)
    total = total[:, :rank] * (1.0 / rows_all)
    new_block, record = orthogonalized(total, window_ref[...], near_part_ref[...] + far_part)
    store_rows(block_ref, new_block)
    records_ref[0] = first_ref[...]
    records_ref[1] = record


def call(kernel, name, outs, ins, places, scratch=(), vmem=16 << 20, bytes_accessed=1 << 20):
    spaces = {"s": pltpu.SMEM, "v": pltpu.VMEM, "h": pltpu.HBM}
    return pl.pallas_call(
        kernel,
        name=name,
        out_shape=[jax.ShapeDtypeStruct(shape, dtype) for shape, dtype in outs],
        in_specs=[pl.BlockSpec(memory_space=spaces[place]) for place in places],
        out_specs=[pl.BlockSpec(memory_space=pltpu.VMEM)] * len(outs),
        scratch_shapes=list(scratch),
        cost_estimate=pl.CostEstimate(flops=0, bytes_accessed=bytes_accessed, transcendentals=0),
        compiler_params=pltpu.CompilerParams(vmem_limit_bytes=vmem),
    )(*ins)


def exchange(slots):
    return lax.all_to_all(slots, AXES, 0, 0, tiled=True)


def local(
    krylov_basis,
    near_block,
    near_col,
    near_count,
    far_col,
    v_basis,
    u_basis,
    far_coupling,
    transfer,
    top_coupling,
):
    basis, _, size = krylov_basis.shape
    trees = lax.axis_size("lvl")
    devices = lax.axis_size("clus") * trees
    rows_all = float(devices * size)
    flat_basis = krylov_basis.reshape(-1, LANES)
    v_own, u_own, transfer_own = v_basis[0, 0], u_basis[0, 0], transfer[0, 0]
    rank = v_own.shape[0]
    far_own, top_own, near_own = far_coupling[0, 0], top_coupling[0, 0], near_block[0, 0]
    image_like = ((VECS, size), F32)
    window_like = ((basis, size), F32)
    record_like = ((VECS, basis + VECS), F32)
    weights_like = ((3, rank, (far_own.shape[0] + trees) * LANES), BF16)
    slots, window = call(
        functools.partial(begin_kernel, trees),
        "begin",
        [((devices, VECS, size + 2 * LANES), BF16), window_like],
        [flat_basis, v_own, transfer_own],
        "hhh",
        [
            pltpu.VMEM(flat_basis.shape, F32),
            pltpu.VMEM(v_own.shape, BF16),
            pltpu.VMEM(transfer_own.shape, F32),
            pltpu.SemaphoreType.DMA((3,)),
        ],
        vmem=None,
    )
    arrived = exchange(slots)
    weights, near_here = call(
        prepare_kernel,
        "prepare",
        [weights_like, (near_own.shape, BF16)],
        [near_col, near_count, far_col, near_own, far_own, transfer_own, top_own],
        "ssshvvv",
        [pltpu.SemaphoreType.DMA],
    )
    image, slots, window_coupled = call(
        functools.partial(first_kernel, trees),
        "first",
        [image_like, ((devices, VECS, size + LANES), F32), ((basis, rank), F32)],
        [
            near_col,
            near_count,
            far_col,
            arrived,
            window,
            weights,
            near_here,
            u_own,
            v_own,
            transfer_own,
        ],
        "sssvvvvvvv",
    )
    arrived = exchange(slots)
    slots, window, near_part, record = call(
        functools.partial(middle_kernel, trees, rows_all),
        "middle",
        [((devices, VECS, LANES), F32), window_like, image_like, record_like],
        [
            near_col,
            near_count,
            far_col,
            arrived,
            window,
            image,
            window_coupled,
            weights,
            near_here,
            u_own,
            v_own,
            transfer_own,
        ],
        "sssvvvvvvvvv",
    )
    arrived = exchange(slots)
    block, records = call(
        functools.partial(end_kernel, trees, rows_all),
        "end",
        [((VECS * size // LANES, LANES), F32), ((STEPS,) + record_like[0], F32)],
        [far_col, arrived, window, near_part, weights, u_own, record],
        "svvvvvv",
    )
    return (block.reshape(VECS, 1, size), jnp.transpose(records, (0, 2, 1)))


def solution(mesh):
    return jax.shard_map(
        local,
        mesh=mesh,
        in_specs=(
            P(None, "lvl", "clus"),
            P("lvl", "clus", None, None, None),
            P("lvl", "clus", None),
            P("lvl", "clus"),
            P("lvl", "clus", None),
            P("lvl", "clus", None, None),
            P("lvl", "clus", None, None),
            P("lvl", "clus", None, None, None),
            P("lvl", "clus", None, None),
            P("lvl", "clus", None, None, None),
        ),
        out_specs=(P(None, "lvl", "clus"), P()),
        check_vma=False,
    )
```

```python
import functools

import jax
import jax.numpy as jnp
from jax import lax
from jax.experimental import pallas as pl
from jax.experimental.pallas import tpu as pltpu
from jax.sharding import PartitionSpec as P

VECS = 4
STEPS = 2
LANES = 128
PIECE = 16
UNROLL = 32
AXES = ("clus", "lvl")

PRECISE = lax.Precision.HIGHEST
ROWS_DIMS = (((1,), (1,)), ((), ()))
F32, BF16 = jnp.float32, jnp.bfloat16


def rows_dot(left, right, precision=None):
    return lax.dot_general(
        left, right, ROWS_DIMS, precision=precision, preferred_element_type=F32
    )


def precise_dot(left, right):
    return jnp.dot(left, right, precision=PRECISE, preferred_element_type=F32)


def three_parts(values):
    high = values.astype(BF16)
    rest = values - high.astype(F32)
    middle = rest.astype(BF16)
    low = (rest - middle.astype(F32)).astype(BF16)
    return high, middle, low


def lane_parts(values, part):
    high = values.astype(BF16).astype(F32)
    rest = values - high
    middle = rest.astype(BF16).astype(F32)
    low = rest - middle
    return jnp.where(part == 0, high, jnp.where(part == 1, middle, jnp.where(part == 2, low, 0.0)))


def lanes_of(shape):
    return lax.broadcasted_iota(jnp.int32, shape, len(shape) - 1)


def over_slots(count, store):
    step = min(count, UNROLL)
    if count == step:
        for slot in range(count):
            store(slot, slot)
        return

    def body(at, carry):
        for inner in range(step):
            store(at * step + inner, inner)
        return carry

    lax.fori_loop(0, count // step, body, 0)


def split_rows(flat, rows):
    halves = flat.shape[0] // rows
    return jnp.concatenate(
        [flat[pl.ds(half, rows, stride=halves), :] for half in range(halves)], axis=1
    )


def store_rows(flat_ref, values):
    rows = values.shape[0]
    halves = flat_ref.shape[0] // rows
    for half in range(halves):
        flat_ref[pl.ds(half, rows, stride=halves), :] = values[:, half * LANES : (half + 1) * LANES]


def row_groups(rows):
    return [rows[at : at + VECS] for at in range(0, rows.shape[0], VECS)]


def lane_tiles(values):
    return [values[:, at : at + LANES] for at in range(0, values.shape[1], LANES)]


def replicated(column):
    return jnp.broadcast_to(column, (column.shape[0], LANES))


def lane_sum(pairs):
    return replicated(jnp.sum(sum(left * right for left, right in pairs), axis=1, keepdims=True))


def begin_kernel(trees, basis_hbm, v_hbm, transfer_hbm, slots_ref, window_ref, *scratch):
    basis_ref, v_ref, transfer_ref, sems = scratch
    copies = [
        pltpu.make_async_copy(source, target, sems.at[at])
        for at, (source, target) in enumerate(
            ((basis_hbm, basis_ref), (v_hbm, v_ref), (transfer_hbm, transfer_ref))
        )
    ]
    for copy in copies:
        copy.start()
    for copy in copies:
        copy.wait()
    basis, size = window_ref.shape
    rank = v_ref.shape[0]
    window = split_rows(basis_ref, basis)
    window_ref[...] = window
    current = window[basis - VECS :]
    lowered = current.astype(BF16)
    rest = current - lowered.astype(F32)
    parts = [lowered, *three_parts(window[: basis - VECS]), *three_parts(rest)[:2]]
    parts = jnp.concatenate([part.astype(F32) for part in parts], axis=0).astype(BF16)
    repeats = LANES // rank
    wide_basis = jnp.concatenate([v_ref[...]] * repeats, axis=0)
    rows = row_groups(rows_dot(parts, wide_basis))
    skeletons = jnp.concatenate([rows[0], rows[1] + rows[2] + rows[3], rows[4] + rows[5]], axis=0)
    wide_transfer = jnp.concatenate([transfer_ref[...]] * repeats, axis=1)
    coarse = precise_dot(skeletons[:, :rank], wide_transfer)
    own_tree = lax.axis_index("lvl")

    def tails(values):
        exact, old, extra = row_groups(values)
        group = lanes_of((VECS, LANES)) // rank
        first = jnp.where(group < 3, lane_parts(exact, group), extra)
        return first.astype(BF16), lane_parts(old, group - (repeats - 2))

    tree_first, tree_second = tails(skeletons)
    level_first, level_second = tails(coarse)
    lane = lanes_of((VECS, LANES))
    turns = LANES // PIECE
    kept = lane >= LANES - 2 * rank
    tiles = [
        window[row : row + VECS, at : at + LANES]
        for row in range(0, basis, VECS)
        for at in range(0, size, LANES)
    ]
    turned = [
        [pltpu.roll(tile, (LANES - PIECE * c) % LANES, 1) if c else tile for c in range(turns)]
        for tile in tiles
    ]
    part = lane // PIECE

    def store(slot, at):
        tile = turned[at // turns % len(tiles)]
        c = at % turns
        copies_of = jnp.where(
            part == 0, tile[c], jnp.where(part == 1, tile[(c - 1) % turns], tile[(c - 2) % turns])
        )
        piece = lane_parts(copies_of, part)
        same = lax.rem(jnp.int32(slot), jnp.int32(trees)) == own_tree
        second = jnp.where(same, tree_second, level_second)
        slots_ref[slot, :, :size] = lowered
        slots_ref[slot, :, size : size + LANES] = level_first
        slots_ref[slot, :, size + LANES :] = jnp.where(kept, second, piece).astype(BF16)

    over_slots(slots_ref.shape[0], store)

    def store_tree(leaf, at):
        slots_ref[leaf * trees + own_tree, :, size : size + LANES] = tree_first

    over_slots(slots_ref.shape[0] // trees, store_tree)


def prepare_kernel(
    near_col_ref,
    near_count_ref,
    far_col_ref,
    near_hbm,
    far_coupling_ref,
    v_ref,
    transfer_ref,
    top_ref,
    weights_ref,
    near_ref,
    maps_ref,
    sem,
):
    copy = pltpu.make_async_copy(near_hbm, near_ref, sem)
    copy.start()
    own_tree = lax.axis_index("lvl")
    far_slots = far_coupling_ref.shape[0]
    trees, rank = top_ref.shape[0], top_ref.shape[1]
    transfer = transfer_ref[...]
    for slot in range(far_slots + trees):
        if slot < far_slots:
            block = far_coupling_ref[slot]
        else:
            tree = slot - far_slots
            block = precise_dot(transfer, jnp.where(tree != own_tree, top_ref[tree], 0.0))
        wide = jnp.concatenate([block] * (LANES // rank), axis=1)
        for part, piece in enumerate(three_parts(wide)):
            weights_ref[part, :, slot * LANES : (slot + 1) * LANES] = piece
    v_basis = v_ref[...]
    carried = precise_dot(transfer.T, v_basis.astype(F32))
    for part, piece in enumerate((v_basis, *three_parts(carried))):
        for at in range(part * LANES, (part + 1) * LANES, rank):
            maps_ref[at : at + rank] = piece
    copy.wait()


def sources_of(far_col_ref, trees):
    own_tree = lax.axis_index("lvl")
    own_leaf = lax.axis_index("clus")
    places = [far_col_ref[0, 0, slot] * trees + own_tree for slot in range(far_col_ref.shape[2])]
    return places + [own_leaf * trees + tree for tree in range(trees)]


def couple(values, weights_ref):
    lowered = values.astype(BF16)
    return sum(rows_dot(lowered, weights_ref[part]) for part in range(3))


def product_lanes(window, image, at):
    basis = window.shape[0]
    window, image = lane_tiles(window), lane_tiles(image)
    lane = lanes_of((VECS, LANES))
    packed = jnp.zeros((VECS, LANES), F32)
    for b in range(basis):
        product = lane_sum([(tile, other[b : b + 1]) for tile, other in zip(image, window)])
        packed = jnp.where(lane == at + b, product, packed)
    at = at + basis
    for u in range(VECS):
        product = lane_sum([(tile, tile[u : u + 1]) for tile in image])
        packed = jnp.where(lane == at + u, product, packed)
    at = at + VECS
    for b in range(basis):
        product = lane_sum([(tile, tile[b : b + 1]) for tile in window])
        for group in range(basis // VECS):
            rows = product[group * VECS : (group + 1) * VECS]
            packed = jnp.where(lane == at + group * basis + b, rows, packed)
    return packed


def mapped(rows, maps_ref):
    products = lane_tiles(rows_dot(rows, maps_ref[...]))
    skeleton, coarse = products[0], products[1] + products[2] + products[3]
    return sum(row_groups(skeleton)), sum(row_groups(coarse))


def first_kernel(
    trees,
    near_col_ref,
    near_count_ref,
    far_col_ref,
    arrived_ref,
    window_ref,
    weights_ref,
    near_ref,
    u_ref,
    maps_ref,
    image_ref,
    slots_ref,
    window_coupled_ref,
):
    own_tree = lax.axis_index("lvl")
    size = near_ref.shape[1]
    rank = u_ref.shape[0]
    places = sources_of(far_col_ref, trees)
    first = [arrived_ref[place, :, size : size + LANES] for place in places]
    second = [arrived_ref[place, :, size + LANES :] for place in places]
    first = jnp.concatenate(first, axis=1).astype(F32)
    second = jnp.concatenate(second, axis=1).astype(F32)
    lane = lanes_of(first.shape) % LANES
    exact = jnp.where(lane < 3 * rank, first, 0.0)
    old = jnp.where(lane >= LANES - 2 * rank, second, 0.0)
    rows = couple(jnp.concatenate([exact, first, old], axis=0), weights_ref)
    linear = jnp.concatenate([rows[2 * VECS :], rows[VECS : 2 * VECS]], axis=0)
    blank = jnp.zeros((2 * VECS, LANES - rank), F32)
    window_coupled_ref[...] = jnp.concatenate([linear, blank], axis=1)
    image = jnp.dot(rows[:VECS].astype(BF16), u_ref[...], preferred_element_type=F32)
    count = near_count_ref[0, 0]
    for slot in range(near_ref.shape[0]):
        source = arrived_ref[near_col_ref[0, 0, slot] * trees + own_tree, :, :size]
        source = jnp.where(slot < count, source, jnp.zeros_like(source))
        image = image + rows_dot(source, near_ref[slot])
    image_ref[...] = image
    packed = product_lanes(window_ref[...], image, PIECE)
    parts = [part.astype(F32) for part in three_parts(image)]
    skeleton, coarse = mapped(jnp.concatenate(parts, axis=0).astype(BF16), maps_ref)
    kept = lanes_of((VECS, LANES)) < LANES - 2 * rank
    tree_tail = jnp.where(kept, packed, skeleton)
    level_tail = jnp.where(kept, packed, coarse)
    narrow = lanes_of((VECS, LANES))
    from_low = narrow < PIECE
    from_high = (narrow >= 3 * PIECE) & (narrow < 4 * PIECE)
    total = slots_ref.shape[0]

    def store(slot, at):
        if isinstance(slot, int):
            low, high = max(slot - trees, 0), min(slot + trees, total - 1)
        else:
            low, high = jnp.maximum(slot - trees, 0), jnp.minimum(slot + trees, total - 1)
        low = arrived_ref[low, :, size + LANES :].astype(F32)
        high = arrived_ref[high, :, size + LANES :].astype(F32)
        both = jnp.where(narrow < 3 * PIECE, low, pltpu.roll(high, 3 * PIECE, 1))
        both = both + pltpu.roll(both, LANES - PIECE, 1) + pltpu.roll(both, LANES - 2 * PIECE, 1)
        same = lax.rem(jnp.int32(slot), jnp.int32(trees)) == own_tree
        tail = jnp.where(same, tree_tail, level_tail)
        slots_ref[slot, :, :size] = image
        slots_ref[slot, :, size:] = jnp.where(from_low | from_high, both, tail)

    over_slots(total, store)


def orthogonalized(total, at, windows, images):
    basis = windows[0].shape[0]

    def column_of(lane):
        return replicated(total[:, lane : lane + 1])

    projection = [column_of(at + b) for b in range(basis)]
    square = [column_of(at + basis + u) for u in range(VECS)]
    start = at + basis + VECS
    inner = []
    for other in range(basis):
        value = -2.0 * projection[other]
        for group in range(basis // VECS):
            metric = column_of(start + group * basis + other)
            for v in range(VECS):
                value = value + projection[group * VECS + v] * metric[v : v + 1]
        inner.append(value)
    columns = []
    for u in range(VECS):
        value = square[u]
        for b in range(basis):
            value = value + inner[b] * projection[b][u : u + 1]
        columns.append(value)
    remainders = []
    for window, image in zip(windows, images):
        for b in range(basis):
            image = image - projection[b] * window[b : b + 1]
        remainders.append(image)
    row = lax.broadcasted_iota(jnp.int32, (VECS, LANES), 0)
    lane = lanes_of((VECS, LANES))
    record = total if at == 0 else pltpu.roll(total, LANES - at, 1)
    for j in range(VECS):
        pivot = columns[j][j : j + 1]
        scale = lax.rsqrt(pivot)
        lower = jnp.where(row > j, columns[j] * scale, 0.0)
        record = jnp.where(lane == basis + j, jnp.where(row == j, pivot * scale, lower), record)
        for u in range(j + 1, VECS):
            columns[u] = columns[u] - lower * lower[u : u + 1]
        for t, remainder in enumerate(remainders):
            solved = remainder[j : j + 1] * scale
            remainders[t] = jnp.where(row == j, solved, remainder - lower * solved)
    return remainders, record


def middle_kernel(
    trees,
    rows_all,
    near_col_ref,
    near_count_ref,
    far_col_ref,
    arrived_ref,
    window_ref,
    image_ref,
    window_coupled_ref,
    weights_ref,
    near_ref,
    u_ref,
    maps_ref,
    slots_ref,
    next_window_ref,
    near_part_ref,
    record_ref,
):
    own_tree = lax.axis_index("lvl")
    own_leaf = lax.axis_index("clus")
    window = window_ref[...]
    basis, size = window.shape
    rank = u_ref.shape[0]
    lane = lanes_of((VECS, LANES))
    group = lane // PIECE
    turns = LANES // PIECE
    tile_count = basis // VECS * (size // LANES)
    low_tiles, high_tiles = [], []
    total = jnp.zeros((VECS, LANES), F32)
    for slot in range(tile_count * turns):
        tail = arrived_ref[slot, :, size:]
        total = total + tail
        c = slot % turns
        turned = pltpu.roll(tail, PIECE * c, 1) if c else tail
        if c == 0:
            low_tiles.append(turned)
            high_tiles.append(turned)
        else:
            low_tiles[-1] = jnp.where(group == c, turned, low_tiles[-1])
            high_tiles[-1] = jnp.where(group == (c + 3) % turns, turned, high_tiles[-1])
    slots = arrived_ref.shape[0]
    if slots > tile_count * turns:
        total = lax.fori_loop(
            tile_count * turns, slots, lambda at, held: held + arrived_ref[at, :, size:], total
        )
    high_tiles = [pltpu.roll(tile, LANES - 3 * PIECE, 1) for tile in high_tiles]
    total = total * (1.0 / rows_all)

    def rows_from(tiles):
        per_row = size // LANES
        return [
            jnp.concatenate(tiles[at::per_row], axis=0) for at in range(per_row)
        ]

    leaves = slots // trees
    low_place = jnp.maximum(own_leaf - 1, 0) * trees + own_tree
    high_place = jnp.minimum(own_leaf + 1, leaves - 1) * trees + own_tree
    tails = jnp.concatenate(
        [arrived_ref[place, :, size:] for place in sources_of(far_col_ref, trees)], axis=1
    )
    tails = lane_parts(tails, lanes_of(tails.shape) % LANES // rank - (LANES // rank - 2))
    wide_lane = lanes_of(tails.shape) % LANES
    tails = jnp.where(wide_lane >= LANES - 2 * rank, tails, 0.0)
    coupled = couple(tails, weights_ref)
    images = [
        *lane_tiles(arrived_ref[low_place, :, :size]),
        *lane_tiles(image_ref[...]),
        *lane_tiles(arrived_ref[high_place, :, :size]),
        jnp.concatenate([coupled, jnp.zeros((VECS, LANES - rank), F32)], axis=1),
    ]
    windows = [
        *rows_from(low_tiles),
        *lane_tiles(window),
        *rows_from(high_tiles),
        window_coupled_ref[...],
    ]
    solved, record = orthogonalized(total, PIECE, windows, images)
    record_ref[...] = record
    per_row = size // LANES
    low_block, new_block, high_block = (
        jnp.concatenate(solved[at : at + per_row], axis=1)
        for at in range(0, 3 * per_row, per_row)
    )
    next_window = jnp.concatenate([window[VECS:], new_block], axis=0)
    next_window_ref[...] = next_window
    count = near_count_ref[0, 0]
    near_part = jnp.zeros((VECS, size), F32)
    for slot in range(near_ref.shape[0]):
        leaf = near_col_ref[0, 0, slot]
        source = jnp.where(leaf < own_leaf, low_block, jnp.where(leaf > own_leaf, high_block, new_block))
        source = jnp.where(slot < count, source, 0.0).astype(BF16)
        near_part = near_part + rows_dot(source, near_ref[slot])
    near_part_ref[...] = near_part
    far_part = jnp.dot(
        solved[-1][:, :rank].astype(BF16), u_ref[...], preferred_element_type=F32
    )
    skeleton, coarse = mapped(new_block.astype(BF16), maps_ref)
    packed = product_lanes(next_window, near_part + far_part, 0)
    tree_tail = jnp.where(lane < rank, packed, skeleton)
    level_tail = jnp.where(lane < rank, packed, coarse)

    def store(slot, at):
        slots_ref[slot] = level_tail

    over_slots(slots, store)

    def store_tree(leaf, at):
        slots_ref[leaf * trees + own_tree] = tree_tail

    over_slots(leaves, store_tree)


def end_kernel(
    trees,
    rows_all,
    far_col_ref,
    arrived_ref,
    window_ref,
    near_part_ref,
    weights_ref,
    u_ref,
    first_ref,
    block_ref,
    records_ref,
):
    rank = u_ref.shape[0]
    tails = jnp.concatenate(
        [arrived_ref[place] for place in sources_of(far_col_ref, trees)], axis=1
    )
    part = lanes_of(tails.shape) % LANES // rank - 1
    coupled = couple(jnp.where(part >= 0, lane_parts(tails, part), 0.0), weights_ref)
    far_part = jnp.dot(coupled.astype(BF16), u_ref[...], preferred_element_type=F32)
    slots = arrived_ref.shape[0]
    near = min(slots, UNROLL)
    total = arrived_ref[0]
    for slot in range(1, near):
        total = total + arrived_ref[slot]
    if slots > near:
        total = lax.fori_loop(near, slots, lambda at, held: held + arrived_ref[at], total)
    total = total * (1.0 / rows_all)
    image = near_part_ref[...] + far_part
    solved, record = orthogonalized(total, 0, lane_tiles(window_ref[...]), lane_tiles(image))
    store_rows(block_ref, jnp.concatenate(solved, axis=1))
    used = records_ref.shape[2]
    records_ref[0] = first_ref[:, :used]
    records_ref[1] = record[:, :used]


def call(kernel, name, outs, ins, places, scratch=(), vmem=16 << 20, bytes_accessed=1 << 20):
    spaces = {"s": pltpu.SMEM, "v": pltpu.VMEM, "h": pltpu.HBM}
    return pl.pallas_call(
        kernel,
        name=name,
        out_shape=[jax.ShapeDtypeStruct(shape, dtype) for shape, dtype in outs],
        in_specs=[pl.BlockSpec(memory_space=spaces[place]) for place in places],
        out_specs=[pl.BlockSpec(memory_space=pltpu.VMEM)] * len(outs),
        scratch_shapes=list(scratch),
        cost_estimate=pl.CostEstimate(flops=0, bytes_accessed=bytes_accessed, transcendentals=0),
        compiler_params=pltpu.CompilerParams(vmem_limit_bytes=vmem),
    )(*ins)


def exchange(slots):
    return lax.all_to_all(slots, AXES, 0, 0, tiled=True)


def local(
    krylov_basis,
    near_block,
    near_col,
    near_count,
    far_col,
    v_basis,
    u_basis,
    far_coupling,
    transfer,
    top_coupling,
):
    basis, _, size = krylov_basis.shape
    trees = lax.axis_size("lvl")
    devices = lax.axis_size("clus") * trees
    rows_all = float(devices * size)
    flat_basis = krylov_basis.reshape(-1, LANES)
    v_own, u_own, transfer_own = v_basis[0, 0], u_basis[0, 0], transfer[0, 0]
    rank = v_own.shape[0]
    far_own, top_own, near_own = far_coupling[0, 0], top_coupling[0, 0], near_block[0, 0]
    image_like = ((VECS, size), F32)
    window_like = ((basis, size), F32)
    record_like = ((VECS, LANES), F32)
    maps_like = ((4 * LANES, size), BF16)
    weights_like = ((3, rank, (far_own.shape[0] + trees) * LANES), BF16)
    slots, window = call(
        functools.partial(begin_kernel, trees),
        "begin",
        [((devices, VECS, size + 2 * LANES), BF16), window_like],
        [flat_basis, v_own, transfer_own],
        "hhh",
        [
            pltpu.VMEM(flat_basis.shape, F32),
            pltpu.VMEM(v_own.shape, BF16),
            pltpu.VMEM(transfer_own.shape, F32),
            pltpu.SemaphoreType.DMA((3,)),
        ],
        vmem=None,
    )
    arrived = exchange(slots)
    weights, near_here, maps = call(
        prepare_kernel,
        "prepare",
        [weights_like, (near_own.shape, BF16), maps_like],
        [near_col, near_count, far_col, near_own, far_own, v_own, transfer_own, top_own],
        "ssshvvvv",
        [pltpu.SemaphoreType.DMA],
    )
    image, slots, window_coupled = call(
        functools.partial(first_kernel, trees),
        "first",
        [image_like, ((devices, VECS, size + LANES), F32), ((basis, LANES), F32)],
        [
            near_col,
            near_count,
            far_col,
            arrived,
            window,
            weights,
            near_here,
            u_own,
            maps,
        ],
        "sssvvvvvv",
    )
    arrived = exchange(slots)
    slots, window, near_part, record = call(
        functools.partial(middle_kernel, trees, rows_all),
        "middle",
        [((devices, VECS, LANES), F32), window_like, image_like, record_like],
        [
            near_col,
            near_count,
            far_col,
            arrived,
            window,
            image,
            window_coupled,
            weights,
            near_here,
            u_own,
            maps,
        ],
        "sssvvvvvvvv",
    )
    arrived = exchange(slots)
    block, records = call(
        functools.partial(end_kernel, trees, rows_all),
        "end",
        [((VECS * size // LANES, LANES), F32), ((STEPS, VECS, basis + VECS), F32)],
        [far_col, arrived, window, near_part, weights, u_own, record],
        "svvvvvv",
    )
    return (block.reshape(VECS, 1, size), jnp.transpose(records, (0, 2, 1)))


def solution(mesh):
    return jax.shard_map(
        local,
        mesh=mesh,
        in_specs=(
            P(None, "lvl", "clus"),
            P("lvl", "clus", None, None, None),
            P("lvl", "clus", None),
            P("lvl", "clus"),
            P("lvl", "clus", None),
            P("lvl", "clus", None, None),
            P("lvl", "clus", None, None),
            P("lvl", "clus", None, None, None),
            P("lvl", "clus", None, None),
            P("lvl", "clus", None, None, None),
        ),
        out_specs=(P(None, "lvl", "clus"), P()),
        check_vma=False,
    )
```

```python
import functools

import jax
import jax.numpy as jnp
from jax import lax
from jax.experimental import pallas as pl
from jax.experimental.pallas import tpu as pltpu
from jax.sharding import PartitionSpec as P

VECS = 4
STEPS = 2
LANES = 128
PIECE = 16
UNROLL = 32
AXES = ("clus", "lvl")

PRECISE = lax.Precision.HIGHEST
ROWS_DIMS = (((1,), (1,)), ((), ()))
F32, BF16 = jnp.float32, jnp.bfloat16


def rows_dot(left, right, precision=None):
    return lax.dot_general(
        left, right, ROWS_DIMS, precision=precision, preferred_element_type=F32
    )


def precise_dot(left, right):
    return jnp.dot(left, right, precision=PRECISE, preferred_element_type=F32)


def three_parts(values):
    high = values.astype(BF16)
    rest = values - high.astype(F32)
    middle = rest.astype(BF16)
    low = (rest - middle.astype(F32)).astype(BF16)
    return high, middle, low


def lane_parts(values, part):
    high = values.astype(BF16).astype(F32)
    rest = values - high
    middle = rest.astype(BF16).astype(F32)
    low = rest - middle
    return jnp.where(part == 0, high, jnp.where(part == 1, middle, jnp.where(part == 2, low, 0.0)))


def lanes_of(shape):
    return lax.broadcasted_iota(jnp.int32, shape, len(shape) - 1)


def over_slots(count, store):
    step = min(count, UNROLL)
    if count == step:
        for slot in range(count):
            store(slot, slot)
        return

    def body(at, carry):
        for inner in range(step):
            store(at * step + inner, inner)
        return carry

    lax.fori_loop(0, count // step, body, 0)


def split_rows(flat, rows):
    halves = flat.shape[0] // rows
    return jnp.concatenate(
        [flat[pl.ds(half, rows, stride=halves), :] for half in range(halves)], axis=1
    )


def store_rows(flat_ref, values):
    rows = values.shape[0]
    halves = flat_ref.shape[0] // rows
    for half in range(halves):
        flat_ref[pl.ds(half, rows, stride=halves), :] = values[:, half * LANES : (half + 1) * LANES]


def row_groups(rows):
    return [rows[at : at + VECS] for at in range(0, rows.shape[0], VECS)]


def lane_tiles(values):
    return [values[:, at : at + LANES] for at in range(0, values.shape[1], LANES)]


def replicated(column):
    return jnp.broadcast_to(column, (column.shape[0], LANES))


def lane_sum(pairs):
    return replicated(jnp.sum(sum(left * right for left, right in pairs), axis=1, keepdims=True))


def begin_kernel(trees, basis_hbm, v_hbm, transfer_hbm, slots_ref, window_ref, *scratch):
    basis_ref, v_ref, transfer_ref, sems = scratch
    copies = [
        pltpu.make_async_copy(source, target, sems.at[at])
        for at, (source, target) in enumerate(
            ((basis_hbm, basis_ref), (v_hbm, v_ref), (transfer_hbm, transfer_ref))
        )
    ]
    for copy in copies:
        copy.start()
    for copy in copies:
        copy.wait()
    basis, size = window_ref.shape
    rank = v_ref.shape[0]
    window = split_rows(basis_ref, basis)
    window_ref[...] = window
    current = window[basis - VECS :]
    lowered = current.astype(BF16)
    rest = current - lowered.astype(F32)
    parts = [lowered, *three_parts(window[: basis - VECS]), *three_parts(rest)[:2]]
    parts = jnp.concatenate([part.astype(F32) for part in parts], axis=0).astype(BF16)
    repeats = LANES // rank
    wide_basis = jnp.concatenate([v_ref[...]] * repeats, axis=0)
    rows = row_groups(rows_dot(parts, wide_basis))
    skeletons = jnp.concatenate([rows[0], rows[1] + rows[2] + rows[3], rows[4] + rows[5]], axis=0)
    wide_transfer = jnp.concatenate([transfer_ref[...]] * repeats, axis=1)
    coarse = precise_dot(skeletons[:, :rank], wide_transfer)
    own_tree = lax.axis_index("lvl")

    def tails(values):
        exact, old, extra = row_groups(values)
        group = lanes_of((VECS, LANES)) // rank
        first = jnp.where(group < 3, lane_parts(exact, group), extra)
        return first.astype(BF16), lane_parts(old, group - (repeats - 2))

    tree_first, tree_second = tails(skeletons)
    level_first, level_second = tails(coarse)
    lane = lanes_of((VECS, LANES))
    turns = LANES // PIECE
    kept = lane >= LANES - 2 * rank
    tiles = [
        window[row : row + VECS, at : at + LANES]
        for row in range(0, basis, VECS)
        for at in range(0, size, LANES)
    ]
    turned = [
        [pltpu.roll(tile, (LANES - PIECE * c) % LANES, 1) if c else tile for c in range(turns)]
        for tile in tiles
    ]
    part = lane // PIECE

    def store(slot, at):
        tile = turned[at // turns % len(tiles)]
        c = at % turns
        copies_of = jnp.where(
            part == 0, tile[c], jnp.where(part == 1, tile[(c - 1) % turns], tile[(c - 2) % turns])
        )
        piece = lane_parts(copies_of, part)
        same = lax.rem(jnp.int32(slot), jnp.int32(trees)) == own_tree
        second = jnp.where(same, tree_second, level_second)
        slots_ref[slot, :, :size] = lowered
        slots_ref[slot, :, size : size + LANES] = level_first
        slots_ref[slot, :, size + LANES :] = jnp.where(kept, second, piece).astype(BF16)

    over_slots(slots_ref.shape[0], store)

    def store_tree(leaf, at):
        slots_ref[leaf * trees + own_tree, :, size : size + LANES] = tree_first

    over_slots(slots_ref.shape[0] // trees, store_tree)


def prepare_kernel(
    leaves,
    near_col_ref,
    near_count_ref,
    far_col_ref,
    near_hbm,
    far_coupling_ref,
    v_ref,
    transfer_ref,
    top_ref,
    weights_ref,
    near_ref,
    maps_ref,
    choice_ref,
    sem,
):
    copy = pltpu.make_async_copy(near_hbm, near_ref, sem)
    copy.start()
    own_tree = lax.axis_index("lvl")
    far_slots = far_coupling_ref.shape[0]
    trees, rank = top_ref.shape[0], top_ref.shape[1]
    transfer = transfer_ref[...]
    for slot in range(leaves + trees):
        if slot < leaves:
            block = jnp.zeros((rank, rank), F32)
            for at in range(far_slots):
                block = block + jnp.where(far_col_ref[0, 0, at] == slot, far_coupling_ref[at], 0.0)
        else:
            tree = slot - leaves
            block = precise_dot(transfer, jnp.where(tree != own_tree, top_ref[tree], 0.0))
        wide = jnp.concatenate([block] * (LANES // rank), axis=1)
        for part, piece in enumerate(three_parts(wide)):
            weights_ref[part, :, slot * LANES : (slot + 1) * LANES] = piece
    v_basis = v_ref[...]
    carried = precise_dot(transfer.T, v_basis.astype(F32))
    for part, piece in enumerate((v_basis, *three_parts(carried))):
        for at in range(part * LANES, (part + 1) * LANES, rank):
            maps_ref[at : at + rank] = piece
    own_leaf = lax.axis_index("clus")
    count = near_count_ref[0, 0]
    rows = lax.broadcasted_iota(jnp.int32, choice_ref.shape, 0)
    choice = jnp.zeros(choice_ref.shape, F32)
    for slot in range(near_ref.shape[0]):
        for side in range(3):
            wanted = (near_col_ref[0, 0, slot] == own_leaf + side - 1) & (slot < count)
            choice = jnp.where(rows == 3 * slot + side, jnp.where(wanted, 1.0, 0.0), choice)
    choice_ref[...] = choice
    copy.wait()


def places_of(leaves, trees):
    own_tree = lax.axis_index("lvl")
    own_leaf = lax.axis_index("clus")
    places = [leaf * trees + own_tree for leaf in range(leaves)]
    return places + [own_leaf * trees + tree for tree in range(trees)]


def near_places(leaves, trees):
    own_tree = lax.axis_index("lvl")
    own_leaf = lax.axis_index("clus")
    low = jnp.maximum(own_leaf - 1, 0)
    high = jnp.minimum(own_leaf + 1, leaves - 1)
    return [leaf * trees + own_tree for leaf in (low, own_leaf, high)]


def near_field(blocks, choice_ref, near_ref):
    choice = choice_ref[...]
    blocks = [[tile.astype(F32) for tile in lane_tiles(block)] for block in blocks]
    result = None
    for slot in range(near_ref.shape[0]):
        rows = [choice[3 * slot + side : 3 * slot + side + 1] for side in range(3)]
        tiles = [sum(tile * row for tile, row in zip(sides, rows)) for sides in zip(*blocks)]
        part = rows_dot(jnp.concatenate(tiles, axis=1).astype(BF16), near_ref[slot])
        result = part if result is None else result + part
    return result


def couple(values, weights_ref):
    lowered = values.astype(BF16)
    return sum(rows_dot(lowered, weights_ref[part]) for part in range(3))


def product_lanes(window, image, at):
    basis = window.shape[0]
    window, image = lane_tiles(window), lane_tiles(image)
    lane = lanes_of((VECS, LANES))
    packed = jnp.zeros((VECS, LANES), F32)
    for b in range(basis):
        product = lane_sum([(tile, other[b : b + 1]) for tile, other in zip(image, window)])
        packed = jnp.where(lane == at + b, product, packed)
    at = at + basis
    for u in range(VECS):
        product = lane_sum([(tile, tile[u : u + 1]) for tile in image])
        packed = jnp.where(lane == at + u, product, packed)
    at = at + VECS
    for b in range(basis):
        product = lane_sum([(tile, tile[b : b + 1]) for tile in window])
        for group in range(basis // VECS):
            rows = product[group * VECS : (group + 1) * VECS]
            packed = jnp.where(lane == at + group * basis + b, rows, packed)
    return packed


def mapped(rows, maps_ref):
    products = lane_tiles(rows_dot(rows, maps_ref[...]))
    skeleton, coarse = products[0], products[1] + products[2] + products[3]
    return sum(row_groups(skeleton)), sum(row_groups(coarse))


def first_kernel(
    trees,
    arrived_ref,
    window_ref,
    weights_ref,
    near_ref,
    choice_ref,
    u_ref,
    maps_ref,
    image_ref,
    slots_ref,
    window_coupled_ref,
):
    own_tree = lax.axis_index("lvl")
    size = near_ref.shape[1]
    rank = u_ref.shape[0]
    leaves = arrived_ref.shape[0] // trees
    places = places_of(leaves, trees)
    first = [arrived_ref[place, :, size : size + LANES] for place in places]
    second = [arrived_ref[place, :, size + LANES :] for place in places]
    first = jnp.concatenate(first, axis=1).astype(F32)
    second = jnp.concatenate(second, axis=1).astype(F32)
    lane = lanes_of(first.shape) % LANES
    exact = jnp.where(lane < 3 * rank, first, 0.0)
    old = jnp.where(lane >= LANES - 2 * rank, second, 0.0)
    rows = couple(jnp.concatenate([exact, first, old], axis=0), weights_ref)
    linear = jnp.concatenate([rows[2 * VECS :], rows[VECS : 2 * VECS]], axis=0)
    blank = jnp.zeros((2 * VECS, LANES - rank), F32)
    window_coupled_ref[...] = jnp.concatenate([linear, blank], axis=1)
    image = jnp.dot(rows[:VECS].astype(BF16), u_ref[...], preferred_element_type=F32)
    blocks = [arrived_ref[place, :, :size] for place in near_places(leaves, trees)]
    image = image + near_field(blocks, choice_ref, near_ref)
    image_ref[...] = image
    packed = product_lanes(window_ref[...], image, PIECE)
    parts = [part.astype(F32) for part in three_parts(image)]
    skeleton, coarse = mapped(jnp.concatenate(parts, axis=0).astype(BF16), maps_ref)
    kept = lanes_of((VECS, LANES)) < LANES - 2 * rank
    tree_tail = jnp.where(kept, packed, skeleton)
    level_tail = jnp.where(kept, packed, coarse)
    narrow = lanes_of((VECS, LANES))
    from_low = narrow < PIECE
    from_high = (narrow >= 3 * PIECE) & (narrow < 4 * PIECE)
    total = slots_ref.shape[0]

    def store(slot, at):
        if isinstance(slot, int):
            low, high = max(slot - trees, 0), min(slot + trees, total - 1)
        else:
            low, high = jnp.maximum(slot - trees, 0), jnp.minimum(slot + trees, total - 1)
        low = arrived_ref[low, :, size + LANES :].astype(F32)
        high = arrived_ref[high, :, size + LANES :].astype(F32)
        both = jnp.where(narrow < 3 * PIECE, low, pltpu.roll(high, 3 * PIECE, 1))
        both = both + pltpu.roll(both, LANES - PIECE, 1) + pltpu.roll(both, LANES - 2 * PIECE, 1)
        same = lax.rem(jnp.int32(slot), jnp.int32(trees)) == own_tree
        tail = jnp.where(same, tree_tail, level_tail)
        slots_ref[slot, :, :size] = image
        slots_ref[slot, :, size:] = jnp.where(from_low | from_high, both, tail)

    over_slots(total, store)


def orthogonalized(total, at, windows, images):
    basis = windows[0].shape[0]

    def column_of(lane):
        return replicated(total[:, lane : lane + 1])

    projection = [column_of(at + b) for b in range(basis)]
    square = [column_of(at + basis + u) for u in range(VECS)]
    start = at + basis + VECS
    inner = []
    for other in range(basis):
        value = -2.0 * projection[other]
        for group in range(basis // VECS):
            metric = column_of(start + group * basis + other)
            for v in range(VECS):
                value = value + projection[group * VECS + v] * metric[v : v + 1]
        inner.append(value)
    columns = []
    for u in range(VECS):
        value = square[u]
        for b in range(basis):
            value = value + inner[b] * projection[b][u : u + 1]
        columns.append(value)
    remainders = []
    for window, image in zip(windows, images):
        for b in range(basis):
            image = image - projection[b] * window[b : b + 1]
        remainders.append(image)
    row = lax.broadcasted_iota(jnp.int32, (VECS, LANES), 0)
    lane = lanes_of((VECS, LANES))
    record = total if at == 0 else pltpu.roll(total, LANES - at, 1)
    for j in range(VECS):
        pivot = columns[j][j : j + 1]
        scale = lax.rsqrt(pivot)
        lower = jnp.where(row > j, columns[j] * scale, 0.0)
        record = jnp.where(lane == basis + j, jnp.where(row == j, pivot * scale, lower), record)
        for u in range(j + 1, VECS):
            columns[u] = columns[u] - lower * lower[u : u + 1]
        for t, remainder in enumerate(remainders):
            solved = remainder[j : j + 1] * scale
            remainders[t] = jnp.where(row == j, solved, remainder - lower * solved)
    return remainders, record


def middle_kernel(
    trees,
    rows_all,
    arrived_ref,
    window_ref,
    image_ref,
    window_coupled_ref,
    weights_ref,
    near_ref,
    choice_ref,
    u_ref,
    maps_ref,
    slots_ref,
    next_window_ref,
    near_part_ref,
    record_ref,
):
    own_tree = lax.axis_index("lvl")
    window = window_ref[...]
    basis, size = window.shape
    rank = u_ref.shape[0]
    lane = lanes_of((VECS, LANES))
    group = lane // PIECE
    turns = LANES // PIECE
    tile_count = basis // VECS * (size // LANES)
    low_tiles, high_tiles = [], []
    total = jnp.zeros((VECS, LANES), F32)
    for slot in range(tile_count * turns):
        tail = arrived_ref[slot, :, size:]
        total = total + tail
        c = slot % turns
        turned = pltpu.roll(tail, PIECE * c, 1) if c else tail
        if c == 0:
            low_tiles.append(turned)
            high_tiles.append(turned)
        else:
            low_tiles[-1] = jnp.where(group == c, turned, low_tiles[-1])
            high_tiles[-1] = jnp.where(group == (c + 3) % turns, turned, high_tiles[-1])
    slots = arrived_ref.shape[0]
    if slots > tile_count * turns:
        total = lax.fori_loop(
            tile_count * turns, slots, lambda at, held: held + arrived_ref[at, :, size:], total
        )
    high_tiles = [pltpu.roll(tile, LANES - 3 * PIECE, 1) for tile in high_tiles]
    total = total * (1.0 / rows_all)

    def rows_from(tiles):
        per_row = size // LANES
        return [
            jnp.concatenate(tiles[at::per_row], axis=0) for at in range(per_row)
        ]

    leaves = slots // trees
    low_place, _, high_place = near_places(leaves, trees)
    tails = jnp.concatenate(
        [arrived_ref[place, :, size:] for place in places_of(leaves, trees)], axis=1
    )
    tails = lane_parts(tails, lanes_of(tails.shape) % LANES // rank - (LANES // rank - 2))
    wide_lane = lanes_of(tails.shape) % LANES
    tails = jnp.where(wide_lane >= LANES - 2 * rank, tails, 0.0)
    coupled = couple(tails, weights_ref)
    images = [
        *lane_tiles(arrived_ref[low_place, :, :size]),
        *lane_tiles(image_ref[...]),
        *lane_tiles(arrived_ref[high_place, :, :size]),
        jnp.concatenate([coupled, jnp.zeros((VECS, LANES - rank), F32)], axis=1),
    ]
    windows = [
        *rows_from(low_tiles),
        *lane_tiles(window),
        *rows_from(high_tiles),
        window_coupled_ref[...],
    ]
    solved, record = orthogonalized(total, PIECE, windows, images)
    record_ref[...] = record
    per_row = size // LANES
    low_block, new_block, high_block = (
        jnp.concatenate(solved[at : at + per_row], axis=1)
        for at in range(0, 3 * per_row, per_row)
    )
    next_window = jnp.concatenate([window[VECS:], new_block], axis=0)
    next_window_ref[...] = next_window
    blocks = [block.astype(BF16) for block in (low_block, new_block, high_block)]
    near_part = near_field(blocks, choice_ref, near_ref)
    near_part_ref[...] = near_part
    far_part = jnp.dot(
        solved[-1][:, :rank].astype(BF16), u_ref[...], preferred_element_type=F32
    )
    skeleton, coarse = mapped(new_block.astype(BF16), maps_ref)
    packed = product_lanes(next_window, near_part + far_part, 0)
    tree_tail = jnp.where(lane < rank, packed, skeleton)
    level_tail = jnp.where(lane < rank, packed, coarse)

    def store(slot, at):
        slots_ref[slot] = level_tail

    over_slots(slots, store)

    def store_tree(leaf, at):
        slots_ref[leaf * trees + own_tree] = tree_tail

    over_slots(leaves, store_tree)


def end_kernel(
    trees,
    rows_all,
    arrived_ref,
    window_ref,
    near_part_ref,
    weights_ref,
    u_ref,
    first_ref,
    block_ref,
    records_ref,
):
    rank = u_ref.shape[0]
    leaves = arrived_ref.shape[0] // trees
    tails = jnp.concatenate(
        [arrived_ref[place] for place in places_of(leaves, trees)], axis=1
    )
    part = lanes_of(tails.shape) % LANES // rank - 1
    coupled = couple(jnp.where(part >= 0, lane_parts(tails, part), 0.0), weights_ref)
    far_part = jnp.dot(coupled.astype(BF16), u_ref[...], preferred_element_type=F32)
    slots = arrived_ref.shape[0]
    near = min(slots, UNROLL)
    total = arrived_ref[0]
    for slot in range(1, near):
        total = total + arrived_ref[slot]
    if slots > near:
        total = lax.fori_loop(near, slots, lambda at, held: held + arrived_ref[at], total)
    total = total * (1.0 / rows_all)
    image = near_part_ref[...] + far_part
    solved, record = orthogonalized(total, 0, lane_tiles(window_ref[...]), lane_tiles(image))
    store_rows(block_ref, jnp.concatenate(solved, axis=1))
    used = records_ref.shape[2]
    records_ref[0] = first_ref[:, :used]
    records_ref[1] = record[:, :used]


def call(kernel, name, outs, ins, places, scratch=(), vmem=16 << 20, bytes_accessed=1 << 20):
    spaces = {"s": pltpu.SMEM, "v": pltpu.VMEM, "h": pltpu.HBM}
    return pl.pallas_call(
        kernel,
        name=name,
        out_shape=[jax.ShapeDtypeStruct(shape, dtype) for shape, dtype in outs],
        in_specs=[pl.BlockSpec(memory_space=spaces[place]) for place in places],
        out_specs=[pl.BlockSpec(memory_space=pltpu.VMEM)] * len(outs),
        scratch_shapes=list(scratch),
        cost_estimate=pl.CostEstimate(flops=0, bytes_accessed=bytes_accessed, transcendentals=0),
        compiler_params=pltpu.CompilerParams(vmem_limit_bytes=vmem),
    )(*ins)


def exchange(slots):
    return lax.all_to_all(slots, AXES, 0, 0, tiled=True)


def local(
    krylov_basis,
    near_block,
    near_col,
    near_count,
    far_col,
    v_basis,
    u_basis,
    far_coupling,
    transfer,
    top_coupling,
):
    basis, _, size = krylov_basis.shape
    trees = lax.axis_size("lvl")
    leaves = lax.axis_size("clus")
    devices = leaves * trees
    rows_all = float(devices * size)
    flat_basis = krylov_basis.reshape(-1, LANES)
    v_own, u_own, transfer_own = v_basis[0, 0], u_basis[0, 0], transfer[0, 0]
    rank = v_own.shape[0]
    far_own, top_own, near_own = far_coupling[0, 0], top_coupling[0, 0], near_block[0, 0]
    image_like = ((VECS, size), F32)
    window_like = ((basis, size), F32)
    record_like = ((VECS, LANES), F32)
    maps_like = ((4 * LANES, size), BF16)
    choice_like = ((-(-3 * near_own.shape[0] // 8) * 8, LANES), F32)
    weights_like = ((3, rank, (leaves + trees) * LANES), BF16)
    slots, window = call(
        functools.partial(begin_kernel, trees),
        "begin",
        [((devices, VECS, size + 2 * LANES), BF16), window_like],
        [flat_basis, v_own, transfer_own],
        "hhh",
        [
            pltpu.VMEM(flat_basis.shape, F32),
            pltpu.VMEM(v_own.shape, BF16),
            pltpu.VMEM(transfer_own.shape, F32),
            pltpu.SemaphoreType.DMA((3,)),
        ],
        vmem=None,
    )
    arrived = exchange(slots)
    weights, near_here, maps, choice = call(
        functools.partial(prepare_kernel, leaves),
        "prepare",
        [weights_like, (near_own.shape, BF16), maps_like, choice_like],
        [near_col, near_count, far_col, near_own, far_own, v_own, transfer_own, top_own],
        "ssshvvvv",
        [pltpu.SemaphoreType.DMA],
    )
    image, slots, window_coupled = call(
        functools.partial(first_kernel, trees),
        "first",
        [image_like, ((devices, VECS, size + LANES), F32), ((basis, LANES), F32)],
        [
            arrived,
            window,
            weights,
            near_here,
            choice,
            u_own,
            maps,
        ],
        "v" * 7,
    )
    arrived = exchange(slots)
    slots, window, near_part, record = call(
        functools.partial(middle_kernel, trees, rows_all),
        "middle",
        [((devices, VECS, LANES), F32), window_like, image_like, record_like],
        [
            arrived,
            window,
            image,
            window_coupled,
            weights,
            near_here,
            choice,
            u_own,
            maps,
        ],
        "v" * 9,
    )
    arrived = exchange(slots)
    block, records = call(
        functools.partial(end_kernel, trees, rows_all),
        "end",
        [((VECS * size // LANES, LANES), F32), ((STEPS, VECS, basis + VECS), F32)],
        [arrived, window, near_part, weights, u_own, record],
        "v" * 6,
    )
    return (block.reshape(VECS, 1, size), jnp.transpose(records, (0, 2, 1)))


def solution(mesh):
    return jax.shard_map(
        local,
        mesh=mesh,
        in_specs=(
            P(None, "lvl", "clus"),
            P("lvl", "clus", None, None, None),
            P("lvl", "clus", None),
            P("lvl", "clus"),
            P("lvl", "clus", None),
            P("lvl", "clus", None, None),
            P("lvl", "clus", None, None),
            P("lvl", "clus", None, None, None),
            P("lvl", "clus", None, None),
            P("lvl", "clus", None, None, None),
        ),
        out_specs=(P(None, "lvl", "clus"), P()),
        check_vma=False,
    )
```

```python
import functools

import jax
import jax.numpy as jnp
from jax import lax
from jax.experimental import pallas as pl
from jax.experimental.pallas import tpu as pltpu
from jax.sharding import PartitionSpec as P

VECS = 4
STEPS = 2
LANES = 128
PIECE = 16
UNROLL = 32
AXES = ("lvl", "clus")

PRECISE = lax.Precision.HIGHEST
ROWS_DIMS = (((1,), (1,)), ((), ()))
F32, BF16 = jnp.float32, jnp.bfloat16


def rows_dot(left, right, precision=None):
    return lax.dot_general(
        left, right, ROWS_DIMS, precision=precision, preferred_element_type=F32
    )


def precise_dot(left, right):
    return jnp.dot(left, right, precision=PRECISE, preferred_element_type=F32)


def three_parts(values):
    high = values.astype(BF16)
    rest = values - high.astype(F32)
    middle = rest.astype(BF16)
    low = (rest - middle.astype(F32)).astype(BF16)
    return high, middle, low


def lane_parts(values, part):
    high = values.astype(BF16).astype(F32)
    rest = values - high
    middle = rest.astype(BF16).astype(F32)
    low = rest - middle
    return jnp.where(part == 0, high, jnp.where(part == 1, middle, jnp.where(part == 2, low, 0.0)))


def lanes_of(shape):
    return lax.broadcasted_iota(jnp.int32, shape, len(shape) - 1)


def over_slots(count, store):
    step = min(count, UNROLL)
    if count == step:
        for slot in range(count):
            store(slot, slot)
        return

    def body(at, carry):
        for inner in range(step):
            store(at * step + inner, inner)
        return carry

    lax.fori_loop(0, count // step, body, 0)


def split_rows(flat, rows):
    halves = flat.shape[0] // rows
    return jnp.concatenate(
        [flat[pl.ds(half, rows, stride=halves), :] for half in range(halves)], axis=1
    )


def store_rows(flat_ref, values):
    rows = values.shape[0]
    halves = flat_ref.shape[0] // rows
    for half in range(halves):
        flat_ref[pl.ds(half, rows, stride=halves), :] = values[:, half * LANES : (half + 1) * LANES]


def row_groups(rows):
    return [rows[at : at + VECS] for at in range(0, rows.shape[0], VECS)]


def lane_tiles(values):
    return [values[:, at : at + LANES] for at in range(0, values.shape[1], LANES)]


def replicated(column):
    return jnp.broadcast_to(column, (column.shape[0], LANES))


def lane_sum(pairs):
    return replicated(jnp.sum(sum(left * right for left, right in pairs), axis=1, keepdims=True))


def begin_kernel(leaves, basis_hbm, v_hbm, transfer_hbm, slots_ref, window_ref, *scratch):
    basis_ref, v_ref, transfer_ref, sems = scratch
    copies = [
        pltpu.make_async_copy(source, target, sems.at[at])
        for at, (source, target) in enumerate(
            ((basis_hbm, basis_ref), (v_hbm, v_ref), (transfer_hbm, transfer_ref))
        )
    ]
    for copy in copies:
        copy.start()
    for copy in copies:
        copy.wait()
    basis, size = window_ref.shape
    rank = v_ref.shape[0]
    window = split_rows(basis_ref, basis)
    window_ref[...] = window
    current = window[basis - VECS :]
    lowered = current.astype(BF16)
    rest = current - lowered.astype(F32)
    parts = [lowered, *three_parts(window[: basis - VECS]), *three_parts(rest)[:2]]
    parts = jnp.concatenate([part.astype(F32) for part in parts], axis=0).astype(BF16)
    repeats = LANES // rank
    wide_basis = jnp.concatenate([v_ref[...]] * repeats, axis=0)
    rows = row_groups(rows_dot(parts, wide_basis))
    skeletons = jnp.concatenate([rows[0], rows[1] + rows[2] + rows[3], rows[4] + rows[5]], axis=0)
    wide_transfer = jnp.concatenate([transfer_ref[...]] * repeats, axis=1)
    coarse = precise_dot(skeletons[:, :rank], wide_transfer)
    own_tree = lax.axis_index("lvl")

    def tails(values):
        exact, old, extra = row_groups(values)
        group = lanes_of((VECS, LANES)) // rank
        first = jnp.where(group < 3, lane_parts(exact, group), extra)
        return first.astype(BF16), lane_parts(old, group - (repeats - 2))

    tree_first, tree_second = tails(skeletons)
    level_first, level_second = tails(coarse)
    lane = lanes_of((VECS, LANES))
    turns = LANES // PIECE
    kept = lane >= LANES - 2 * rank
    tiles = [
        window[row : row + VECS, at : at + LANES]
        for row in range(0, basis, VECS)
        for at in range(0, size, LANES)
    ]
    turned = [
        [pltpu.roll(tile, (LANES - PIECE * c) % LANES, 1) if c else tile for c in range(turns)]
        for tile in tiles
    ]
    part = lane // PIECE

    def store(slot, at):
        tile = turned[at // turns % len(tiles)]
        c = at % turns
        copies_of = jnp.where(
            part == 0, tile[c], jnp.where(part == 1, tile[(c - 1) % turns], tile[(c - 2) % turns])
        )
        piece = lane_parts(copies_of, part)
        same = lax.div(jnp.int32(slot), jnp.int32(leaves)) == own_tree
        second = jnp.where(same, tree_second, level_second)
        slots_ref[slot, :, :size] = lowered
        slots_ref[slot, :, size : size + LANES] = level_first
        slots_ref[slot, :, size + LANES :] = jnp.where(kept, second, piece).astype(BF16)

    over_slots(slots_ref.shape[0], store)

    def store_tree(leaf, at):
        slots_ref[own_tree * leaves + leaf, :, size : size + LANES] = tree_first

    over_slots(leaves, store_tree)


def prepare_kernel(
    leaves,
    near_col_ref,
    near_count_ref,
    far_col_ref,
    near_hbm,
    far_coupling_ref,
    v_ref,
    transfer_ref,
    top_ref,
    weights_ref,
    near_ref,
    maps_ref,
    choice_ref,
    sem,
):
    copy = pltpu.make_async_copy(near_hbm, near_ref, sem)
    copy.start()
    own_tree = lax.axis_index("lvl")
    far_slots = far_coupling_ref.shape[0]
    trees, rank = top_ref.shape[0], top_ref.shape[1]
    transfer = transfer_ref[...]
    for slot in range(leaves + trees):
        if slot < leaves:
            block = jnp.zeros((rank, rank), F32)
            for at in range(far_slots):
                block = block + jnp.where(far_col_ref[0, 0, at] == slot, far_coupling_ref[at], 0.0)
        else:
            tree = slot - leaves
            block = precise_dot(transfer, jnp.where(tree != own_tree, top_ref[tree], 0.0))
        wide = jnp.concatenate([block] * (LANES // rank), axis=1)
        for part, piece in enumerate(three_parts(wide)):
            weights_ref[part, :, slot * LANES : (slot + 1) * LANES] = piece
    v_basis = v_ref[...]
    carried = precise_dot(transfer.T, v_basis.astype(F32))
    for part, piece in enumerate((v_basis, *three_parts(carried))):
        for at in range(part * LANES, (part + 1) * LANES, rank):
            maps_ref[at : at + rank] = piece
    own_leaf = lax.axis_index("clus")
    count = near_count_ref[0, 0]
    rows = lax.broadcasted_iota(jnp.int32, choice_ref.shape, 0)
    choice = jnp.zeros(choice_ref.shape, F32)
    for slot in range(near_ref.shape[0]):
        for side in range(3):
            wanted = (near_col_ref[0, 0, slot] == own_leaf + side - 1) & (slot < count)
            choice = jnp.where(rows == 3 * slot + side, jnp.where(wanted, 1.0, 0.0), choice)
    choice_ref[...] = choice
    copy.wait()


def places_of(leaves, trees):
    own_tree = lax.axis_index("lvl")
    own_leaf = lax.axis_index("clus")
    places = [own_tree * leaves + leaf for leaf in range(leaves)]
    return places + [tree * leaves + own_leaf for tree in range(trees)]


def near_places(leaves):
    start = lax.axis_index("lvl") * leaves
    own_leaf = lax.axis_index("clus")
    low = jnp.maximum(own_leaf - 1, 0)
    high = jnp.minimum(own_leaf + 1, leaves - 1)
    return [start + leaf for leaf in (low, own_leaf, high)]


def near_field(blocks, choice_ref, near_ref):
    choice = choice_ref[...]
    blocks = [[tile.astype(F32) for tile in lane_tiles(block)] for block in blocks]
    result = None
    for slot in range(near_ref.shape[0]):
        rows = [choice[3 * slot + side : 3 * slot + side + 1] for side in range(3)]
        tiles = [sum(tile * row for tile, row in zip(sides, rows)) for sides in zip(*blocks)]
        part = rows_dot(jnp.concatenate(tiles, axis=1).astype(BF16), near_ref[slot])
        result = part if result is None else result + part
    return result


def couple(values, weights_ref):
    lowered = values.astype(BF16)
    return sum(rows_dot(lowered, weights_ref[part]) for part in range(3))


def product_lanes(window, image, at, period=LANES):
    basis = window.shape[0]
    window, image = lane_tiles(window), lane_tiles(image)
    lane = lanes_of((VECS, LANES)) % period
    packed = jnp.zeros((VECS, LANES), F32)
    for b in range(basis):
        product = lane_sum([(tile, other[b : b + 1]) for tile, other in zip(image, window)])
        packed = jnp.where(lane == at + b, product, packed)
    at = at + basis
    for u in range(VECS):
        product = lane_sum([(tile, tile[u : u + 1]) for tile in image])
        packed = jnp.where(lane == at + u, product, packed)
    at = at + VECS
    for b in range(basis):
        product = lane_sum([(tile, tile[b : b + 1]) for tile in window])
        for group in range(basis // VECS):
            rows = product[group * VECS : (group + 1) * VECS]
            packed = jnp.where(lane == at + group * basis + b, rows, packed)
    return packed


def one_row(values):
    width = LANES // VECS
    own = lanes_of(values.shape) // width == lax.broadcasted_iota(jnp.int32, values.shape, 0)
    return jnp.sum(jnp.where(own, values, 0.0), axis=0, keepdims=True)


def mapped(rows, maps_ref):
    products = lane_tiles(rows_dot(rows, maps_ref[...]))
    skeleton, coarse = products[0], products[1] + products[2] + products[3]
    return sum(row_groups(skeleton)), sum(row_groups(coarse))


def first_kernel(
    trees,
    arrived_ref,
    window_ref,
    weights_ref,
    near_ref,
    choice_ref,
    u_ref,
    maps_ref,
    image_ref,
    slots_ref,
    window_coupled_ref,
):
    own_tree = lax.axis_index("lvl")
    size = near_ref.shape[1]
    rank = u_ref.shape[0]
    leaves = arrived_ref.shape[0] // trees
    places = places_of(leaves, trees)
    first = [arrived_ref[place, :, size : size + LANES] for place in places]
    second = [arrived_ref[place, :, size + LANES :] for place in places]
    first = jnp.concatenate(first, axis=1).astype(F32)
    second = jnp.concatenate(second, axis=1).astype(F32)
    lane = lanes_of(first.shape) % LANES
    exact = jnp.where(lane < 3 * rank, first, 0.0)
    old = jnp.where(lane >= LANES - 2 * rank, second, 0.0)
    rows = couple(jnp.concatenate([exact, first, old], axis=0), weights_ref)
    linear = jnp.concatenate([rows[2 * VECS :], rows[VECS : 2 * VECS]], axis=0)
    blank = jnp.zeros((2 * VECS, LANES - rank), F32)
    window_coupled_ref[...] = jnp.concatenate([linear, blank], axis=1)
    image = jnp.dot(rows[:VECS].astype(BF16), u_ref[...], preferred_element_type=F32)
    blocks = [arrived_ref[place, :, :size] for place in near_places(leaves)]
    image = image + near_field(blocks, choice_ref, near_ref)
    image_ref[...] = image
    packed = product_lanes(window_ref[...], image, PIECE)
    parts = [part.astype(F32) for part in three_parts(image)]
    skeleton, coarse = mapped(jnp.concatenate(parts, axis=0).astype(BF16), maps_ref)
    kept = lanes_of((VECS, LANES)) < LANES - 2 * rank
    tree_tail = jnp.where(kept, packed, skeleton)
    level_tail = jnp.where(kept, packed, coarse)
    narrow = lanes_of((VECS, LANES))
    from_low = narrow < PIECE
    from_high = (narrow >= 3 * PIECE) & (narrow < 4 * PIECE)
    total = slots_ref.shape[0]

    def store(slot, at):
        if isinstance(slot, int):
            low, high = max(slot - 1, 0), min(slot + 1, total - 1)
        else:
            low, high = jnp.maximum(slot - 1, 0), jnp.minimum(slot + 1, total - 1)
        low = arrived_ref[low, :, size + LANES :].astype(F32)
        high = arrived_ref[high, :, size + LANES :].astype(F32)
        both = jnp.where(narrow < 3 * PIECE, low, pltpu.roll(high, 3 * PIECE, 1))
        both = both + pltpu.roll(both, LANES - PIECE, 1) + pltpu.roll(both, LANES - 2 * PIECE, 1)
        same = lax.div(jnp.int32(slot), jnp.int32(leaves)) == own_tree
        tail = jnp.where(same, tree_tail, level_tail)
        slots_ref[slot, :, :size] = image
        slots_ref[slot, :, size:] = jnp.where(from_low | from_high, both, tail)

    over_slots(total, store)


def orthogonalized(total, at, windows, images):
    basis = windows[0].shape[0]

    def column_of(lane):
        return replicated(total[:, lane : lane + 1])

    projection = [column_of(at + b) for b in range(basis)]
    square = [column_of(at + basis + u) for u in range(VECS)]
    start = at + basis + VECS
    inner = []
    for other in range(basis):
        value = -2.0 * projection[other]
        for group in range(basis // VECS):
            metric = column_of(start + group * basis + other)
            for v in range(VECS):
                value = value + projection[group * VECS + v] * metric[v : v + 1]
        inner.append(value)
    columns = []
    for u in range(VECS):
        value = square[u]
        for b in range(basis):
            value = value + inner[b] * projection[b][u : u + 1]
        columns.append(value)
    remainders = []
    for window, image in zip(windows, images):
        for b in range(basis):
            image = image - projection[b] * window[b : b + 1]
        remainders.append(image)
    row = lax.broadcasted_iota(jnp.int32, (VECS, LANES), 0)
    lane = lanes_of((VECS, LANES))
    record = total if at == 0 else pltpu.roll(total, LANES - at, 1)
    for j in range(VECS):
        pivot = columns[j][j : j + 1]
        scale = lax.rsqrt(pivot)
        lower = jnp.where(row > j, columns[j] * scale, 0.0)
        record = jnp.where(lane == basis + j, jnp.where(row == j, pivot * scale, lower), record)
        for u in range(j + 1, VECS):
            columns[u] = columns[u] - lower * lower[u : u + 1]
        for t, remainder in enumerate(remainders):
            solved = remainder[j : j + 1] * scale
            remainders[t] = jnp.where(row == j, solved, remainder - lower * solved)
    return remainders, record


def middle_kernel(
    trees,
    rows_all,
    arrived_ref,
    window_ref,
    image_ref,
    window_coupled_ref,
    weights_ref,
    near_ref,
    choice_ref,
    u_ref,
    maps_ref,
    slots_ref,
    next_window_ref,
    near_part_ref,
    record_ref,
):
    own_tree = lax.axis_index("lvl")
    window = window_ref[...]
    basis, size = window.shape
    rank = u_ref.shape[0]
    lane = lanes_of((VECS, LANES))
    group = lane // PIECE
    turns = LANES // PIECE
    tile_count = basis // VECS * (size // LANES)
    low_tiles, high_tiles = [], []
    total = jnp.zeros((VECS, LANES), F32)
    for slot in range(tile_count * turns):
        tail = arrived_ref[slot, :, size:]
        total = total + tail
        c = slot % turns
        turned = pltpu.roll(tail, PIECE * c, 1) if c else tail
        if c == 0:
            low_tiles.append(turned)
            high_tiles.append(turned)
        else:
            low_tiles[-1] = jnp.where(group == c, turned, low_tiles[-1])
            high_tiles[-1] = jnp.where(group == (c + 3) % turns, turned, high_tiles[-1])
    slots = arrived_ref.shape[0]
    if slots > tile_count * turns:
        total = lax.fori_loop(
            tile_count * turns, slots, lambda at, held: held + arrived_ref[at, :, size:], total
        )
    high_tiles = [pltpu.roll(tile, LANES - 3 * PIECE, 1) for tile in high_tiles]
    total = total * (1.0 / rows_all)

    def rows_from(tiles):
        per_row = size // LANES
        return [
            jnp.concatenate(tiles[at::per_row], axis=0) for at in range(per_row)
        ]

    leaves = slots // trees
    low_place, _, high_place = near_places(leaves)
    tails = jnp.concatenate(
        [arrived_ref[place, :, size:] for place in places_of(leaves, trees)], axis=1
    )
    tails = lane_parts(tails, lanes_of(tails.shape) % LANES // rank - (LANES // rank - 2))
    wide_lane = lanes_of(tails.shape) % LANES
    tails = jnp.where(wide_lane >= LANES - 2 * rank, tails, 0.0)
    coupled = couple(tails, weights_ref)
    images = [
        *lane_tiles(arrived_ref[low_place, :, :size]),
        *lane_tiles(image_ref[...]),
        *lane_tiles(arrived_ref[high_place, :, :size]),
        jnp.concatenate([coupled, jnp.zeros((VECS, LANES - rank), F32)], axis=1),
    ]
    windows = [
        *rows_from(low_tiles),
        *lane_tiles(window),
        *rows_from(high_tiles),
        window_coupled_ref[...],
    ]
    solved, record = orthogonalized(total, PIECE, windows, images)
    record_ref[...] = record
    per_row = size // LANES
    low_block, new_block, high_block = (
        jnp.concatenate(solved[at : at + per_row], axis=1)
        for at in range(0, 3 * per_row, per_row)
    )
    next_window = jnp.concatenate([window[VECS:], new_block], axis=0)
    next_window_ref[...] = next_window
    blocks = [block.astype(BF16) for block in (low_block, new_block, high_block)]
    near_part = near_field(blocks, choice_ref, near_ref)
    near_part_ref[...] = near_part
    far_part = jnp.dot(
        solved[-1][:, :rank].astype(BF16), u_ref[...], preferred_element_type=F32
    )
    skeleton, coarse = mapped(new_block.astype(BF16), maps_ref)
    width = LANES // VECS
    packed = one_row(product_lanes(next_window, near_part + far_part, 0, width))
    tree_rows = jnp.concatenate([one_row(skeleton), packed], axis=0)
    level_rows = jnp.concatenate([one_row(coarse), packed], axis=0)

    def store(slot, at):
        slots_ref[slot] = level_rows

    over_slots(slots, store)

    def store_tree(leaf, at):
        slots_ref[own_tree * leaves + leaf] = tree_rows

    over_slots(leaves, store_tree)


def end_kernel(
    trees,
    rows_all,
    arrived_ref,
    flat_ref,
    window_ref,
    near_part_ref,
    weights_ref,
    u_ref,
    first_ref,
    block_ref,
    records_ref,
):
    leaves = arrived_ref.shape[0] // trees
    width = LANES // VECS
    rows = jnp.concatenate(
        [arrived_ref[place, 0:1, :] for place in places_of(leaves, trees)], axis=0
    )
    shape = (VECS, LANES)
    row = lax.broadcasted_iota(jnp.int32, shape, 0)
    own = lanes_of(shape) // width == row
    parts = [
        jnp.concatenate(
            [jnp.where(own, part[at : at + 1], 0.0) for at in range(rows.shape[0])], axis=1
        )
        for part in (piece.astype(F32) for piece in three_parts(rows))
    ]
    coupled = sum(row_groups(couple(jnp.concatenate(parts, axis=0), weights_ref)))
    far_part = jnp.dot(coupled.astype(BF16), u_ref[...], preferred_element_type=F32)
    step = flat_ref.shape[0] // arrived_ref.shape[0] * VECS
    total = flat_ref[0:step]
    for at in range(step, flat_ref.shape[0], step):
        total = total + flat_ref[at : at + step]
    total = sum(total[at : at + 1] for at in range(1, step, step // VECS))
    turned = jnp.zeros(shape, F32)
    for v in range(VECS):
        moved = pltpu.roll(total, LANES - width * v, 1) if v else total
        turned = jnp.where(row == v, moved, turned)
    total = turned
    total = total * (1.0 / rows_all)
    image = near_part_ref[...] + far_part
    solved, record = orthogonalized(total, 0, lane_tiles(window_ref[...]), lane_tiles(image))
    store_rows(block_ref, jnp.concatenate(solved, axis=1))
    used = records_ref.shape[2]
    records_ref[0] = first_ref[:, :used]
    records_ref[1] = record[:, :used]


def call(kernel, name, outs, ins, places, scratch=(), vmem=16 << 20, bytes_accessed=1 << 20):
    spaces = {"s": pltpu.SMEM, "v": pltpu.VMEM, "h": pltpu.HBM}
    return pl.pallas_call(
        kernel,
        name=name,
        out_shape=[jax.ShapeDtypeStruct(shape, dtype) for shape, dtype in outs],
        in_specs=[pl.BlockSpec(memory_space=spaces[place]) for place in places],
        out_specs=[pl.BlockSpec(memory_space=pltpu.VMEM)] * len(outs),
        scratch_shapes=list(scratch),
        cost_estimate=pl.CostEstimate(flops=0, bytes_accessed=bytes_accessed, transcendentals=0),
        compiler_params=pltpu.CompilerParams(vmem_limit_bytes=vmem),
    )(*ins)


def exchange(slots):
    return lax.all_to_all(slots, AXES, 0, 0, tiled=True)


def local(
    krylov_basis,
    near_block,
    near_col,
    near_count,
    far_col,
    v_basis,
    u_basis,
    far_coupling,
    transfer,
    top_coupling,
):
    basis, _, size = krylov_basis.shape
    trees = lax.axis_size("lvl")
    leaves = lax.axis_size("clus")
    devices = leaves * trees
    rows_all = float(devices * size)
    flat_basis = krylov_basis.reshape(-1, LANES)
    v_own, u_own, transfer_own = v_basis[0, 0], u_basis[0, 0], transfer[0, 0]
    rank = v_own.shape[0]
    far_own, top_own, near_own = far_coupling[0, 0], top_coupling[0, 0], near_block[0, 0]
    image_like = ((VECS, size), F32)
    window_like = ((basis, size), F32)
    record_like = ((VECS, LANES), F32)
    maps_like = ((4 * LANES, size), BF16)
    choice_like = ((-(-3 * near_own.shape[0] // 8) * 8, LANES), F32)
    weights_like = ((3, rank, (leaves + trees) * LANES), BF16)
    slots, window = call(
        functools.partial(begin_kernel, leaves),
        "begin",
        [((devices, VECS, size + 2 * LANES), BF16), window_like],
        [flat_basis, v_own, transfer_own],
        "hhh",
        [
            pltpu.VMEM(flat_basis.shape, F32),
            pltpu.VMEM(v_own.shape, BF16),
            pltpu.VMEM(transfer_own.shape, F32),
            pltpu.SemaphoreType.DMA((3,)),
        ],
        vmem=None,
    )
    arrived = exchange(slots)
    weights, near_here, maps, choice = call(
        functools.partial(prepare_kernel, leaves),
        "prepare",
        [weights_like, (near_own.shape, BF16), maps_like, choice_like],
        [near_col, near_count, far_col, near_own, far_own, v_own, transfer_own, top_own],
        "ssshvvvv",
        [pltpu.SemaphoreType.DMA],
    )
    image, slots, window_coupled = call(
        functools.partial(first_kernel, trees),
        "first",
        [image_like, ((devices, VECS, size + LANES), F32), ((basis, LANES), F32)],
        [
            arrived,
            window,
            weights,
            near_here,
            choice,
            u_own,
            maps,
        ],
        "v" * 7,
    )
    arrived = exchange(slots)
    slots, window, near_part, record = call(
        functools.partial(middle_kernel, trees, rows_all),
        "middle",
        [((devices, 2, LANES), F32), window_like, image_like, record_like],
        [
            arrived,
            window,
            image,
            window_coupled,
            weights,
            near_here,
            choice,
            u_own,
            maps,
        ],
        "v" * 9,
    )
    arrived = exchange(slots)
    block, records = call(
        functools.partial(end_kernel, trees, rows_all),
        "end",
        [((VECS * size // LANES, LANES), F32), ((STEPS, VECS, basis + VECS), F32)],
        [arrived, arrived.reshape(-1, LANES), window, near_part, weights, u_own, record],
        "v" * 7,
    )
    return (block.reshape(VECS, 1, size), jnp.transpose(records, (0, 2, 1)))


def solution(mesh):
    return jax.shard_map(
        local,
        mesh=mesh,
        in_specs=(
            P(None, "lvl", "clus"),
            P("lvl", "clus", None, None, None),
            P("lvl", "clus", None),
            P("lvl", "clus"),
            P("lvl", "clus", None),
            P("lvl", "clus", None, None),
            P("lvl", "clus", None, None),
            P("lvl", "clus", None, None, None),
            P("lvl", "clus", None, None),
            P("lvl", "clus", None, None, None),
        ),
        out_specs=(P(None, "lvl", "clus"), P()),
        check_vma=False,
    )
```

```python
import functools

import jax
import jax.numpy as jnp
from jax import lax
from jax.experimental import pallas as pl
from jax.experimental.pallas import tpu as pltpu
from jax.sharding import PartitionSpec as P

VECS = 4
STEPS = 2
LANES = 128
PIECE = 16
UNROLL = 32
AXES = ("lvl", "clus")

PRECISE = lax.Precision.HIGHEST
ROWS_DIMS = (((1,), (1,)), ((), ()))
F32, BF16 = jnp.float32, jnp.bfloat16


def rows_dot(left, right, precision=None):
    return lax.dot_general(
        left, right, ROWS_DIMS, precision=precision, preferred_element_type=F32
    )


def precise_dot(left, right):
    return jnp.dot(left, right, precision=PRECISE, preferred_element_type=F32)


def three_parts(values):
    high = values.astype(BF16)
    rest = values - high.astype(F32)
    middle = rest.astype(BF16)
    low = (rest - middle.astype(F32)).astype(BF16)
    return high, middle, low


def lane_parts(values, part):
    high = values.astype(BF16).astype(F32)
    rest = values - high
    middle = rest.astype(BF16).astype(F32)
    low = rest - middle
    return jnp.where(part == 0, high, jnp.where(part == 1, middle, jnp.where(part == 2, low, 0.0)))


def lanes_of(shape):
    return lax.broadcasted_iota(jnp.int32, shape, len(shape) - 1)


def over_slots(count, store):
    step = min(count, UNROLL)
    if count == step:
        for slot in range(count):
            store(slot, slot)
        return

    def body(at, carry):
        for inner in range(step):
            store(at * step + inner, inner)
        return carry

    lax.fori_loop(0, count // step, body, 0)


def split_rows(flat, rows):
    halves = flat.shape[0] // rows
    return jnp.concatenate(
        [flat[pl.ds(half, rows, stride=halves), :] for half in range(halves)], axis=1
    )


def store_rows(flat_ref, values):
    rows = values.shape[0]
    halves = flat_ref.shape[0] // rows
    for half in range(halves):
        flat_ref[pl.ds(half, rows, stride=halves), :] = values[:, half * LANES : (half + 1) * LANES]


def row_groups(rows):
    return [rows[at : at + VECS] for at in range(0, rows.shape[0], VECS)]


def lane_tiles(values):
    return [values[:, at : at + LANES] for at in range(0, values.shape[1], LANES)]


def replicated(column):
    return jnp.broadcast_to(column, (column.shape[0], LANES))


def lane_sum(pairs):
    return replicated(jnp.sum(sum(left * right for left, right in pairs), axis=1, keepdims=True))


def begin_kernel(leaves, basis_hbm, v_hbm, transfer_hbm, slots_ref, window_ref, *scratch):
    basis_ref, v_ref, transfer_ref, sems = scratch
    copies = [
        pltpu.make_async_copy(source, target, sems.at[at])
        for at, (source, target) in enumerate(
            ((basis_hbm, basis_ref), (v_hbm, v_ref), (transfer_hbm, transfer_ref))
        )
    ]
    for copy in copies:
        copy.start()
    for copy in copies:
        copy.wait()
    basis, size = window_ref.shape
    rank = v_ref.shape[0]
    window = split_rows(basis_ref, basis)
    window_ref[...] = window
    current = window[basis - VECS :]
    lowered = current.astype(BF16)
    rest = current - lowered.astype(F32)
    parts = [lowered, *three_parts(window[: basis - VECS]), *three_parts(rest)[:2]]
    parts = jnp.concatenate([part.astype(F32) for part in parts], axis=0).astype(BF16)
    repeats = LANES // rank
    wide_basis = jnp.concatenate([v_ref[...]] * repeats, axis=0)
    rows = row_groups(rows_dot(parts, wide_basis))
    skeletons = jnp.concatenate([rows[0], rows[1] + rows[2] + rows[3], rows[4] + rows[5]], axis=0)
    wide_transfer = jnp.concatenate([transfer_ref[...]] * repeats, axis=1)
    coarse = precise_dot(skeletons[:, :rank], wide_transfer)
    own_tree = lax.axis_index("lvl")

    def tails(values):
        exact, old, extra = row_groups(values)
        group = lanes_of((VECS, LANES)) // rank
        first = jnp.where(group < 3, lane_parts(exact, group), extra)
        return first.astype(BF16), lane_parts(old, group - (repeats - 2))

    tree_first, tree_second = tails(skeletons)
    level_first, level_second = tails(coarse)
    kept = lanes_of((VECS, LANES)) >= LANES - 2 * rank
    flat = basis_ref[...]
    turns = LANES // PIECE
    turned = [pltpu.roll(flat, LANES - PIECE * c, 1) if c else flat for c in range(turns)]
    part = lanes_of(flat.shape) // PIECE
    pieces = [
        lane_parts(
            jnp.where(
                part == 0, turned[c], jnp.where(part == 1, turned[c - 1], turned[c - 2])
            ),
            part,
        )
        for c in range(turns)
    ]

    def store(slot, at):
        row, side = at * VECS // turns % flat.shape[0], at * VECS % turns
        piece = [pieces[side + v][row : row + 1] for v in range(VECS)]
        same = lax.div(jnp.int32(slot), jnp.int32(leaves)) == own_tree
        second = jnp.where(same, tree_second, level_second)
        piece = jnp.where(kept, second, jnp.concatenate(piece, axis=0))
        slots_ref[slot, :, :size] = lowered
        slots_ref[slot, :, size : size + LANES] = level_first
        slots_ref[slot, :, size + LANES :] = piece.astype(BF16)

    over_slots(slots_ref.shape[0], store)

    def store_tree(leaf, at):
        slots_ref[own_tree * leaves + leaf, :, size : size + LANES] = tree_first

    over_slots(leaves, store_tree)


def prepare_kernel(
    leaves,
    near_col_ref,
    near_count_ref,
    far_col_ref,
    near_hbm,
    far_coupling_ref,
    v_ref,
    transfer_ref,
    top_ref,
    weights_ref,
    near_ref,
    maps_ref,
    choice_ref,
    sem,
):
    copy = pltpu.make_async_copy(near_hbm, near_ref, sem)
    copy.start()
    own_tree = lax.axis_index("lvl")
    far_slots = far_coupling_ref.shape[0]
    trees, rank = top_ref.shape[0], top_ref.shape[1]
    transfer = transfer_ref[...]
    for slot in range(leaves + trees):
        if slot < leaves:
            block = jnp.zeros((rank, rank), F32)
            for at in range(far_slots):
                block = block + jnp.where(far_col_ref[0, 0, at] == slot, far_coupling_ref[at], 0.0)
        else:
            tree = slot - leaves
            block = precise_dot(transfer, jnp.where(tree != own_tree, top_ref[tree], 0.0))
        wide = jnp.concatenate([block] * (LANES // rank), axis=1)
        for part, piece in enumerate(three_parts(wide)):
            weights_ref[part, :, slot * LANES : (slot + 1) * LANES] = piece
    v_basis = v_ref[...]
    carried = precise_dot(transfer.T, v_basis.astype(F32))
    for part, piece in enumerate((v_basis, *three_parts(carried))):
        for at in range(part * LANES, (part + 1) * LANES, rank):
            maps_ref[at : at + rank] = piece
    own_leaf = lax.axis_index("clus")
    count = near_count_ref[0, 0]
    rows = lax.broadcasted_iota(jnp.int32, choice_ref.shape, 0)
    choice = jnp.zeros(choice_ref.shape, F32)
    for slot in range(near_ref.shape[0]):
        for side in range(3):
            wanted = (near_col_ref[0, 0, slot] == own_leaf + side - 1) & (slot < count)
            choice = jnp.where(rows == 3 * slot + side, jnp.where(wanted, 1.0, 0.0), choice)
    choice_ref[...] = choice
    copy.wait()


def places_of(leaves, trees):
    own_tree = lax.axis_index("lvl")
    own_leaf = lax.axis_index("clus")
    places = [own_tree * leaves + leaf for leaf in range(leaves)]
    return places + [tree * leaves + own_leaf for tree in range(trees)]


def near_places(leaves):
    start = lax.axis_index("lvl") * leaves
    own_leaf = lax.axis_index("clus")
    low = jnp.maximum(own_leaf - 1, 0)
    high = jnp.minimum(own_leaf + 1, leaves - 1)
    return [start + leaf for leaf in (low, own_leaf, high)]


def tree_sum(values):
    while len(values) > 1:
        values = [sum(values[at : at + 2]) for at in range(0, len(values), 2)]
    return values[0]


def near_field(blocks, choice_ref, near_ref):
    choice = choice_ref[...]
    blocks = [[tile.astype(F32) for tile in lane_tiles(block)] for block in blocks]
    parts = []
    for slot in range(near_ref.shape[0]):
        rows = [choice[3 * slot + side : 3 * slot + side + 1] for side in range(3)]
        tiles = [sum(tile * row for tile, row in zip(sides, rows)) for sides in zip(*blocks)]
        parts.append(rows_dot(jnp.concatenate(tiles, axis=1).astype(BF16), near_ref[slot]))
    return tree_sum(parts)


def couple(values, weights_ref):
    lowered = values.astype(BF16)
    return sum(rows_dot(lowered, weights_ref[part]) for part in range(3))


def product_lanes(window, image, period):
    basis = window.shape[0]
    window, image = lane_tiles(window), lane_tiles(image)
    lane = lanes_of((VECS, LANES)) % period
    packed = jnp.zeros((VECS, LANES), F32)
    for b in range(basis):
        product = lane_sum([(tile, other[b : b + 1]) for tile, other in zip(image, window)])
        packed = jnp.where(lane == b, product, packed)
    at = basis
    for u in range(VECS):
        product = lane_sum([(tile, tile[u : u + 1]) for tile in image])
        packed = jnp.where(lane == at + u, product, packed)
    at = at + VECS
    for b in range(basis):
        product = lane_sum([(tile, tile[b : b + 1]) for tile in window])
        for group in range(basis // VECS):
            rows = product[group * VECS : (group + 1) * VECS]
            packed = jnp.where(lane == at + group * basis + b, rows, packed)
    return packed


def couple_rows(rows, weights_ref):
    shape = (VECS, LANES)
    own = lanes_of(shape) // (LANES // VECS) == lax.broadcasted_iota(jnp.int32, shape, 0)
    parts = [
        jnp.concatenate(
            [jnp.where(own, part[at : at + 1], 0.0) for at in range(rows.shape[0])], axis=1
        )
        for part in (piece.astype(F32) for piece in three_parts(rows))
    ]
    return sum(row_groups(couple(jnp.concatenate(parts, axis=0), weights_ref)))


def one_row(values):
    width = LANES // VECS
    own = lanes_of(values.shape) // width == lax.broadcasted_iota(jnp.int32, values.shape, 0)
    return jnp.sum(jnp.where(own, values, 0.0), axis=0, keepdims=True)


def mapped(rows, maps_ref):
    products = lane_tiles(rows_dot(rows, maps_ref[...]))
    skeleton, coarse = products[0], products[1] + products[2] + products[3]
    return sum(row_groups(skeleton)), sum(row_groups(coarse))


def first_kernel(
    trees,
    arrived_ref,
    window_ref,
    weights_ref,
    near_ref,
    choice_ref,
    u_ref,
    maps_ref,
    image_ref,
    slots_ref,
    window_coupled_ref,
):
    own_tree = lax.axis_index("lvl")
    size = near_ref.shape[1]
    rank = u_ref.shape[0]
    leaves = arrived_ref.shape[0] // trees
    places = places_of(leaves, trees)
    first = [arrived_ref[place, :, size : size + LANES] for place in places]
    second = [arrived_ref[place, :, size + LANES :] for place in places]
    first = jnp.concatenate(first, axis=1).astype(F32)
    second = jnp.concatenate(second, axis=1).astype(F32)
    lane = lanes_of(first.shape) % LANES
    exact = jnp.where(lane < 3 * rank, first, 0.0)
    old = jnp.where(lane >= LANES - 2 * rank, second, 0.0)
    rows = couple(jnp.concatenate([exact, first, old], axis=0), weights_ref)
    linear = jnp.concatenate([rows[2 * VECS :], rows[VECS : 2 * VECS]], axis=0)
    blank = jnp.zeros((2 * VECS, LANES - rank), F32)
    window_coupled_ref[...] = jnp.concatenate([linear, blank], axis=1)
    image = jnp.dot(rows[:VECS].astype(BF16), u_ref[...], preferred_element_type=F32)
    blocks = [arrived_ref[place, :, :size] for place in near_places(leaves)]
    image = image + near_field(blocks, choice_ref, near_ref)
    image_ref[...] = image
    width = LANES // VECS
    packed = one_row(product_lanes(window_ref[...], image, width))
    parts = [part.astype(F32) for part in three_parts(image)]
    skeleton, coarse = mapped(jnp.concatenate(parts, axis=0).astype(BF16), maps_ref)
    tree_row, level_row = one_row(skeleton), one_row(coarse)
    image_rows = jnp.concatenate(lane_tiles(image), axis=0)
    per_slot = image_rows.shape[0] + 3
    total = slots_ref.shape[0] // per_slot
    step = min(total, UNROLL)
    shape = (2 * VECS, LANES)
    lane = lanes_of(shape)
    row = lax.broadcasted_iota(jnp.int32, shape, 0)
    own = lane // PIECE % VECS == row % VECS

    def fill(part_ref, start):
        for inner in range(0, step, 2):
            sides = []
            for shift in (-1, 1):
                near = [start + inner + at + shift for at in range(2)]
                if isinstance(start, int):
                    near = [min(max(slot, 0), total - 1) for slot in near]
                else:
                    near = [jnp.clip(slot, 0, total - 1) for slot in near]
                near = [arrived_ref[slot, :, size + LANES :].astype(F32) for slot in near]
                sides.append(jnp.concatenate(near, axis=0))
            both = jnp.where(lane < LANES // 2, sides[0], pltpu.roll(sides[1], LANES // 2, 1))
            both = (
                both
                + pltpu.roll(both, LANES - PIECE, 1)
                + pltpu.roll(both, LANES - 2 * PIECE, 1)
            )
            both = jnp.where(own, pltpu.roll(both, 0, 1, stride=PIECE, stride_axis=0), 0.0)
            for at in range(2):
                relay = jnp.sum(both[at * VECS : (at + 1) * VECS], axis=0, keepdims=True)
                slot = jnp.int32(start + inner + at)
                same = lax.div(slot, jnp.int32(leaves)) == own_tree
                far = jnp.where(same, tree_row, level_row)
                first_row = (inner + at) * per_slot
                part_ref[first_row : first_row + per_slot] = jnp.concatenate(
                    [image_rows, far, relay, packed], axis=0
                )

    if total == step:
        fill(slots_ref, 0)
    else:

        def body(at, carry):
            start = pl.multiple_of(at * (step * per_slot), 8)
            fill(slots_ref.at[pl.ds(start, step * per_slot)], at * step)
            return carry

        lax.fori_loop(0, total // step, body, 0)


def orthogonalized(total, windows, images):
    basis = windows[0].shape[0]
    shape = (VECS, LANES)
    row, lane = lax.broadcasted_iota(jnp.int32, shape, 0), lanes_of(shape)
    total = jnp.broadcast_to(total, shape)

    def column_of(at):
        places = row * (LANES // VECS) + at
        return jnp.take_along_axis(total, places, axis=1, mode="promise_in_bounds")

    projection = [column_of(b) for b in range(basis)]
    square = [column_of(basis + u) for u in range(VECS)]
    start = basis + VECS
    inner = []
    for other in range(basis):
        value = -2.0 * projection[other]
        for group in range(basis // VECS):
            metric = column_of(start + group * basis + other)
            for v in range(VECS):
                value = value + projection[group * VECS + v] * metric[v : v + 1]
        inner.append(value)
    columns = []
    for u in range(VECS):
        value = square[u]
        for b in range(basis):
            value = value + inner[b] * projection[b][u : u + 1]
        columns.append(value)
    remainders = []
    for window, image in zip(windows, images):
        for b in range(basis):
            image = image - projection[b] * window[b : b + 1]
        remainders.append(image)
    record = jnp.zeros(shape, F32)
    for b in range(basis):
        record = jnp.where(lane == b, projection[b], record)
    for j in range(VECS):
        pivot = columns[j][j : j + 1]
        scale = lax.rsqrt(pivot)
        lower = jnp.where(row > j, columns[j] * scale, 0.0)
        record = jnp.where(lane == basis + j, jnp.where(row == j, pivot * scale, lower), record)
        for u in range(j + 1, VECS):
            columns[u] = columns[u] - lower * lower[u : u + 1]
        for t, remainder in enumerate(remainders):
            solved = remainder[j : j + 1] * scale
            remainders[t] = jnp.where(row == j, solved, remainder - lower * solved)
    return remainders, record


def middle_kernel(
    trees,
    rows_all,
    arrived_ref,
    flat_ref,
    window_ref,
    image_ref,
    window_coupled_ref,
    weights_ref,
    near_ref,
    choice_ref,
    u_ref,
    maps_ref,
    slots_ref,
    next_window_ref,
    near_part_ref,
    record_ref,
):
    own_tree = lax.axis_index("lvl")
    window = window_ref[...]
    basis, size = window.shape
    rank = u_ref.shape[0]
    lane = lanes_of((VECS, LANES))
    slots = arrived_ref.shape[0]
    leaves = slots // trees
    per_slot = flat_ref.shape[0] // slots
    per_row = size // LANES
    image_count = VECS * per_row
    rows = [
        flat_ref[pl.ds(per_slot * at + image_count + 2, 8, stride=per_slot), :]
        for at in range(0, slots, 8)
    ]
    total = jnp.sum(tree_sum(rows), axis=0, keepdims=True) * (1.0 / rows_all)
    first_tiles, other_tiles = [], []
    left = lanes_of((basis, LANES)) < LANES // 2
    for half in range(per_row):
        even, odd = (
            flat_ref[
                pl.ds(
                    per_slot * (2 * half + side) + image_count + 1,
                    basis,
                    stride=2 * per_row * per_slot,
                ),
                :,
            ]
            for side in range(2)
        )
        first_tiles.append(jnp.where(left, even, pltpu.roll(odd, LANES // 2, 1)))
        other_tiles.append(jnp.where(left, pltpu.roll(even, LANES // 2, 1), odd))
    own_slot = own_tree * leaves + lax.axis_index("clus")
    even_slot = lax.rem(own_slot, jnp.int32(2)) == 0
    low_tiles = [jnp.where(even_slot, a, b) for a, b in zip(first_tiles, other_tiles)]
    high_tiles = [jnp.where(even_slot, b, a) for a, b in zip(first_tiles, other_tiles)]

    def rows_of(place, start, count):
        at = [(start + row) * LANES for row in range(count)]
        return jnp.concatenate(
            [arrived_ref[place, 0:1, lane : lane + LANES] for lane in at], axis=0
        )

    low_place, _, high_place = near_places(leaves)
    coupled = couple_rows(
        jnp.concatenate(
            [rows_of(place, image_count, 1) for place in places_of(leaves, trees)], axis=0
        ),
        weights_ref,
    )
    images = [
        *row_groups(rows_of(low_place, 0, image_count)),
        *lane_tiles(image_ref[...]),
        *row_groups(rows_of(high_place, 0, image_count)),
        jnp.concatenate([coupled, jnp.zeros((VECS, LANES - rank), F32)], axis=1),
    ]
    windows = [
        *low_tiles,
        *lane_tiles(window),
        *high_tiles,
        window_coupled_ref[...],
    ]
    solved, record = orthogonalized(total, windows, images)
    record_ref[...] = record
    low_block, new_block, high_block = (
        jnp.concatenate(solved[at : at + per_row], axis=1)
        for at in range(0, 3 * per_row, per_row)
    )
    next_window = jnp.concatenate([window[VECS:], new_block], axis=0)
    next_window_ref[...] = next_window
    blocks = [block.astype(BF16) for block in (low_block, new_block, high_block)]
    near_part = near_field(blocks, choice_ref, near_ref)
    near_part_ref[...] = near_part
    far_part = jnp.dot(
        solved[-1][:, :rank].astype(BF16), u_ref[...], preferred_element_type=F32
    )
    skeleton, coarse = mapped(new_block.astype(BF16), maps_ref)
    width = LANES // VECS
    packed = one_row(product_lanes(next_window, near_part + far_part, width))
    tree_rows = jnp.concatenate([one_row(skeleton), packed], axis=0)
    level_rows = jnp.concatenate([one_row(coarse), packed], axis=0)

    def store(slot, at):
        slots_ref[slot] = level_rows

    over_slots(slots, store)

    def store_tree(leaf, at):
        slots_ref[own_tree * leaves + leaf] = tree_rows

    over_slots(leaves, store_tree)


def end_kernel(
    trees,
    rows_all,
    arrived_ref,
    flat_ref,
    window_ref,
    near_part_ref,
    weights_ref,
    u_ref,
    first_ref,
    block_ref,
    records_ref,
):
    leaves = arrived_ref.shape[0] // trees
    rows = jnp.concatenate(
        [arrived_ref[place, 0:1, :] for place in places_of(leaves, trees)], axis=0
    )
    coupled = couple_rows(rows, weights_ref)
    far_part = jnp.dot(coupled.astype(BF16), u_ref[...], preferred_element_type=F32)
    step = flat_ref.shape[0] // arrived_ref.shape[0] * VECS
    total = flat_ref[0:step]
    for at in range(step, flat_ref.shape[0], step):
        total = total + flat_ref[at : at + step]
    total = sum(total[at : at + 1] for at in range(1, step, step // VECS))
    total = total * (1.0 / rows_all)
    image = near_part_ref[...] + far_part
    solved, record = orthogonalized(total, lane_tiles(window_ref[...]), lane_tiles(image))
    store_rows(block_ref, jnp.concatenate(solved, axis=1))
    used = records_ref.shape[2]
    records_ref[0] = first_ref[:, :used]
    records_ref[1] = record[:, :used]


def call(kernel, name, outs, ins, places, scratch=(), vmem=16 << 20, bytes_accessed=1 << 20):
    spaces = {"s": pltpu.SMEM, "v": pltpu.VMEM, "h": pltpu.HBM}
    return pl.pallas_call(
        kernel,
        name=name,
        out_shape=[jax.ShapeDtypeStruct(shape, dtype) for shape, dtype in outs],
        in_specs=[pl.BlockSpec(memory_space=spaces[place]) for place in places],
        out_specs=[pl.BlockSpec(memory_space=pltpu.VMEM)] * len(outs),
        scratch_shapes=list(scratch),
        cost_estimate=pl.CostEstimate(flops=0, bytes_accessed=bytes_accessed, transcendentals=0),
        compiler_params=pltpu.CompilerParams(vmem_limit_bytes=vmem),
    )(*ins)


def exchange(slots):
    return lax.all_to_all(slots, AXES, 0, 0, tiled=True)


def local(
    krylov_basis,
    near_block,
    near_col,
    near_count,
    far_col,
    v_basis,
    u_basis,
    far_coupling,
    transfer,
    top_coupling,
):
    basis, _, size = krylov_basis.shape
    trees = lax.axis_size("lvl")
    leaves = lax.axis_size("clus")
    devices = leaves * trees
    rows_all = float(devices * size)
    flat_basis = krylov_basis.reshape(-1, LANES)
    v_own, u_own, transfer_own = v_basis[0, 0], u_basis[0, 0], transfer[0, 0]
    rank = v_own.shape[0]
    far_own, top_own, near_own = far_coupling[0, 0], top_coupling[0, 0], near_block[0, 0]
    image_like = ((VECS, size), F32)
    window_like = ((basis, size), F32)
    per_slot = VECS * size // LANES + 3
    record_like = ((VECS, LANES), F32)
    maps_like = ((4 * LANES, size), BF16)
    choice_like = ((-(-3 * near_own.shape[0] // 8) * 8, LANES), F32)
    weights_like = ((3, rank, (leaves + trees) * LANES), BF16)
    slots, window = call(
        functools.partial(begin_kernel, leaves),
        "begin",
        [((devices, VECS, size + 2 * LANES), BF16), window_like],
        [flat_basis, v_own, transfer_own],
        "hhh",
        [
            pltpu.VMEM(flat_basis.shape, F32),
            pltpu.VMEM(v_own.shape, BF16),
            pltpu.VMEM(transfer_own.shape, F32),
            pltpu.SemaphoreType.DMA((3,)),
        ],
        vmem=None,
    )
    arrived = exchange(slots)
    weights, near_here, maps, choice = call(
        functools.partial(prepare_kernel, leaves),
        "prepare",
        [weights_like, (near_own.shape, BF16), maps_like, choice_like],
        [near_col, near_count, far_col, near_own, far_own, v_own, transfer_own, top_own],
        "ssshvvvv",
        [pltpu.SemaphoreType.DMA],
    )
    image, slots, window_coupled = call(
        functools.partial(first_kernel, trees),
        "first",
        [image_like, ((devices * per_slot, LANES), F32), ((basis, LANES), F32)],
        [
            arrived,
            window,
            weights,
            near_here,
            choice,
            u_own,
            maps,
        ],
        "v" * 7,
    )
    arrived = exchange(slots.reshape(devices, 1, per_slot * LANES))
    slots, window, near_part, record = call(
        functools.partial(middle_kernel, trees, rows_all),
        "middle",
        [((devices, 2, LANES), F32), window_like, image_like, record_like],
        [
            arrived,
            arrived.reshape(-1, LANES),
            window,
            image,
            window_coupled,
            weights,
            near_here,
            choice,
            u_own,
            maps,
        ],
        "v" * 10,
    )
    arrived = exchange(slots)
    block, records = call(
        functools.partial(end_kernel, trees, rows_all),
        "end",
        [((VECS * size // LANES, LANES), F32), ((STEPS, VECS, basis + VECS), F32)],
        [arrived, arrived.reshape(-1, LANES), window, near_part, weights, u_own, record],
        "v" * 7,
    )
    return (block.reshape(VECS, 1, size), jnp.transpose(records, (0, 2, 1)))


def solution(mesh):
    return jax.shard_map(
        local,
        mesh=mesh,
        in_specs=(
            P(None, "lvl", "clus"),
            P("lvl", "clus", None, None, None),
            P("lvl", "clus", None),
            P("lvl", "clus"),
            P("lvl", "clus", None),
            P("lvl", "clus", None, None),
            P("lvl", "clus", None, None),
            P("lvl", "clus", None, None, None),
            P("lvl", "clus", None, None),
            P("lvl", "clus", None, None, None),
        ),
        out_specs=(P(None, "lvl", "clus"), P()),
        check_vma=False,
    )
```

```python
import functools

import jax
import jax.numpy as jnp
from jax import lax
from jax.experimental import pallas as pl
from jax.experimental.pallas import tpu as pltpu
from jax.sharding import PartitionSpec as P

VECS = 4
STEPS = 2
LANES = 128
PIECE = 16
UNROLL = 32
AXES = ("lvl", "clus")

PRECISE = lax.Precision.HIGHEST
ROWS_DIMS = (((1,), (1,)), ((), ()))
F32, BF16 = jnp.float32, jnp.bfloat16


def rows_dot(left, right, precision=None):
    return lax.dot_general(
        left, right, ROWS_DIMS, precision=precision, preferred_element_type=F32
    )


def precise_dot(left, right):
    return jnp.dot(left, right, precision=PRECISE, preferred_element_type=F32)


def three_parts(values):
    high = values.astype(BF16)
    rest = values - high.astype(F32)
    middle = rest.astype(BF16)
    low = (rest - middle.astype(F32)).astype(BF16)
    return high, middle, low


def lane_parts(values, part):
    high = values.astype(BF16).astype(F32)
    rest = values - high
    middle = rest.astype(BF16).astype(F32)
    low = rest - middle
    return jnp.where(part == 0, high, jnp.where(part == 1, middle, jnp.where(part == 2, low, 0.0)))


def lanes_of(shape):
    return lax.broadcasted_iota(jnp.int32, shape, len(shape) - 1)


def over_slots(count, store):
    step = min(count, UNROLL)
    if count == step:
        for slot in range(count):
            store(slot, slot)
        return

    def body(at, carry):
        for inner in range(step):
            store(at * step + inner, inner)
        return carry

    lax.fori_loop(0, count // step, body, 0)


def split_rows(flat, rows):
    halves = flat.shape[0] // rows
    return jnp.concatenate(
        [flat[pl.ds(half, rows, stride=halves), :] for half in range(halves)], axis=1
    )


def store_rows(flat_ref, values):
    rows = values.shape[0]
    halves = flat_ref.shape[0] // rows
    for half in range(halves):
        flat_ref[pl.ds(half, rows, stride=halves), :] = values[:, half * LANES : (half + 1) * LANES]


def row_groups(rows):
    return [rows[at : at + VECS] for at in range(0, rows.shape[0], VECS)]


def lane_tiles(values):
    return [values[:, at : at + LANES] for at in range(0, values.shape[1], LANES)]


def replicated(column):
    return jnp.broadcast_to(column, (column.shape[0], LANES))


def lane_sum(pairs):
    return replicated(jnp.sum(sum(left * right for left, right in pairs), axis=1, keepdims=True))


def begin_kernel(leaves, basis_hbm, v_hbm, transfer_hbm, slots_ref, window_ref, *scratch):
    basis_ref, v_ref, transfer_ref, sems = scratch
    copies = [
        pltpu.make_async_copy(source, target, sems.at[at])
        for at, (source, target) in enumerate(
            ((basis_hbm, basis_ref), (v_hbm, v_ref), (transfer_hbm, transfer_ref))
        )
    ]
    for copy in copies:
        copy.start()
    for copy in copies:
        copy.wait()
    basis, size = window_ref.shape
    rank = v_ref.shape[0]
    window = split_rows(basis_ref, basis)
    window_ref[...] = window
    current = window[basis - VECS :]
    lowered = current.astype(BF16)
    rest = current - lowered.astype(F32)
    parts = [lowered, *three_parts(window[: basis - VECS]), *three_parts(rest)[:2]]
    parts = jnp.concatenate([part.astype(F32) for part in parts], axis=0).astype(BF16)
    repeats = LANES // rank
    wide_basis = jnp.concatenate([v_ref[...]] * repeats, axis=0)
    rows = row_groups(rows_dot(parts, wide_basis))
    skeletons = jnp.concatenate([rows[0], rows[1] + rows[2] + rows[3], rows[4] + rows[5]], axis=0)
    wide_transfer = jnp.concatenate([transfer_ref[...]] * repeats, axis=1)
    wide_transfer = jnp.concatenate(three_parts(wide_transfer), axis=1)
    wide_transfer = jnp.concatenate([wide_transfer] * repeats, axis=0)
    split = lane_parts(skeletons, lanes_of(skeletons.shape) // rank).astype(BF16)
    coarse = sum(lane_tiles(jnp.dot(split, wide_transfer, preferred_element_type=F32)))
    own_tree = lax.axis_index("lvl")

    def tails(values):
        exact, old, extra = row_groups(values)
        group = lanes_of((VECS, LANES)) // rank
        first = jnp.where(group < 3, lane_parts(exact, group), extra)
        return first.astype(BF16), lane_parts(old, group - (repeats - 2))

    tree_first, tree_second = tails(skeletons)
    level_first, level_second = tails(coarse)
    kept = lanes_of((VECS, LANES)) >= LANES - 2 * rank
    flat = basis_ref[...]
    turns = LANES // PIECE
    turned = [pltpu.roll(flat, LANES - PIECE * c, 1) if c else flat for c in range(turns)]
    part = lanes_of(flat.shape) // PIECE
    pieces = [
        lane_parts(
            jnp.where(
                part == 0, turned[c], jnp.where(part == 1, turned[c - 1], turned[c - 2])
            ),
            part,
        )
        for c in range(turns)
    ]

    def store(slot, at):
        row, side = at * VECS // turns % flat.shape[0], at * VECS % turns
        piece = [pieces[side + v][row : row + 1] for v in range(VECS)]
        same = lax.div(jnp.int32(slot), jnp.int32(leaves)) == own_tree
        second = jnp.where(same, tree_second, level_second)
        piece = jnp.where(kept, second, jnp.concatenate(piece, axis=0))
        slots_ref[slot, :, :size] = lowered
        slots_ref[slot, :, size : size + LANES] = level_first
        slots_ref[slot, :, size + LANES :] = piece.astype(BF16)

    over_slots(slots_ref.shape[0], store)

    def store_tree(leaf, at):
        slots_ref[own_tree * leaves + leaf, :, size : size + LANES] = tree_first

    over_slots(leaves, store_tree)


def prepare_kernel(
    leaves,
    near_col_ref,
    near_count_ref,
    far_col_ref,
    near_hbm,
    far_coupling_ref,
    v_ref,
    transfer_ref,
    top_ref,
    weights_ref,
    near_ref,
    maps_ref,
    choice_ref,
    sem,
):
    copy = pltpu.make_async_copy(near_hbm, near_ref, sem)
    copy.start()
    own_tree = lax.axis_index("lvl")
    far_slots = far_coupling_ref.shape[0]
    trees, rank = top_ref.shape[0], top_ref.shape[1]
    transfer = transfer_ref[...]
    own_leaf = lax.axis_index("clus")
    for slot in range(leaves + trees - 2):
        if slot < leaves - 1:
            leaf = lax.rem(own_leaf + 1 + slot, jnp.int32(leaves))
            block = jnp.zeros((rank, rank), F32)
            for at in range(far_slots):
                block = block + jnp.where(far_col_ref[0, 0, at] == leaf, far_coupling_ref[at], 0.0)
        else:
            tree = lax.rem(own_tree + 2 + slot - leaves, jnp.int32(trees))
            block = precise_dot(transfer, top_ref[tree])
        wide = jnp.concatenate([block] * (LANES // rank), axis=1)
        for part, piece in enumerate(three_parts(wide)):
            weights_ref[part, :, slot * LANES : (slot + 1) * LANES] = piece
    v_basis = v_ref[...]
    carried = precise_dot(transfer.T, v_basis.astype(F32))
    for part, piece in enumerate((v_basis, *three_parts(carried))):
        for at in range(part * LANES, (part + 1) * LANES, rank):
            maps_ref[at : at + rank] = piece
    count = near_count_ref[0, 0]
    rows = lax.broadcasted_iota(jnp.int32, choice_ref.shape, 0)
    choice = jnp.zeros(choice_ref.shape, F32)
    for slot in range(near_ref.shape[0]):
        for side in range(3):
            wanted = (near_col_ref[0, 0, slot] == own_leaf + side - 1) & (slot < count)
            choice = jnp.where(rows == 3 * slot + side, jnp.where(wanted, 1.0, 0.0), choice)
    choice_ref[...] = choice
    copy.wait()


def places_of(leaves, trees):
    own_tree = lax.axis_index("lvl")
    own_leaf = lax.axis_index("clus")
    others = [lax.rem(own_leaf + 1 + at, jnp.int32(leaves)) for at in range(leaves - 1)]
    places = [own_tree * leaves + leaf for leaf in others]
    others = [lax.rem(own_tree + 1 + at, jnp.int32(trees)) for at in range(trees - 1)]
    return places + [tree * leaves + own_leaf for tree in others]


def near_places(leaves):
    start = lax.axis_index("lvl") * leaves
    own_leaf = lax.axis_index("clus")
    low = jnp.maximum(own_leaf - 1, 0)
    high = jnp.minimum(own_leaf + 1, leaves - 1)
    return [start + leaf for leaf in (low, own_leaf, high)]


def tree_sum(values):
    while len(values) > 1:
        values = [sum(values[at : at + 2]) for at in range(0, len(values), 2)]
    return values[0]


def near_field(blocks, choice_ref, near_ref):
    choice = choice_ref[...]
    blocks = [[tile.astype(F32) for tile in lane_tiles(block)] for block in blocks]
    parts = []
    for slot in range(near_ref.shape[0]):
        rows = [choice[3 * slot + side : 3 * slot + side + 1] for side in range(3)]
        tiles = [sum(tile * row for tile, row in zip(sides, rows)) for sides in zip(*blocks)]
        parts.append(rows_dot(jnp.concatenate(tiles, axis=1).astype(BF16), near_ref[slot]))
    return tree_sum(parts)


def couple(values, weights_ref):
    lowered = values.astype(BF16)
    return sum(rows_dot(lowered, weights_ref[part]) for part in range(3))


def product_lanes(window, image, period):
    basis = window.shape[0]
    window, image = lane_tiles(window), lane_tiles(image)
    lane = lanes_of((VECS, LANES)) % period
    packed = jnp.zeros((VECS, LANES), F32)
    for b in range(basis):
        product = lane_sum([(tile, other[b : b + 1]) for tile, other in zip(image, window)])
        packed = jnp.where(lane == b, product, packed)
    at = basis
    for u in range(VECS):
        product = lane_sum([(tile, tile[u : u + 1]) for tile in image])
        packed = jnp.where(lane == at + u, product, packed)
    at = at + VECS
    for b in range(basis):
        product = lane_sum([(tile, tile[b : b + 1]) for tile in window])
        for group in range(basis // VECS):
            rows = product[group * VECS : (group + 1) * VECS]
            packed = jnp.where(lane == at + group * basis + b, rows, packed)
    return packed


def couple_rows(rows, weights_ref):
    shape = (VECS, LANES)
    own = lanes_of(shape) // (LANES // VECS) == lax.broadcasted_iota(jnp.int32, shape, 0)
    parts = [
        jnp.concatenate(
            [jnp.where(own, part[at : at + 1], 0.0) for at in range(rows.shape[0])], axis=1
        )
        for part in (piece.astype(F32) for piece in three_parts(rows))
    ]
    return sum(row_groups(couple(jnp.concatenate(parts, axis=0), weights_ref)))


def one_row(values):
    width = LANES // VECS
    own = lanes_of(values.shape) // width == lax.broadcasted_iota(jnp.int32, values.shape, 0)
    return jnp.sum(jnp.where(own, values, 0.0), axis=0, keepdims=True)


def mapped(rows, maps_ref):
    products = lane_tiles(rows_dot(rows, maps_ref[...]))
    skeleton, coarse = products[0], products[1] + products[2] + products[3]
    return sum(row_groups(skeleton)), sum(row_groups(coarse))


def first_kernel(
    trees,
    arrived_ref,
    window_ref,
    weights_ref,
    near_ref,
    choice_ref,
    u_ref,
    maps_ref,
    image_ref,
    slots_ref,
    window_coupled_ref,
):
    own_tree = lax.axis_index("lvl")
    size = near_ref.shape[1]
    rank = u_ref.shape[0]
    leaves = arrived_ref.shape[0] // trees
    places = places_of(leaves, trees)
    first = [arrived_ref[place, :, size : size + LANES] for place in places]
    second = [arrived_ref[place, :, size + LANES :] for place in places]
    first = jnp.concatenate(first, axis=1).astype(F32)
    second = jnp.concatenate(second, axis=1).astype(F32)
    lane = lanes_of(first.shape) % LANES
    exact = jnp.where(lane < 3 * rank, first, 0.0)
    old = jnp.where(lane >= LANES - 2 * rank, second, 0.0)
    rows = couple(jnp.concatenate([exact, first, old], axis=0), weights_ref)
    linear = jnp.concatenate([rows[2 * VECS :], rows[VECS : 2 * VECS]], axis=0)
    blank = jnp.zeros((2 * VECS, LANES - rank), F32)
    window_coupled_ref[...] = jnp.concatenate([linear, blank], axis=1)
    image = jnp.dot(rows[:VECS].astype(BF16), u_ref[...], preferred_element_type=F32)
    blocks = [arrived_ref[place, :, :size] for place in near_places(leaves)]
    image = image + near_field(blocks, choice_ref, near_ref)
    image_ref[...] = image
    width = LANES // VECS
    packed = one_row(product_lanes(window_ref[...], image, width))
    parts = [part.astype(F32) for part in three_parts(image)]
    skeleton, coarse = mapped(jnp.concatenate(parts, axis=0).astype(BF16), maps_ref)
    tree_row, level_row = one_row(skeleton), one_row(coarse)
    image_rows = jnp.concatenate(lane_tiles(image), axis=0)
    per_slot = image_rows.shape[0] + 3
    total = slots_ref.shape[0] // per_slot
    step = min(total, UNROLL)
    shape = (2 * VECS, LANES)
    lane = lanes_of(shape)
    row = lax.broadcasted_iota(jnp.int32, shape, 0)
    own = lane // PIECE % VECS == row % VECS

    def fill(part_ref, start):
        for inner in range(0, step, 2):
            sides = []
            for shift in (-1, 1):
                near = [start + inner + at + shift for at in range(2)]
                if isinstance(start, int):
                    near = [min(max(slot, 0), total - 1) for slot in near]
                else:
                    near = [jnp.clip(slot, 0, total - 1) for slot in near]
                near = [arrived_ref[slot, :, size + LANES :].astype(F32) for slot in near]
                sides.append(jnp.concatenate(near, axis=0))
            both = jnp.where(lane < LANES // 2, sides[0], pltpu.roll(sides[1], LANES // 2, 1))
            both = (
                both
                + pltpu.roll(both, LANES - PIECE, 1)
                + pltpu.roll(both, LANES - 2 * PIECE, 1)
            )
            both = jnp.where(own, pltpu.roll(both, 0, 1, stride=PIECE, stride_axis=0), 0.0)
            for at in range(2):
                relay = jnp.sum(both[at * VECS : (at + 1) * VECS], axis=0, keepdims=True)
                slot = jnp.int32(start + inner + at)
                same = lax.div(slot, jnp.int32(leaves)) == own_tree
                far = jnp.where(same, tree_row, level_row)
                first_row = (inner + at) * per_slot
                part_ref[first_row : first_row + per_slot] = jnp.concatenate(
                    [image_rows, far, relay, packed], axis=0
                )

    if total == step:
        fill(slots_ref, 0)
    else:

        def body(at, carry):
            start = pl.multiple_of(at * (step * per_slot), 8)
            fill(slots_ref.at[pl.ds(start, step * per_slot)], at * step)
            return carry

        lax.fori_loop(0, total // step, body, 0)


def orthogonalized(total, windows, images):
    basis = windows[0].shape[0]
    shape = (VECS, LANES)
    row, lane = lax.broadcasted_iota(jnp.int32, shape, 0), lanes_of(shape)
    total = jnp.broadcast_to(total, shape)

    def column_of(at):
        places = row * (LANES // VECS) + at
        return jnp.take_along_axis(total, places, axis=1, mode="promise_in_bounds")

    projection = [column_of(b) for b in range(basis)]
    square = [column_of(basis + u) for u in range(VECS)]
    start = basis + VECS
    inner = []
    for other in range(basis):
        value = -2.0 * projection[other]
        for group in range(basis // VECS):
            metric = column_of(start + group * basis + other)
            for v in range(VECS):
                value = value + projection[group * VECS + v] * metric[v : v + 1]
        inner.append(value)
    columns = []
    for u in range(VECS):
        value = square[u]
        for b in range(basis):
            value = value + inner[b] * projection[b][u : u + 1]
        columns.append(value)
    remainders = []
    for window, image in zip(windows, images):
        for b in range(basis):
            image = image - projection[b] * window[b : b + 1]
        remainders.append(image)
    record = jnp.zeros(shape, F32)
    for b in range(basis):
        record = jnp.where(lane == b, projection[b], record)
    for j in range(VECS):
        pivot = columns[j][j : j + 1]
        scale = lax.rsqrt(pivot)
        lower = jnp.where(row > j, columns[j] * scale, 0.0)
        record = jnp.where(lane == basis + j, jnp.where(row == j, pivot * scale, lower), record)
        for u in range(j + 1, VECS):
            columns[u] = columns[u] - lower * lower[u : u + 1]
        for t, remainder in enumerate(remainders):
            solved = remainder[j : j + 1] * scale
            remainders[t] = jnp.where(row == j, solved, remainder - lower * solved)
    return remainders, record


def middle_kernel(
    trees,
    rows_all,
    arrived_ref,
    flat_ref,
    window_ref,
    image_ref,
    window_coupled_ref,
    weights_ref,
    near_ref,
    choice_ref,
    u_ref,
    maps_ref,
    slots_ref,
    next_window_ref,
    near_part_ref,
    record_ref,
):
    own_tree = lax.axis_index("lvl")
    window = window_ref[...]
    basis, size = window.shape
    rank = u_ref.shape[0]
    lane = lanes_of((VECS, LANES))
    slots = arrived_ref.shape[0]
    leaves = slots // trees
    per_slot = flat_ref.shape[0] // slots
    per_row = size // LANES
    image_count = VECS * per_row
    rows = [
        flat_ref[pl.ds(per_slot * at + image_count + 2, 8, stride=per_slot), :]
        for at in range(0, slots, 8)
    ]
    total = jnp.sum(tree_sum(rows), axis=0, keepdims=True) * (1.0 / rows_all)
    first_tiles, other_tiles = [], []
    left = lanes_of((basis, LANES)) < LANES // 2
    for half in range(per_row):
        even, odd = (
            flat_ref[
                pl.ds(
                    per_slot * (2 * half + side) + image_count + 1,
                    basis,
                    stride=2 * per_row * per_slot,
                ),
                :,
            ]
            for side in range(2)
        )
        first_tiles.append(jnp.where(left, even, pltpu.roll(odd, LANES // 2, 1)))
        other_tiles.append(jnp.where(left, pltpu.roll(even, LANES // 2, 1), odd))
    own_slot = own_tree * leaves + lax.axis_index("clus")
    even_slot = lax.rem(own_slot, jnp.int32(2)) == 0
    low_tiles = [jnp.where(even_slot, a, b) for a, b in zip(first_tiles, other_tiles)]
    high_tiles = [jnp.where(even_slot, b, a) for a, b in zip(first_tiles, other_tiles)]

    def rows_of(place, start, count):
        at = [(start + row) * LANES for row in range(count)]
        return jnp.concatenate(
            [arrived_ref[place, 0:1, lane : lane + LANES] for lane in at], axis=0
        )

    low_place, _, high_place = near_places(leaves)
    coupled = couple_rows(
        jnp.concatenate(
            [rows_of(place, image_count, 1) for place in places_of(leaves, trees)], axis=0
        ),
        weights_ref,
    )
    images = [
        *row_groups(rows_of(low_place, 0, image_count)),
        *lane_tiles(image_ref[...]),
        *row_groups(rows_of(high_place, 0, image_count)),
        jnp.concatenate([coupled, jnp.zeros((VECS, LANES - rank), F32)], axis=1),
    ]
    windows = [
        *low_tiles,
        *lane_tiles(window),
        *high_tiles,
        window_coupled_ref[...],
    ]
    solved, record = orthogonalized(total, windows, images)
    record_ref[...] = record
    low_block, new_block, high_block = (
        jnp.concatenate(solved[at : at + per_row], axis=1)
        for at in range(0, 3 * per_row, per_row)
    )
    next_window = jnp.concatenate([window[VECS:], new_block], axis=0)
    next_window_ref[...] = next_window
    blocks = [block.astype(BF16) for block in (low_block, new_block, high_block)]
    near_part = near_field(blocks, choice_ref, near_ref)
    near_part_ref[...] = near_part
    far_part = jnp.dot(
        solved[-1][:, :rank].astype(BF16), u_ref[...], preferred_element_type=F32
    )
    skeleton, coarse = mapped(new_block.astype(BF16), maps_ref)
    width = LANES // VECS
    packed = one_row(product_lanes(next_window, near_part + far_part, width))
    tree_rows = jnp.concatenate([one_row(skeleton), packed], axis=0)
    level_rows = jnp.concatenate([one_row(coarse), packed], axis=0)

    def store(slot, at):
        slots_ref[slot] = level_rows

    over_slots(slots, store)

    def store_tree(leaf, at):
        slots_ref[own_tree * leaves + leaf] = tree_rows

    over_slots(leaves, store_tree)


def end_kernel(
    trees,
    rows_all,
    arrived_ref,
    flat_ref,
    window_ref,
    near_part_ref,
    weights_ref,
    u_ref,
    first_ref,
    block_ref,
    records_ref,
):
    leaves = arrived_ref.shape[0] // trees
    rows = jnp.concatenate(
        [arrived_ref[place, 0:1, :] for place in places_of(leaves, trees)], axis=0
    )
    coupled = couple_rows(rows, weights_ref)
    far_part = jnp.dot(coupled.astype(BF16), u_ref[...], preferred_element_type=F32)
    step = flat_ref.shape[0] // arrived_ref.shape[0] * VECS
    total = flat_ref[0:step]
    for at in range(step, flat_ref.shape[0], step):
        total = total + flat_ref[at : at + step]
    total = sum(total[at : at + 1] for at in range(1, step, step // VECS))
    total = total * (1.0 / rows_all)
    image = near_part_ref[...] + far_part
    solved, record = orthogonalized(total, lane_tiles(window_ref[...]), lane_tiles(image))
    store_rows(block_ref, jnp.concatenate(solved, axis=1))
    used = records_ref.shape[2]
    records_ref[0] = first_ref[:, :used]
    records_ref[1] = record[:, :used]


def call(kernel, name, outs, ins, places, scratch=(), vmem=16 << 20, bytes_accessed=1 << 20):
    spaces = {"s": pltpu.SMEM, "v": pltpu.VMEM, "h": pltpu.HBM}
    return pl.pallas_call(
        kernel,
        name=name,
        out_shape=[jax.ShapeDtypeStruct(shape, dtype) for shape, dtype in outs],
        in_specs=[pl.BlockSpec(memory_space=spaces[place]) for place in places],
        out_specs=[pl.BlockSpec(memory_space=pltpu.VMEM)] * len(outs),
        scratch_shapes=list(scratch),
        cost_estimate=pl.CostEstimate(flops=0, bytes_accessed=bytes_accessed, transcendentals=0),
        compiler_params=pltpu.CompilerParams(vmem_limit_bytes=vmem),
    )(*ins)


def exchange(slots):
    return lax.all_to_all(slots, AXES, 0, 0, tiled=True)


def local(
    krylov_basis,
    near_block,
    near_col,
    near_count,
    far_col,
    v_basis,
    u_basis,
    far_coupling,
    transfer,
    top_coupling,
):
    basis, _, size = krylov_basis.shape
    trees = lax.axis_size("lvl")
    leaves = lax.axis_size("clus")
    devices = leaves * trees
    rows_all = float(devices * size)
    flat_basis = krylov_basis.reshape(-1, LANES)
    v_own, u_own, transfer_own = v_basis[0, 0], u_basis[0, 0], transfer[0, 0]
    rank = v_own.shape[0]
    far_own, top_own, near_own = far_coupling[0, 0], top_coupling[0, 0], near_block[0, 0]
    image_like = ((VECS, size), F32)
    window_like = ((basis, size), F32)
    per_slot = VECS * size // LANES + 3
    record_like = ((VECS, LANES), F32)
    maps_like = ((4 * LANES, size), BF16)
    choice_like = ((-(-3 * near_own.shape[0] // 8) * 8, LANES), F32)
    weights_like = ((3, rank, (leaves + trees - 2) * LANES), BF16)
    slots, window = call(
        functools.partial(begin_kernel, leaves),
        "begin",
        [((devices, VECS, size + 2 * LANES), BF16), window_like],
        [flat_basis, v_own, transfer_own],
        "hhh",
        [
            pltpu.VMEM(flat_basis.shape, F32),
            pltpu.VMEM(v_own.shape, BF16),
            pltpu.VMEM(transfer_own.shape, F32),
            pltpu.SemaphoreType.DMA((3,)),
        ],
        vmem=None,
    )
    arrived = exchange(slots)
    weights, near_here, maps, choice = call(
        functools.partial(prepare_kernel, leaves),
        "prepare",
        [weights_like, (near_own.shape, BF16), maps_like, choice_like],
        [near_col, near_count, far_col, near_own, far_own, v_own, transfer_own, top_own],
        "ssshvvvv",
        [pltpu.SemaphoreType.DMA],
    )
    image, slots, window_coupled = call(
        functools.partial(first_kernel, trees),
        "first",
        [image_like, ((devices * per_slot, LANES), F32), ((basis, LANES), F32)],
        [
            arrived,
            window,
            weights,
            near_here,
            choice,
            u_own,
            maps,
        ],
        "v" * 7,
    )
    arrived = exchange(slots.reshape(devices, 1, per_slot * LANES))
    slots, window, near_part, record = call(
        functools.partial(middle_kernel, trees, rows_all),
        "middle",
        [((devices, 2, LANES), F32), window_like, image_like, record_like],
        [
            arrived,
            arrived.reshape(-1, LANES),
            window,
            image,
            window_coupled,
            weights,
            near_here,
            choice,
            u_own,
            maps,
        ],
        "v" * 10,
    )
    arrived = exchange(slots)
    block, records = call(
        functools.partial(end_kernel, trees, rows_all),
        "end",
        [((VECS * size // LANES, LANES), F32), ((STEPS, VECS, basis + VECS), F32)],
        [arrived, arrived.reshape(-1, LANES), window, near_part, weights, u_own, record],
        "v" * 7,
    )
    return (block.reshape(VECS, 1, size), jnp.transpose(records, (0, 2, 1)))


def solution(mesh):
    return jax.shard_map(
        local,
        mesh=mesh,
        in_specs=(
            P(None, "lvl", "clus"),
            P("lvl", "clus", None, None, None),
            P("lvl", "clus", None),
            P("lvl", "clus"),
            P("lvl", "clus", None),
            P("lvl", "clus", None, None),
            P("lvl", "clus", None, None),
            P("lvl", "clus", None, None, None),
            P("lvl", "clus", None, None),
            P("lvl", "clus", None, None, None),
        ),
        out_specs=(P(None, "lvl", "clus"), P()),
        check_vma=False,
    )
```

```python
import functools

import jax
import jax.numpy as jnp
from jax import lax
from jax.experimental import pallas as pl
from jax.experimental.pallas import tpu as pltpu
from jax.sharding import PartitionSpec as P

VECS = 4
STEPS = 2
LANES = 128
PIECE = 16
UNROLL = 32
AXES = ("lvl", "clus")

PRECISE = lax.Precision.HIGHEST
ROWS_DIMS = (((1,), (1,)), ((), ()))
F32, BF16 = jnp.float32, jnp.bfloat16


def rows_dot(left, right, precision=None):
    return lax.dot_general(
        left, right, ROWS_DIMS, precision=precision, preferred_element_type=F32
    )


def precise_dot(left, right):
    return jnp.dot(left, right, precision=PRECISE, preferred_element_type=F32)


def three_parts(values):
    high = values.astype(BF16)
    rest = values - high.astype(F32)
    middle = rest.astype(BF16)
    low = (rest - middle.astype(F32)).astype(BF16)
    return high, middle, low


def lane_parts(values, part):
    high = values.astype(BF16).astype(F32)
    rest = values - high
    middle = rest.astype(BF16).astype(F32)
    low = rest - middle
    return jnp.where(part == 0, high, jnp.where(part == 1, middle, jnp.where(part == 2, low, 0.0)))


def lanes_of(shape):
    return lax.broadcasted_iota(jnp.int32, shape, len(shape) - 1)


def over_slots(count, store):
    step = min(count, UNROLL)
    if count == step:
        for slot in range(count):
            store(slot, slot)
        return

    def body(at, carry):
        for inner in range(step):
            store(at * step + inner, inner)
        return carry

    lax.fori_loop(0, count // step, body, 0)


def split_rows(flat, rows):
    halves = flat.shape[0] // rows
    return jnp.concatenate(
        [flat[pl.ds(half, rows, stride=halves), :] for half in range(halves)], axis=1
    )


def store_rows(flat_ref, values):
    rows = values.shape[0]
    halves = flat_ref.shape[0] // rows
    for half in range(halves):
        flat_ref[pl.ds(half, rows, stride=halves), :] = values[:, half * LANES : (half + 1) * LANES]


def row_groups(rows):
    return [rows[at : at + VECS] for at in range(0, rows.shape[0], VECS)]


def lane_tiles(values):
    return [values[:, at : at + LANES] for at in range(0, values.shape[1], LANES)]


def replicated(column):
    return jnp.broadcast_to(column, (column.shape[0], LANES))


def lane_sum(pairs):
    return replicated(jnp.sum(sum(left * right for left, right in pairs), axis=1, keepdims=True))


def begin_kernel(leaves, basis_hbm, v_hbm, transfer_hbm, slots_ref, *scratch):
    basis_ref, v_ref, transfer_ref, sems = scratch
    copies = [
        pltpu.make_async_copy(source, target, sems.at[at])
        for at, (source, target) in enumerate(
            ((basis_hbm, basis_ref), (v_hbm, v_ref), (transfer_hbm, transfer_ref))
        )
    ]
    for copy in copies:
        copy.start()
    for copy in copies:
        copy.wait()
    rank, size = v_ref.shape
    basis = basis_ref.shape[0] * LANES // size
    window = split_rows(basis_ref, basis)
    current = window[basis - VECS :]
    lowered = current.astype(BF16)
    rest = current - lowered.astype(F32)
    parts = [lowered, *three_parts(window[: basis - VECS]), *three_parts(rest)[:2]]
    parts = jnp.concatenate([part.astype(F32) for part in parts], axis=0).astype(BF16)
    repeats = LANES // rank
    wide_basis = jnp.concatenate([v_ref[...]] * repeats, axis=0)
    rows = row_groups(rows_dot(parts, wide_basis))
    skeletons = jnp.concatenate([rows[0], rows[1] + rows[2] + rows[3], rows[4] + rows[5]], axis=0)
    wide_transfer = jnp.concatenate([transfer_ref[...]] * repeats, axis=1)
    wide_transfer = jnp.concatenate(three_parts(wide_transfer), axis=1)
    wide_transfer = jnp.concatenate([wide_transfer] * repeats, axis=0)
    split = lane_parts(skeletons, lanes_of(skeletons.shape) // rank).astype(BF16)
    coarse = sum(lane_tiles(jnp.dot(split, wide_transfer, preferred_element_type=F32)))
    own_tree = lax.axis_index("lvl")

    def tails(values):
        exact, old, extra = row_groups(values)
        group = lanes_of((VECS, LANES)) // rank
        first = jnp.where(group < 3, lane_parts(exact, group), extra)
        return first.astype(BF16), lane_parts(old, group - (repeats - 2))

    tree_first, tree_second = tails(skeletons)
    level_first, level_second = tails(coarse)
    kept = lanes_of((VECS, LANES)) >= LANES - 2 * rank
    flat = basis_ref[...]
    turns = LANES // PIECE
    turned = [pltpu.roll(flat, LANES - PIECE * c, 1) if c else flat for c in range(turns)]
    part = lanes_of(flat.shape) // PIECE
    pieces = [
        lane_parts(
            jnp.where(
                part == 0, turned[c], jnp.where(part == 1, turned[c - 1], turned[c - 2])
            ),
            part,
        )
        for c in range(turns)
    ]

    def store(slot, at):
        row, side = at * VECS // turns % flat.shape[0], at * VECS % turns
        piece = [pieces[side + v][row : row + 1] for v in range(VECS)]
        same = lax.div(jnp.int32(slot), jnp.int32(leaves)) == own_tree
        second = jnp.where(same, tree_second, level_second)
        piece = jnp.where(kept, second, jnp.concatenate(piece, axis=0))
        slots_ref[slot, :, :size] = lowered
        slots_ref[slot, :, size : size + LANES] = level_first
        slots_ref[slot, :, size + LANES :] = piece.astype(BF16)

    over_slots(slots_ref.shape[0], store)

    def store_tree(leaf, at):
        slots_ref[own_tree * leaves + leaf, :, size : size + LANES] = tree_first

    over_slots(leaves, store_tree)


def prepare_kernel(
    leaves,
    near_col_ref,
    near_count_ref,
    far_col_ref,
    near_hbm,
    far_coupling_ref,
    v_ref,
    transfer_ref,
    top_ref,
    weights_ref,
    near_ref,
    maps_ref,
    choice_ref,
    sem,
):
    copy = pltpu.make_async_copy(near_hbm, near_ref, sem)
    copy.start()
    own_tree = lax.axis_index("lvl")
    far_slots = far_coupling_ref.shape[0]
    trees, rank = top_ref.shape[0], top_ref.shape[1]
    transfer = transfer_ref[...]
    own_leaf = lax.axis_index("clus")
    for slot in range(leaves + trees - 2):
        if slot < leaves - 1:
            leaf = lax.rem(own_leaf + 1 + slot, jnp.int32(leaves))
            block = jnp.zeros((rank, rank), F32)
            for at in range(far_slots):
                block = block + jnp.where(far_col_ref[0, 0, at] == leaf, far_coupling_ref[at], 0.0)
        else:
            tree = lax.rem(own_tree + 2 + slot - leaves, jnp.int32(trees))
            block = precise_dot(transfer, top_ref[tree])
        wide = jnp.concatenate([block] * (LANES // rank), axis=1)
        for part, piece in enumerate(three_parts(wide)):
            weights_ref[part, :, slot * LANES : (slot + 1) * LANES] = piece
    v_basis = v_ref[...]
    carried = precise_dot(transfer.T, v_basis.astype(F32))
    for part, piece in enumerate((v_basis, *three_parts(carried))):
        for at in range(part * LANES, (part + 1) * LANES, rank):
            maps_ref[at : at + rank] = piece
    count = near_count_ref[0, 0]
    rows = lax.broadcasted_iota(jnp.int32, choice_ref.shape, 0)
    choice = jnp.zeros(choice_ref.shape, F32)
    for slot in range(near_ref.shape[0]):
        for side in range(3):
            wanted = (near_col_ref[0, 0, slot] == own_leaf + side - 1) & (slot < count)
            choice = jnp.where(rows == 3 * slot + side, jnp.where(wanted, 1.0, 0.0), choice)
    choice_ref[...] = choice
    copy.wait()


def places_of(leaves, trees):
    own_tree = lax.axis_index("lvl")
    own_leaf = lax.axis_index("clus")
    others = [lax.rem(own_leaf + 1 + at, jnp.int32(leaves)) for at in range(leaves - 1)]
    places = [own_tree * leaves + leaf for leaf in others]
    others = [lax.rem(own_tree + 1 + at, jnp.int32(trees)) for at in range(trees - 1)]
    return places + [tree * leaves + own_leaf for tree in others]


def near_places(leaves):
    start = lax.axis_index("lvl") * leaves
    own_leaf = lax.axis_index("clus")
    low = jnp.maximum(own_leaf - 1, 0)
    high = jnp.minimum(own_leaf + 1, leaves - 1)
    return [start + leaf for leaf in (low, own_leaf, high)]


def tree_sum(values):
    while len(values) > 1:
        values = [sum(values[at : at + 2]) for at in range(0, len(values), 2)]
    return values[0]


def near_field(blocks, choice_ref, near_ref):
    choice = choice_ref[...]
    blocks = [[tile.astype(F32) for tile in lane_tiles(block)] for block in blocks]
    parts = []
    for slot in range(near_ref.shape[0]):
        rows = [choice[3 * slot + side : 3 * slot + side + 1] for side in range(3)]
        tiles = [sum(tile * row for tile, row in zip(sides, rows)) for sides in zip(*blocks)]
        parts.append(rows_dot(jnp.concatenate(tiles, axis=1).astype(BF16), near_ref[slot]))
    return tree_sum(parts)


def couple(values, weights_ref):
    lowered = values.astype(BF16)
    return sum(rows_dot(lowered, weights_ref[part]) for part in range(3))


def product_lanes(window, image, period):
    basis = window.shape[0]
    window, image = lane_tiles(window), lane_tiles(image)
    lane = lanes_of((VECS, LANES)) % period
    packed = jnp.zeros((VECS, LANES), F32)
    for b in range(basis):
        product = lane_sum([(tile, other[b : b + 1]) for tile, other in zip(image, window)])
        packed = jnp.where(lane == b, product, packed)
    at = basis
    for u in range(VECS):
        product = lane_sum([(tile, tile[u : u + 1]) for tile in image])
        packed = jnp.where(lane == at + u, product, packed)
    at = at + VECS
    for b in range(basis):
        product = lane_sum([(tile, tile[b : b + 1]) for tile in window])
        for group in range(basis // VECS):
            rows = product[group * VECS : (group + 1) * VECS]
            packed = jnp.where(lane == at + group * basis + b, rows, packed)
    return packed


def couple_rows(rows, weights_ref):
    shape = (VECS, LANES)
    own = lanes_of(shape) // (LANES // VECS) == lax.broadcasted_iota(jnp.int32, shape, 0)
    parts = [
        jnp.concatenate(
            [jnp.where(own, part[at : at + 1], 0.0) for at in range(rows.shape[0])], axis=1
        )
        for part in (piece.astype(F32) for piece in three_parts(rows))
    ]
    return sum(row_groups(couple(jnp.concatenate(parts, axis=0), weights_ref)))


def one_row(values):
    width = LANES // VECS
    own = lanes_of(values.shape) // width == lax.broadcasted_iota(jnp.int32, values.shape, 0)
    return jnp.sum(jnp.where(own, values, 0.0), axis=0, keepdims=True)


def mapped(rows, maps_ref):
    products = lane_tiles(rows_dot(rows, maps_ref[...]))
    skeleton, coarse = products[0], products[1] + products[2] + products[3]
    return sum(row_groups(skeleton)), sum(row_groups(coarse))


def first_kernel(
    trees,
    arrived_ref,
    basis_ref,
    weights_ref,
    near_ref,
    choice_ref,
    u_ref,
    maps_ref,
    image_ref,
    slots_ref,
    window_coupled_ref,
):
    own_tree = lax.axis_index("lvl")
    size = near_ref.shape[1]
    rank = u_ref.shape[0]
    leaves = arrived_ref.shape[0] // trees
    places = places_of(leaves, trees)
    first = [arrived_ref[place, :, size : size + LANES] for place in places]
    second = [arrived_ref[place, :, size + LANES :] for place in places]
    first = jnp.concatenate(first, axis=1).astype(F32)
    second = jnp.concatenate(second, axis=1).astype(F32)
    lane = lanes_of(first.shape) % LANES
    exact = jnp.where(lane < 3 * rank, first, 0.0)
    old = jnp.where(lane >= LANES - 2 * rank, second, 0.0)
    rows = couple(jnp.concatenate([exact, first, old], axis=0), weights_ref)
    linear = jnp.concatenate([rows[2 * VECS :], rows[VECS : 2 * VECS]], axis=0)
    blank = jnp.zeros((2 * VECS, LANES - rank), F32)
    window_coupled_ref[...] = jnp.concatenate([linear, blank], axis=1)
    image = jnp.dot(rows[:VECS].astype(BF16), u_ref[...], preferred_element_type=F32)
    blocks = [arrived_ref[place, :, :size] for place in near_places(leaves)]
    image = image + near_field(blocks, choice_ref, near_ref)
    image_ref[...] = image
    width = LANES // VECS
    packed = one_row(product_lanes(split_rows(basis_ref, window_coupled_ref.shape[0]), image, width))
    parts = [part.astype(F32) for part in three_parts(image)]
    skeleton, coarse = mapped(jnp.concatenate(parts, axis=0).astype(BF16), maps_ref)
    tree_row, level_row = one_row(skeleton), one_row(coarse)
    image_rows = jnp.concatenate(lane_tiles(image), axis=0)
    per_slot = image_rows.shape[0] + 3
    total = slots_ref.shape[0] // per_slot
    step = min(total, UNROLL)
    shape = (2 * VECS, LANES)
    lane = lanes_of(shape)
    row = lax.broadcasted_iota(jnp.int32, shape, 0)
    own = lane // PIECE % VECS == row % VECS

    def fill(part_ref, start):
        for inner in range(0, step, 2):
            sides = []
            for shift in (-1, 1):
                near = [start + inner + at + shift for at in range(2)]
                if isinstance(start, int):
                    near = [min(max(slot, 0), total - 1) for slot in near]
                else:
                    near = [jnp.clip(slot, 0, total - 1) for slot in near]
                near = [arrived_ref[slot, :, size + LANES :].astype(F32) for slot in near]
                sides.append(jnp.concatenate(near, axis=0))
            both = jnp.where(lane < LANES // 2, sides[0], pltpu.roll(sides[1], LANES // 2, 1))
            both = (
                both
                + pltpu.roll(both, LANES - PIECE, 1)
                + pltpu.roll(both, LANES - 2 * PIECE, 1)
            )
            both = jnp.where(own, pltpu.roll(both, 0, 1, stride=PIECE, stride_axis=0), 0.0)
            for at in range(2):
                relay = jnp.sum(both[at * VECS : (at + 1) * VECS], axis=0, keepdims=True)
                slot = jnp.int32(start + inner + at)
                same = lax.div(slot, jnp.int32(leaves)) == own_tree
                far = jnp.where(same, tree_row, level_row)
                first_row = (inner + at) * per_slot
                part_ref[first_row : first_row + per_slot] = jnp.concatenate(
                    [image_rows, far, relay, packed], axis=0
                )

    if total == step:
        fill(slots_ref, 0)
    else:

        def body(at, carry):
            start = pl.multiple_of(at * (step * per_slot), 8)
            fill(slots_ref.at[pl.ds(start, step * per_slot)], at * step)
            return carry

        lax.fori_loop(0, total // step, body, 0)


def orthogonalized(total, windows, images, more=()):
    basis = windows[0].shape[0]
    shape = (VECS, LANES)
    row, lane = lax.broadcasted_iota(jnp.int32, shape, 0), lanes_of(shape)
    total = jnp.broadcast_to(total, shape)

    def column_of(at):
        places = row * (LANES // VECS) + at
        return jnp.take_along_axis(total, places, axis=1, mode="promise_in_bounds")

    projection = [column_of(b) for b in range(basis)]
    square = [column_of(basis + u) for u in range(VECS)]
    start = basis + VECS
    inner = []
    for other in range(basis):
        value = -2.0 * projection[other]
        for group in range(basis // VECS):
            metric = column_of(start + group * basis + other)
            for v in range(VECS):
                value = value + projection[group * VECS + v] * metric[v : v + 1]
        inner.append(value)
    columns = []
    for u in range(VECS):
        value = square[u]
        for b in range(basis):
            value = value + inner[b] * projection[b][u : u + 1]
        columns.append(value)
    remainders = []
    for window, image in zip(windows, images):
        for b in range(basis):
            image = image - projection[b] * window[b : b + 1]
        remainders.append(image)
    remainders = [sum(pair) for pair in zip(remainders, more)] if more else remainders
    record = jnp.zeros(shape, F32)
    for b in range(basis):
        record = jnp.where(lane == b, projection[b], record)
    for j in range(VECS):
        pivot = columns[j][j : j + 1]
        scale = lax.rsqrt(pivot)
        lower = jnp.where(row > j, columns[j] * scale, 0.0)
        record = jnp.where(lane == basis + j, jnp.where(row == j, pivot * scale, lower), record)
        for u in range(j + 1, VECS):
            columns[u] = columns[u] - lower * lower[u : u + 1]
        for t, remainder in enumerate(remainders):
            solved = remainder[j : j + 1] * scale
            remainders[t] = jnp.where(row == j, solved, remainder - lower * solved)
    return remainders, record


def middle_kernel(
    trees,
    rows_all,
    arrived_ref,
    flat_ref,
    basis_ref,
    image_ref,
    window_coupled_ref,
    weights_ref,
    near_ref,
    choice_ref,
    u_ref,
    maps_ref,
    slots_ref,
    next_window_ref,
    near_part_ref,
    record_ref,
):
    own_tree = lax.axis_index("lvl")
    basis, size = next_window_ref.shape
    window = split_rows(basis_ref, basis)
    rank = u_ref.shape[0]
    lane = lanes_of((VECS, LANES))
    slots = arrived_ref.shape[0]
    leaves = slots // trees
    per_slot = flat_ref.shape[0] // slots
    per_row = size // LANES
    image_count = VECS * per_row
    rows = [
        flat_ref[pl.ds(per_slot * at + image_count + 2, 8, stride=per_slot), :]
        for at in range(0, slots, 8)
    ]
    total = jnp.sum(tree_sum(rows), axis=0, keepdims=True) * (1.0 / rows_all)
    first_tiles, other_tiles = [], []
    left = lanes_of((basis, LANES)) < LANES // 2
    for half in range(per_row):
        even, odd = (
            flat_ref[
                pl.ds(
                    per_slot * (2 * half + side) + image_count + 1,
                    basis,
                    stride=2 * per_row * per_slot,
                ),
                :,
            ]
            for side in range(2)
        )
        first_tiles.append(jnp.where(left, even, pltpu.roll(odd, LANES // 2, 1)))
        other_tiles.append(jnp.where(left, pltpu.roll(even, LANES // 2, 1), odd))
    own_slot = own_tree * leaves + lax.axis_index("clus")
    even_slot = lax.rem(own_slot, jnp.int32(2)) == 0
    low_tiles = [jnp.where(even_slot, a, b) for a, b in zip(first_tiles, other_tiles)]
    high_tiles = [jnp.where(even_slot, b, a) for a, b in zip(first_tiles, other_tiles)]

    def rows_of(place, start, count):
        at = [(start + row) * LANES for row in range(count)]
        return jnp.concatenate(
            [arrived_ref[place, 0:1, lane : lane + LANES] for lane in at], axis=0
        )

    low_place, _, high_place = near_places(leaves)
    coupled = couple_rows(
        jnp.concatenate(
            [rows_of(place, image_count, 1) for place in places_of(leaves, trees)], axis=0
        ),
        weights_ref,
    )
    images = [
        *row_groups(rows_of(low_place, 0, image_count)),
        *lane_tiles(image_ref[...]),
        *row_groups(rows_of(high_place, 0, image_count)),
        jnp.concatenate([coupled, jnp.zeros((VECS, LANES - rank), F32)], axis=1),
    ]
    windows = [
        *low_tiles,
        *lane_tiles(window),
        *high_tiles,
        window_coupled_ref[...],
    ]
    solved, record = orthogonalized(total, windows, images)
    record_ref[...] = record
    low_block, new_block, high_block = (
        jnp.concatenate(solved[at : at + per_row], axis=1)
        for at in range(0, 3 * per_row, per_row)
    )
    next_window = jnp.concatenate([window[VECS:], new_block], axis=0)
    next_window_ref[...] = next_window
    blocks = [block.astype(BF16) for block in (low_block, new_block, high_block)]
    near_part = near_field(blocks, choice_ref, near_ref)
    near_part_ref[...] = near_part
    far_part = jnp.dot(
        solved[-1][:, :rank].astype(BF16), u_ref[...], preferred_element_type=F32
    )
    skeleton, coarse = mapped(new_block.astype(BF16), maps_ref)
    width = LANES // VECS
    packed = one_row(product_lanes(next_window, near_part + far_part, width))
    tree_rows = jnp.concatenate([one_row(skeleton), packed], axis=0)
    level_rows = jnp.concatenate([one_row(coarse), packed], axis=0)

    def store(slot, at):
        slots_ref[slot] = level_rows

    over_slots(slots, store)

    def store_tree(leaf, at):
        slots_ref[own_tree * leaves + leaf] = tree_rows

    over_slots(leaves, store_tree)


def end_kernel(
    trees,
    rows_all,
    arrived_ref,
    flat_ref,
    window_ref,
    near_part_ref,
    weights_ref,
    u_ref,
    first_ref,
    block_ref,
    records_ref,
):
    leaves = arrived_ref.shape[0] // trees
    rows = jnp.concatenate(
        [arrived_ref[place, 0:1, :] for place in places_of(leaves, trees)], axis=0
    )
    coupled = couple_rows(rows, weights_ref)
    far_part = jnp.dot(coupled.astype(BF16), u_ref[...], preferred_element_type=F32)
    step = flat_ref.shape[0] // arrived_ref.shape[0] * VECS
    total = flat_ref[0:step]
    for at in range(step, flat_ref.shape[0], step):
        total = total + flat_ref[at : at + step]
    total = sum(total[at : at + 1] for at in range(1, step, step // VECS))
    total = total * (1.0 / rows_all)
    solved, record = orthogonalized(
        total,
        lane_tiles(window_ref[...]),
        lane_tiles(near_part_ref[...]),
        lane_tiles(far_part),
    )
    store_rows(block_ref, jnp.concatenate(solved, axis=1))
    used = records_ref.shape[2]
    records_ref[0] = first_ref[:, :used]
    records_ref[1] = record[:, :used]


def call(kernel, name, outs, ins, places, scratch=(), vmem=16 << 20, bytes_accessed=1 << 20):
    spaces = {"s": pltpu.SMEM, "v": pltpu.VMEM, "h": pltpu.HBM}
    return pl.pallas_call(
        kernel,
        name=name,
        out_shape=[jax.ShapeDtypeStruct(shape, dtype) for shape, dtype in outs],
        in_specs=[pl.BlockSpec(memory_space=spaces[place]) for place in places],
        out_specs=[pl.BlockSpec(memory_space=pltpu.VMEM)] * len(outs),
        scratch_shapes=list(scratch),
        cost_estimate=pl.CostEstimate(flops=0, bytes_accessed=bytes_accessed, transcendentals=0),
        compiler_params=pltpu.CompilerParams(vmem_limit_bytes=vmem),
    )(*ins)


def exchange(slots):
    return lax.all_to_all(slots, AXES, 0, 0, tiled=True)


def local(
    krylov_basis,
    near_block,
    near_col,
    near_count,
    far_col,
    v_basis,
    u_basis,
    far_coupling,
    transfer,
    top_coupling,
):
    basis, _, size = krylov_basis.shape
    trees = lax.axis_size("lvl")
    leaves = lax.axis_size("clus")
    devices = leaves * trees
    rows_all = float(devices * size)
    flat_basis = krylov_basis.reshape(-1, LANES)
    v_own, u_own, transfer_own = v_basis[0, 0], u_basis[0, 0], transfer[0, 0]
    rank = v_own.shape[0]
    far_own, top_own, near_own = far_coupling[0, 0], top_coupling[0, 0], near_block[0, 0]
    image_like = ((VECS, size), F32)
    window_like = ((basis, size), F32)
    per_slot = VECS * size // LANES + 3
    record_like = ((VECS, LANES), F32)
    maps_like = ((4 * LANES, size), BF16)
    choice_like = ((-(-3 * near_own.shape[0] // 8) * 8, LANES), F32)
    weights_like = ((3, rank, (leaves + trees - 2) * LANES), BF16)
    (slots,) = call(
        functools.partial(begin_kernel, leaves),
        "begin",
        [((devices, VECS, size + 2 * LANES), BF16)],
        [flat_basis, v_own, transfer_own],
        "hhh",
        [
            pltpu.VMEM(flat_basis.shape, F32),
            pltpu.VMEM(v_own.shape, BF16),
            pltpu.VMEM(transfer_own.shape, F32),
            pltpu.SemaphoreType.DMA((3,)),
        ],
        vmem=None,
    )
    arrived = exchange(slots)
    weights, near_here, maps, choice = call(
        functools.partial(prepare_kernel, leaves),
        "prepare",
        [weights_like, (near_own.shape, BF16), maps_like, choice_like],
        [near_col, near_count, far_col, near_own, far_own, v_own, transfer_own, top_own],
        "ssshvvvv",
        [pltpu.SemaphoreType.DMA],
    )
    image, slots, window_coupled = call(
        functools.partial(first_kernel, trees),
        "first",
        [image_like, ((devices * per_slot, LANES), F32), ((basis, LANES), F32)],
        [
            arrived,
            flat_basis,
            weights,
            near_here,
            choice,
            u_own,
            maps,
        ],
        "v" * 7,
    )
    arrived = exchange(slots.reshape(devices, 1, per_slot * LANES))
    slots, window, near_part, record = call(
        functools.partial(middle_kernel, trees, rows_all),
        "middle",
        [((devices, 2, LANES), F32), window_like, image_like, record_like],
        [
            arrived,
            arrived.reshape(-1, LANES),
            flat_basis,
            image,
            window_coupled,
            weights,
            near_here,
            choice,
            u_own,
            maps,
        ],
        "v" * 10,
    )
    arrived = exchange(slots)
    block, records = call(
        functools.partial(end_kernel, trees, rows_all),
        "end",
        [((VECS * size // LANES, LANES), F32), ((STEPS, VECS, basis + VECS), F32)],
        [arrived, arrived.reshape(-1, LANES), window, near_part, weights, u_own, record],
        "v" * 7,
    )
    return (block.reshape(VECS, 1, size), jnp.transpose(records, (0, 2, 1)))


def solution(mesh):
    return jax.shard_map(
        local,
        mesh=mesh,
        in_specs=(
            P(None, "lvl", "clus"),
            P("lvl", "clus", None, None, None),
            P("lvl", "clus", None),
            P("lvl", "clus"),
            P("lvl", "clus", None),
            P("lvl", "clus", None, None),
            P("lvl", "clus", None, None),
            P("lvl", "clus", None, None, None),
            P("lvl", "clus", None, None),
            P("lvl", "clus", None, None, None),
        ),
        out_specs=(P(None, "lvl", "clus"), P()),
        check_vma=False,
    )
```

```python
import functools

import jax
import jax.numpy as jnp
from jax import lax
from jax.experimental import pallas as pl
from jax.experimental.pallas import tpu as pltpu
from jax.sharding import PartitionSpec as P

VECS = 4
STEPS = 2
LANES = 128
PIECE = 16
UNROLL = 32
AXES = ("lvl", "clus")

PRECISE = lax.Precision.HIGHEST
ROWS_DIMS = (((1,), (1,)), ((), ()))
F32, BF16 = jnp.float32, jnp.bfloat16


def rows_dot(left, right, precision=None):
    return lax.dot_general(
        left, right, ROWS_DIMS, precision=precision, preferred_element_type=F32
    )


def precise_dot(left, right):
    return jnp.dot(left, right, precision=PRECISE, preferred_element_type=F32)


def three_parts(values):
    high = values.astype(BF16)
    rest = values - high.astype(F32)
    middle = rest.astype(BF16)
    low = (rest - middle.astype(F32)).astype(BF16)
    return high, middle, low


def lane_parts(values, part):
    high = values.astype(BF16).astype(F32)
    rest = values - high
    middle = rest.astype(BF16).astype(F32)
    low = rest - middle
    return jnp.where(part == 0, high, jnp.where(part == 1, middle, jnp.where(part == 2, low, 0.0)))


def lanes_of(shape):
    return lax.broadcasted_iota(jnp.int32, shape, len(shape) - 1)


def over_slots(count, store):
    step = min(count, UNROLL)
    if count == step:
        for slot in range(count):
            store(slot, slot)
        return

    def body(at, carry):
        for inner in range(step):
            store(at * step + inner, inner)
        return carry

    lax.fori_loop(0, count // step, body, 0)


def split_rows(flat, rows):
    halves = flat.shape[0] // rows
    return jnp.concatenate(
        [flat[pl.ds(half, rows, stride=halves), :] for half in range(halves)], axis=1
    )


def store_rows(flat_ref, values):
    rows = values.shape[0]
    halves = flat_ref.shape[0] // rows
    for half in range(halves):
        flat_ref[pl.ds(half, rows, stride=halves), :] = values[:, half * LANES : (half + 1) * LANES]


def row_groups(rows):
    return [rows[at : at + VECS] for at in range(0, rows.shape[0], VECS)]


def lane_tiles(values):
    return [values[:, at : at + LANES] for at in range(0, values.shape[1], LANES)]


def replicated(column):
    return jnp.broadcast_to(column, (column.shape[0], LANES))


def lane_sum(pairs):
    return replicated(jnp.sum(sum(left * right for left, right in pairs), axis=1, keepdims=True))


def begin_kernel(leaves, basis_hbm, v_hbm, transfer_hbm, slots_ref, *scratch):
    basis_ref, v_ref, transfer_ref, sems = scratch
    copies = [
        pltpu.make_async_copy(source, target, sems.at[at])
        for at, (source, target) in enumerate(
            ((basis_hbm, basis_ref), (v_hbm, v_ref), (transfer_hbm, transfer_ref))
        )
    ]
    for copy in copies:
        copy.start()
    for copy in copies:
        copy.wait()
    rank, size = v_ref.shape
    basis = basis_ref.shape[0] * LANES // size
    window = split_rows(basis_ref, basis)
    current = window[basis - VECS :]
    lowered = current.astype(BF16)
    rest = current - lowered.astype(F32)
    parts = [lowered, *three_parts(window[: basis - VECS]), *three_parts(rest)[:2]]
    parts = jnp.concatenate([part.astype(F32) for part in parts], axis=0).astype(BF16)
    repeats = LANES // rank
    wide_basis = jnp.concatenate([v_ref[...]] * repeats, axis=0)
    rows = row_groups(rows_dot(parts, wide_basis))
    skeletons = jnp.concatenate([rows[0], rows[1] + rows[2] + rows[3], rows[4] + rows[5]], axis=0)
    wide_transfer = jnp.concatenate([transfer_ref[...]] * repeats, axis=1)
    wide_transfer = jnp.concatenate(three_parts(wide_transfer), axis=1)
    wide_transfer = jnp.concatenate([wide_transfer] * repeats, axis=0)
    split = lane_parts(skeletons, lanes_of(skeletons.shape) // rank).astype(BF16)
    coarse = sum(lane_tiles(jnp.dot(split, wide_transfer, preferred_element_type=F32)))
    own_tree = lax.axis_index("lvl")

    def tails(values):
        exact, old, extra = row_groups(values)
        group = lanes_of((VECS, LANES)) // rank
        first = jnp.where(group < 3, lane_parts(exact, group), extra)
        return first.astype(BF16), lane_parts(old, group - (repeats - 2))

    tree_first, tree_second = tails(skeletons)
    level_first, level_second = tails(coarse)
    kept = lanes_of((VECS, LANES)) >= LANES - 2 * rank
    flat = basis_ref[...]
    turns = LANES // PIECE
    turned = [pltpu.roll(flat, LANES - PIECE * c, 1) if c else flat for c in range(turns)]
    part = lanes_of(flat.shape) // PIECE
    pieces = [
        lane_parts(
            jnp.where(
                part == 0, turned[c], jnp.where(part == 1, turned[c - 1], turned[c - 2])
            ),
            part,
        )
        for c in range(turns)
    ]

    def store(slot, at):
        row, side = at * VECS // turns % flat.shape[0], at * VECS % turns
        piece = [pieces[side + v][row : row + 1] for v in range(VECS)]
        same = lax.div(jnp.int32(slot), jnp.int32(leaves)) == own_tree
        second = jnp.where(same, tree_second, level_second)
        piece = jnp.where(kept, second, jnp.concatenate(piece, axis=0))
        slots_ref[slot, :, :size] = lowered
        slots_ref[slot, :, size : size + LANES] = level_first
        slots_ref[slot, :, size + LANES :] = piece.astype(BF16)

    over_slots(slots_ref.shape[0], store)

    def store_tree(leaf, at):
        slots_ref[own_tree * leaves + leaf, :, size : size + LANES] = tree_first

    over_slots(leaves, store_tree)


def prepare_kernel(
    leaves,
    near_col_ref,
    near_count_ref,
    far_col_ref,
    near_hbm,
    far_coupling_ref,
    v_ref,
    transfer_ref,
    top_ref,
    weights_ref,
    near_ref,
    maps_ref,
    choice_ref,
    sem,
):
    copy = pltpu.make_async_copy(near_hbm, near_ref, sem)
    copy.start()
    own_tree = lax.axis_index("lvl")
    far_slots = far_coupling_ref.shape[0]
    trees, rank = top_ref.shape[0], top_ref.shape[1]
    transfer = transfer_ref[...]
    own_leaf = lax.axis_index("clus")
    for slot in range(leaves + trees - 2):
        if slot < leaves - 1:
            leaf = lax.rem(own_leaf + 1 + slot, jnp.int32(leaves))
            block = jnp.zeros((rank, rank), F32)
            for at in range(far_slots):
                block = block + jnp.where(far_col_ref[0, 0, at] == leaf, far_coupling_ref[at], 0.0)
        else:
            tree = lax.rem(own_tree + 2 + slot - leaves, jnp.int32(trees))
            block = precise_dot(transfer, top_ref[tree])
        wide = jnp.concatenate([block] * (LANES // rank), axis=1)
        for part, piece in enumerate(three_parts(wide)):
            weights_ref[part, :, slot * LANES : (slot + 1) * LANES] = piece
    v_basis = v_ref[...]
    carried = precise_dot(transfer.T, v_basis.astype(F32))
    for part, piece in enumerate((v_basis, *three_parts(carried))):
        maps_ref[part * rank : (part + 1) * rank] = piece
    count = near_count_ref[0, 0]
    rows = lax.broadcasted_iota(jnp.int32, choice_ref.shape, 0)
    choice = jnp.zeros(choice_ref.shape, F32)
    for slot in range(near_ref.shape[0]):
        for side in range(3):
            wanted = (near_col_ref[0, 0, slot] == own_leaf + side - 1) & (slot < count)
            choice = jnp.where(rows == 3 * slot + side, jnp.where(wanted, 1.0, 0.0), choice)
    choice_ref[...] = choice
    copy.wait()


def places_of(leaves, trees):
    own_tree = lax.axis_index("lvl")
    own_leaf = lax.axis_index("clus")
    others = [lax.rem(own_leaf + 1 + at, jnp.int32(leaves)) for at in range(leaves - 1)]
    places = [own_tree * leaves + leaf for leaf in others]
    others = [lax.rem(own_tree + 1 + at, jnp.int32(trees)) for at in range(trees - 1)]
    return places + [tree * leaves + own_leaf for tree in others]


def near_places(leaves):
    start = lax.axis_index("lvl") * leaves
    own_leaf = lax.axis_index("clus")
    low = jnp.maximum(own_leaf - 1, 0)
    high = jnp.minimum(own_leaf + 1, leaves - 1)
    return [start + leaf for leaf in (low, own_leaf, high)]


def tree_sum(values):
    while len(values) > 1:
        values = [sum(values[at : at + 2]) for at in range(0, len(values), 2)]
    return values[0]


def near_field(blocks, choice_ref, near_ref):
    choice = choice_ref[...]
    blocks = [[tile.astype(F32) for tile in lane_tiles(block)] for block in blocks]
    parts = []
    for slot in range(near_ref.shape[0]):
        rows = [choice[3 * slot + side : 3 * slot + side + 1] for side in range(3)]
        tiles = [sum(tile * row for tile, row in zip(sides, rows)) for sides in zip(*blocks)]
        parts.append(rows_dot(jnp.concatenate(tiles, axis=1).astype(BF16), near_ref[slot]))
    return tree_sum(parts)


def couple(values, weights_ref):
    lowered = values.astype(BF16)
    return sum(rows_dot(lowered, weights_ref[part]) for part in range(3))


def product_lanes(window, image, period):
    basis = window.shape[0]
    window, image = lane_tiles(window), lane_tiles(image)
    lane = lanes_of((VECS, LANES)) % period
    packed = jnp.zeros((VECS, LANES), F32)
    for b in range(basis):
        product = lane_sum([(tile, other[b : b + 1]) for tile, other in zip(image, window)])
        packed = jnp.where(lane == b, product, packed)
    at = basis
    for u in range(VECS):
        product = lane_sum([(tile, tile[u : u + 1]) for tile in image])
        packed = jnp.where(lane == at + u, product, packed)
    at = at + VECS
    for b in range(basis):
        product = lane_sum([(tile, tile[b : b + 1]) for tile in window])
        for group in range(basis // VECS):
            rows = product[group * VECS : (group + 1) * VECS]
            packed = jnp.where(lane == at + group * basis + b, rows, packed)
    return packed


def couple_rows(rows, weights_ref):
    shape = (VECS, LANES)
    own = lanes_of(shape) // (LANES // VECS) == lax.broadcasted_iota(jnp.int32, shape, 0)
    parts = [
        jnp.concatenate(
            [jnp.where(own, part[at : at + 1], 0.0) for at in range(rows.shape[0])], axis=1
        )
        for part in (piece.astype(F32) for piece in three_parts(rows))
    ]
    return sum(row_groups(couple(jnp.concatenate(parts, axis=0), weights_ref)))


def one_row(values):
    width = LANES // VECS
    own = lanes_of(values.shape) // width == lax.broadcasted_iota(jnp.int32, values.shape, 0)
    return jnp.sum(jnp.where(own, values, 0.0), axis=0, keepdims=True)


def mapped(rows, maps_ref):
    products = sum(row_groups(rows_dot(rows, maps_ref[...])))
    rank = maps_ref.shape[0] // 4
    lane = lanes_of(products.shape) % rank
    spread = [
        jnp.take_along_axis(products, lane + part * rank, axis=1, mode="promise_in_bounds")
        for part in range(4)
    ]
    return spread[0], spread[1] + spread[2] + spread[3]


def first_kernel(
    trees,
    arrived_ref,
    basis_ref,
    weights_ref,
    near_ref,
    choice_ref,
    u_ref,
    maps_ref,
    image_ref,
    slots_ref,
    window_coupled_ref,
):
    own_tree = lax.axis_index("lvl")
    size = near_ref.shape[1]
    rank = u_ref.shape[0]
    leaves = arrived_ref.shape[0] // trees
    places = places_of(leaves, trees)
    first = [arrived_ref[place, :, size : size + LANES] for place in places]
    second = [arrived_ref[place, :, size + LANES :] for place in places]
    first = jnp.concatenate(first, axis=1).astype(F32)
    second = jnp.concatenate(second, axis=1).astype(F32)
    lane = lanes_of(first.shape) % LANES
    exact = jnp.where(lane < 3 * rank, first, 0.0)
    old = jnp.where(lane >= LANES - 2 * rank, second, 0.0)
    rows = couple(jnp.concatenate([exact, first, old], axis=0), weights_ref)
    linear = jnp.concatenate([rows[2 * VECS :], rows[VECS : 2 * VECS]], axis=0)
    blank = jnp.zeros((2 * VECS, LANES - rank), F32)
    window_coupled_ref[...] = jnp.concatenate([linear, blank], axis=1)
    image = jnp.dot(rows[:VECS].astype(BF16), u_ref[...], preferred_element_type=F32)
    blocks = [arrived_ref[place, :, :size] for place in near_places(leaves)]
    image = image + near_field(blocks, choice_ref, near_ref)
    image_ref[...] = image
    width = LANES // VECS
    packed = one_row(product_lanes(split_rows(basis_ref, window_coupled_ref.shape[0]), image, width))
    parts = [part.astype(F32) for part in three_parts(image)]
    skeleton, coarse = mapped(jnp.concatenate(parts, axis=0).astype(BF16), maps_ref)
    tree_row, level_row = one_row(skeleton), one_row(coarse)
    image_rows = jnp.concatenate(lane_tiles(image), axis=0)
    per_slot = image_rows.shape[0] + 3
    total = slots_ref.shape[0] // per_slot
    step = min(total, UNROLL)
    shape = (2 * VECS, LANES)
    lane = lanes_of(shape)
    row = lax.broadcasted_iota(jnp.int32, shape, 0)
    own = lane // PIECE % VECS == row % VECS

    def fill(part_ref, start):
        for inner in range(0, step, 2):
            sides = []
            for shift in (-1, 1):
                near = [start + inner + at + shift for at in range(2)]
                if isinstance(start, int):
                    near = [min(max(slot, 0), total - 1) for slot in near]
                else:
                    near = [jnp.clip(slot, 0, total - 1) for slot in near]
                near = [arrived_ref[slot, :, size + LANES :].astype(F32) for slot in near]
                sides.append(jnp.concatenate(near, axis=0))
            both = jnp.where(lane < LANES // 2, sides[0], pltpu.roll(sides[1], LANES // 2, 1))
            both = (
                both
                + pltpu.roll(both, LANES - PIECE, 1)
                + pltpu.roll(both, LANES - 2 * PIECE, 1)
            )
            both = jnp.where(own, pltpu.roll(both, 0, 1, stride=PIECE, stride_axis=0), 0.0)
            for at in range(2):
                relay = jnp.sum(both[at * VECS : (at + 1) * VECS], axis=0, keepdims=True)
                slot = jnp.int32(start + inner + at)
                same = lax.div(slot, jnp.int32(leaves)) == own_tree
                far = jnp.where(same, tree_row, level_row)
                first_row = (inner + at) * per_slot
                part_ref[first_row : first_row + per_slot] = jnp.concatenate(
                    [image_rows, far, relay, packed], axis=0
                )

    if total == step:
        fill(slots_ref, 0)
    else:

        def body(at, carry):
            start = pl.multiple_of(at * (step * per_slot), 8)
            fill(slots_ref.at[pl.ds(start, step * per_slot)], at * step)
            return carry

        lax.fori_loop(0, total // step, body, 0)


def orthogonalized(total, windows, images, more=()):
    basis = windows[0].shape[0]
    shape = (VECS, LANES)
    row, lane = lax.broadcasted_iota(jnp.int32, shape, 0), lanes_of(shape)
    total = jnp.broadcast_to(total, shape)

    def column_of(at):
        places = row * (LANES // VECS) + at
        return jnp.take_along_axis(total, places, axis=1, mode="promise_in_bounds")

    projection = [column_of(b) for b in range(basis)]
    square = [column_of(basis + u) for u in range(VECS)]
    start = basis + VECS
    inner = []
    for other in range(basis):
        value = -2.0 * projection[other]
        for group in range(basis // VECS):
            metric = column_of(start + group * basis + other)
            for v in range(VECS):
                value = value + projection[group * VECS + v] * metric[v : v + 1]
        inner.append(value)
    columns = []
    for u in range(VECS):
        value = square[u]
        for b in range(basis):
            value = value + inner[b] * projection[b][u : u + 1]
        columns.append(value)
    remainders = []
    for window, image in zip(windows, images):
        for b in range(basis):
            image = image - projection[b] * window[b : b + 1]
        remainders.append(image)
    remainders = [sum(pair) for pair in zip(remainders, more)] if more else remainders
    record = jnp.zeros(shape, F32)
    for b in range(basis):
        record = jnp.where(lane == b, projection[b], record)
    for j in range(VECS):
        pivot = columns[j][j : j + 1]
        scale = lax.rsqrt(pivot)
        lower = jnp.where(row > j, columns[j] * scale, 0.0)
        record = jnp.where(lane == basis + j, jnp.where(row == j, pivot * scale, lower), record)
        for u in range(j + 1, VECS):
            columns[u] = columns[u] - lower * lower[u : u + 1]
        for t, remainder in enumerate(remainders):
            solved = remainder[j : j + 1] * scale
            remainders[t] = jnp.where(row == j, solved, remainder - lower * solved)
    return remainders, record


def middle_kernel(
    trees,
    rows_all,
    arrived_ref,
    flat_ref,
    basis_ref,
    image_ref,
    window_coupled_ref,
    weights_ref,
    near_ref,
    choice_ref,
    u_ref,
    maps_ref,
    slots_ref,
    next_window_ref,
    near_part_ref,
    record_ref,
):
    own_tree = lax.axis_index("lvl")
    basis, size = next_window_ref.shape
    window = split_rows(basis_ref, basis)
    rank = u_ref.shape[0]
    lane = lanes_of((VECS, LANES))
    slots = arrived_ref.shape[0]
    leaves = slots // trees
    per_slot = flat_ref.shape[0] // slots
    per_row = size // LANES
    image_count = VECS * per_row
    rows = [
        flat_ref[pl.ds(per_slot * at + image_count + 2, 8, stride=per_slot), :]
        for at in range(0, slots, 8)
    ]
    total = jnp.sum(tree_sum(rows), axis=0, keepdims=True) * (1.0 / rows_all)
    first_tiles, other_tiles = [], []
    left = lanes_of((basis, LANES)) < LANES // 2
    for half in range(per_row):
        even, odd = (
            flat_ref[
                pl.ds(
                    per_slot * (2 * half + side) + image_count + 1,
                    basis,
                    stride=2 * per_row * per_slot,
                ),
                :,
            ]
            for side in range(2)
        )
        first_tiles.append(jnp.where(left, even, pltpu.roll(odd, LANES // 2, 1)))
        other_tiles.append(jnp.where(left, pltpu.roll(even, LANES // 2, 1), odd))
    own_slot = own_tree * leaves + lax.axis_index("clus")
    even_slot = lax.rem(own_slot, jnp.int32(2)) == 0
    low_tiles = [jnp.where(even_slot, a, b) for a, b in zip(first_tiles, other_tiles)]
    high_tiles = [jnp.where(even_slot, b, a) for a, b in zip(first_tiles, other_tiles)]

    def rows_of(place, start, count):
        at = [(start + row) * LANES for row in range(count)]
        return jnp.concatenate(
            [arrived_ref[place, 0:1, lane : lane + LANES] for lane in at], axis=0
        )

    low_place, _, high_place = near_places(leaves)
    coupled = couple_rows(
        jnp.concatenate(
            [rows_of(place, image_count, 1) for place in places_of(leaves, trees)], axis=0
        ),
        weights_ref,
    )
    images = [
        *row_groups(rows_of(low_place, 0, image_count)),
        *lane_tiles(image_ref[...]),
        *row_groups(rows_of(high_place, 0, image_count)),
        jnp.concatenate([coupled, jnp.zeros((VECS, LANES - rank), F32)], axis=1),
    ]
    windows = [
        *low_tiles,
        *lane_tiles(window),
        *high_tiles,
        window_coupled_ref[...],
    ]
    solved, record = orthogonalized(total, windows, images)
    record_ref[...] = record
    low_block, new_block, high_block = (
        jnp.concatenate(solved[at : at + per_row], axis=1)
        for at in range(0, 3 * per_row, per_row)
    )
    next_window = jnp.concatenate([window[VECS:], new_block], axis=0)
    next_window_ref[...] = next_window
    blocks = [block.astype(BF16) for block in (low_block, new_block, high_block)]
    near_part = near_field(blocks, choice_ref, near_ref)
    near_part_ref[...] = near_part
    far_part = jnp.dot(
        solved[-1][:, :rank].astype(BF16), u_ref[...], preferred_element_type=F32
    )
    skeleton, coarse = mapped(new_block.astype(BF16), maps_ref)
    width = LANES // VECS
    packed = one_row(product_lanes(next_window, near_part + far_part, width))
    tree_rows = jnp.concatenate([one_row(skeleton), packed], axis=0)
    level_rows = jnp.concatenate([one_row(coarse), packed], axis=0)

    def store(slot, at):
        slots_ref[slot] = level_rows

    over_slots(slots, store)

    def store_tree(leaf, at):
        slots_ref[own_tree * leaves + leaf] = tree_rows

    over_slots(leaves, store_tree)


def end_kernel(
    trees,
    rows_all,
    arrived_ref,
    flat_ref,
    window_ref,
    near_part_ref,
    weights_ref,
    u_ref,
    first_ref,
    block_ref,
    records_ref,
):
    leaves = arrived_ref.shape[0] // trees
    rows = jnp.concatenate(
        [arrived_ref[place, 0:1, :] for place in places_of(leaves, trees)], axis=0
    )
    coupled = couple_rows(rows, weights_ref)
    far_part = jnp.dot(coupled.astype(BF16), u_ref[...], preferred_element_type=F32)
    step = flat_ref.shape[0] // arrived_ref.shape[0] * VECS
    total = flat_ref[0:step]
    for at in range(step, flat_ref.shape[0], step):
        total = total + flat_ref[at : at + step]
    total = sum(total[at : at + 1] for at in range(1, step, step // VECS))
    total = total * (1.0 / rows_all)
    solved, record = orthogonalized(
        total,
        lane_tiles(window_ref[...]),
        lane_tiles(near_part_ref[...]),
        lane_tiles(far_part),
    )
    store_rows(block_ref, jnp.concatenate(solved, axis=1))
    used = records_ref.shape[2]
    records_ref[0] = first_ref[:, :used]
    records_ref[1] = record[:, :used]


def call(kernel, name, outs, ins, places, scratch=(), vmem=16 << 20, bytes_accessed=1 << 20):
    spaces = {"s": pltpu.SMEM, "v": pltpu.VMEM, "h": pltpu.HBM}
    return pl.pallas_call(
        kernel,
        name=name,
        out_shape=[jax.ShapeDtypeStruct(shape, dtype) for shape, dtype in outs],
        in_specs=[pl.BlockSpec(memory_space=spaces[place]) for place in places],
        out_specs=[pl.BlockSpec(memory_space=pltpu.VMEM)] * len(outs),
        scratch_shapes=list(scratch),
        cost_estimate=pl.CostEstimate(flops=0, bytes_accessed=bytes_accessed, transcendentals=0),
        compiler_params=pltpu.CompilerParams(vmem_limit_bytes=vmem),
    )(*ins)


def exchange(slots):
    return lax.all_to_all(slots, AXES, 0, 0, tiled=True)


def local(
    krylov_basis,
    near_block,
    near_col,
    near_count,
    far_col,
    v_basis,
    u_basis,
    far_coupling,
    transfer,
    top_coupling,
):
    basis, _, size = krylov_basis.shape
    trees = lax.axis_size("lvl")
    leaves = lax.axis_size("clus")
    devices = leaves * trees
    rows_all = float(devices * size)
    flat_basis = krylov_basis.reshape(-1, LANES)
    v_own, u_own, transfer_own = v_basis[0, 0], u_basis[0, 0], transfer[0, 0]
    rank = v_own.shape[0]
    far_own, top_own, near_own = far_coupling[0, 0], top_coupling[0, 0], near_block[0, 0]
    image_like = ((VECS, size), F32)
    window_like = ((basis, size), F32)
    per_slot = VECS * size // LANES + 3
    record_like = ((VECS, LANES), F32)
    maps_like = ((4 * rank, size), BF16)
    choice_like = ((-(-3 * near_own.shape[0] // 8) * 8, LANES), F32)
    weights_like = ((3, rank, (leaves + trees - 2) * LANES), BF16)
    (slots,) = call(
        functools.partial(begin_kernel, leaves),
        "begin",
        [((devices, VECS, size + 2 * LANES), BF16)],
        [flat_basis, v_own, transfer_own],
        "hhh",
        [
            pltpu.VMEM(flat_basis.shape, F32),
            pltpu.VMEM(v_own.shape, BF16),
            pltpu.VMEM(transfer_own.shape, F32),
            pltpu.SemaphoreType.DMA((3,)),
        ],
        vmem=None,
    )
    arrived = exchange(slots)
    weights, near_here, maps, choice = call(
        functools.partial(prepare_kernel, leaves),
        "prepare",
        [weights_like, (near_own.shape, BF16), maps_like, choice_like],
        [near_col, near_count, far_col, near_own, far_own, v_own, transfer_own, top_own],
        "ssshvvvv",
        [pltpu.SemaphoreType.DMA],
    )
    image, slots, window_coupled = call(
        functools.partial(first_kernel, trees),
        "first",
        [image_like, ((devices * per_slot, LANES), F32), ((basis, LANES), F32)],
        [
            arrived,
            flat_basis,
            weights,
            near_here,
            choice,
            u_own,
            maps,
        ],
        "v" * 7,
    )
    arrived = exchange(slots.reshape(devices, 1, per_slot * LANES))
    slots, window, near_part, record = call(
        functools.partial(middle_kernel, trees, rows_all),
        "middle",
        [((devices, 2, LANES), F32), window_like, image_like, record_like],
        [
            arrived,
            arrived.reshape(-1, LANES),
            flat_basis,
            image,
            window_coupled,
            weights,
            near_here,
            choice,
            u_own,
            maps,
        ],
        "v" * 10,
    )
    arrived = exchange(slots)
    block, records = call(
        functools.partial(end_kernel, trees, rows_all),
        "end",
        [((VECS * size // LANES, LANES), F32), ((STEPS, VECS, basis + VECS), F32)],
        [arrived, arrived.reshape(-1, LANES), window, near_part, weights, u_own, record],
        "v" * 7,
    )
    return (block.reshape(VECS, 1, size), jnp.transpose(records, (0, 2, 1)))


def solution(mesh):
    return jax.shard_map(
        local,
        mesh=mesh,
        in_specs=(
            P(None, "lvl", "clus"),
            P("lvl", "clus", None, None, None),
            P("lvl", "clus", None),
            P("lvl", "clus"),
            P("lvl", "clus", None),
            P("lvl", "clus", None, None),
            P("lvl", "clus", None, None),
            P("lvl", "clus", None, None, None),
            P("lvl", "clus", None, None),
            P("lvl", "clus", None, None, None),
        ),
        out_specs=(P(None, "lvl", "clus"), P()),
        check_vma=False,
    )
```

```python
import functools

import jax
import jax.numpy as jnp
from jax import lax
from jax.experimental import pallas as pl
from jax.experimental.pallas import tpu as pltpu
from jax.sharding import PartitionSpec as P

VECS = 4
STEPS = 2
LANES = 128
PIECE = 16
UNROLL = 32
AXES = ("lvl", "clus")

PRECISE = lax.Precision.HIGHEST
ROWS_DIMS = (((1,), (1,)), ((), ()))
F32, BF16 = jnp.float32, jnp.bfloat16


def rows_dot(left, right, precision=None):
    return lax.dot_general(
        left, right, ROWS_DIMS, precision=precision, preferred_element_type=F32
    )


def precise_dot(left, right):
    return jnp.dot(left, right, precision=PRECISE, preferred_element_type=F32)


def three_parts(values):
    high = values.astype(BF16)
    rest = values - high.astype(F32)
    middle = rest.astype(BF16)
    low = (rest - middle.astype(F32)).astype(BF16)
    return high, middle, low


def lane_parts(values, part):
    high = values.astype(BF16).astype(F32)
    rest = values - high
    middle = rest.astype(BF16).astype(F32)
    low = rest - middle
    return jnp.where(part == 0, high, jnp.where(part == 1, middle, jnp.where(part == 2, low, 0.0)))


def lanes_of(shape):
    return lax.broadcasted_iota(jnp.int32, shape, len(shape) - 1)


def over_slots(count, store):
    step = min(count, UNROLL)
    if count == step:
        for slot in range(count):
            store(slot, slot)
        return

    def body(at, carry):
        for inner in range(step):
            store(at * step + inner, inner)
        return carry

    lax.fori_loop(0, count // step, body, 0)


def split_rows(flat, rows):
    halves = flat.shape[0] // rows
    return jnp.concatenate(
        [flat[pl.ds(half, rows, stride=halves), :] for half in range(halves)], axis=1
    )


def store_rows(flat_ref, values):
    rows = values.shape[0]
    halves = flat_ref.shape[0] // rows
    for half in range(halves):
        flat_ref[pl.ds(half, rows, stride=halves), :] = values[:, half * LANES : (half + 1) * LANES]


def row_groups(rows):
    return [rows[at : at + VECS] for at in range(0, rows.shape[0], VECS)]


def lane_tiles(values):
    return [values[:, at : at + LANES] for at in range(0, values.shape[1], LANES)]


def replicated(column):
    return jnp.broadcast_to(column, (column.shape[0], LANES))


def lane_sum(pairs):
    return replicated(jnp.sum(sum(left * right for left, right in pairs), axis=1, keepdims=True))


def begin_kernel(leaves, basis_hbm, v_hbm, transfer_hbm, slots_ref, *scratch):
    basis_ref, v_ref, transfer_ref, sems = scratch
    copies = [
        pltpu.make_async_copy(source, target, sems.at[at])
        for at, (source, target) in enumerate(
            ((basis_hbm, basis_ref), (v_hbm, v_ref), (transfer_hbm, transfer_ref))
        )
    ]
    for copy in copies:
        copy.start()
    for copy in copies:
        copy.wait()
    rank, size = v_ref.shape
    basis = basis_ref.shape[0] * LANES // size
    window = split_rows(basis_ref, basis)
    current = window[basis - VECS :]
    lowered = current.astype(BF16)
    rest = current - lowered.astype(F32)
    parts = [lowered, *three_parts(window[: basis - VECS]), *three_parts(rest)[:2]]
    parts = jnp.concatenate([part.astype(F32) for part in parts], axis=0).astype(BF16)
    repeats = LANES // rank
    wide_basis = jnp.concatenate([v_ref[...]] * repeats, axis=0)
    rows = row_groups(rows_dot(parts, wide_basis))
    skeletons = jnp.concatenate([rows[0], rows[1] + rows[2] + rows[3], rows[4] + rows[5]], axis=0)
    wide_transfer = jnp.concatenate([transfer_ref[...]] * repeats, axis=1)
    wide_transfer = jnp.concatenate(three_parts(wide_transfer), axis=1)
    wide_transfer = jnp.concatenate([wide_transfer] * repeats, axis=0)
    split = lane_parts(skeletons, lanes_of(skeletons.shape) // rank).astype(BF16)
    coarse = sum(lane_tiles(jnp.dot(split, wide_transfer, preferred_element_type=F32)))
    own_tree = lax.axis_index("lvl")

    def tails(values):
        exact, old, extra = row_groups(values)
        group = lanes_of((VECS, LANES)) // rank
        first = jnp.where(group < 3, lane_parts(exact, group), extra)
        return first.astype(BF16), lane_parts(old, group - (repeats - 2))

    tree_first, tree_second = tails(skeletons)
    level_first, level_second = tails(coarse)
    kept = lanes_of((VECS, LANES)) >= LANES - 2 * rank
    flat = basis_ref[...]
    turns = LANES // PIECE
    turned = [pltpu.roll(flat, LANES - PIECE * c, 1) if c else flat for c in range(turns)]
    part = lanes_of(flat.shape) // PIECE
    pieces = [
        lane_parts(
            jnp.where(
                part == 0, turned[c], jnp.where(part == 1, turned[c - 1], turned[c - 2])
            ),
            part,
        )
        for c in range(turns)
    ]

    def store(slot, at):
        row, side = at * VECS // turns % flat.shape[0], at * VECS % turns
        piece = [pieces[side + v][row : row + 1] for v in range(VECS)]
        same = lax.div(jnp.int32(slot), jnp.int32(leaves)) == own_tree
        second = jnp.where(same, tree_second, level_second)
        piece = jnp.where(kept, second, jnp.concatenate(piece, axis=0))
        slots_ref[slot, :, :size] = lowered
        slots_ref[slot, :, size : size + LANES] = level_first
        slots_ref[slot, :, size + LANES :] = piece.astype(BF16)

    over_slots(slots_ref.shape[0], store)

    def store_tree(leaf, at):
        slots_ref[own_tree * leaves + leaf, :, size : size + LANES] = tree_first

    over_slots(leaves, store_tree)


def prepare_kernel(
    leaves,
    near_col_ref,
    near_count_ref,
    far_col_ref,
    near_hbm,
    far_coupling_ref,
    v_ref,
    transfer_ref,
    top_ref,
    weights_ref,
    near_ref,
    maps_ref,
    choice_ref,
    sem,
):
    copy = pltpu.make_async_copy(near_hbm, near_ref, sem)
    copy.start()
    own_tree = lax.axis_index("lvl")
    far_slots = far_coupling_ref.shape[0]
    trees, rank = top_ref.shape[0], top_ref.shape[1]
    transfer = transfer_ref[...]
    own_leaf = lax.axis_index("clus")
    for slot in range(leaves + trees - 2):
        if slot < leaves - 1:
            leaf = lax.rem(own_leaf + 1 + slot, jnp.int32(leaves))
            block = jnp.zeros((rank, rank), F32)
            for at in range(far_slots):
                block = block + jnp.where(far_col_ref[0, 0, at] == leaf, far_coupling_ref[at], 0.0)
        else:
            tree = lax.rem(own_tree + 2 + slot - leaves, jnp.int32(trees))
            block = precise_dot(transfer, top_ref[tree])
        wide = jnp.concatenate([block] * (LANES // rank), axis=1)
        for part, piece in enumerate(three_parts(wide)):
            weights_ref[part, :, slot * LANES : (slot + 1) * LANES] = piece
    v_basis = v_ref[...]
    carried = precise_dot(transfer.T, v_basis.astype(F32))
    for part, piece in enumerate((v_basis, *three_parts(carried))):
        maps_ref[part * rank : (part + 1) * rank] = piece
    count = near_count_ref[0, 0]
    rows = lax.broadcasted_iota(jnp.int32, choice_ref.shape, 0)
    choice = jnp.zeros(choice_ref.shape, F32)
    for slot in range(near_ref.shape[0]):
        for side in range(3):
            wanted = (near_col_ref[0, 0, slot] == own_leaf + side - 1) & (slot < count)
            choice = jnp.where(rows == 3 * slot + side, jnp.where(wanted, 1.0, 0.0), choice)
    choice_ref[...] = choice
    copy.wait()


def places_of(leaves, trees):
    own_tree = lax.axis_index("lvl")
    own_leaf = lax.axis_index("clus")
    others = [lax.rem(own_leaf + 1 + at, jnp.int32(leaves)) for at in range(leaves - 1)]
    places = [own_tree * leaves + leaf for leaf in others]
    others = [lax.rem(own_tree + 1 + at, jnp.int32(trees)) for at in range(trees - 1)]
    return places + [tree * leaves + own_leaf for tree in others]


def near_places(leaves):
    start = lax.axis_index("lvl") * leaves
    own_leaf = lax.axis_index("clus")
    low = jnp.maximum(own_leaf - 1, 0)
    high = jnp.minimum(own_leaf + 1, leaves - 1)
    return [start + leaf for leaf in (low, own_leaf, high)]


def tree_sum(values):
    while len(values) > 1:
        values = [sum(values[at : at + 2]) for at in range(0, len(values), 2)]
    return values[0]


def near_field(blocks, choice_ref, near_ref):
    choice = choice_ref[...]
    low, own, high = blocks
    parts = [rows_dot(own, near_ref[0])]
    low, high = ([tile.astype(F32) for tile in lane_tiles(block)] for block in (low, high))
    for slot in range(1, near_ref.shape[0]):
        rows = [choice[3 * slot + side : 3 * slot + side + 1] for side in (0, 2)]
        tiles = [before * rows[0] + after * rows[1] for before, after in zip(low, high)]
        parts.append(rows_dot(jnp.concatenate(tiles, axis=1).astype(BF16), near_ref[slot]))
    return tree_sum(parts)


def couple(values, weights_ref):
    lowered = values.astype(BF16)
    return sum(rows_dot(lowered, weights_ref[part]) for part in range(3))


def product_lanes(window, image, period):
    basis = window.shape[0]
    window, image = lane_tiles(window), lane_tiles(image)
    lane = lanes_of((VECS, LANES)) % period
    packed = jnp.zeros((VECS, LANES), F32)
    for b in range(basis):
        product = lane_sum([(tile, other[b : b + 1]) for tile, other in zip(image, window)])
        packed = jnp.where(lane == b, product, packed)
    at = basis
    for u in range(VECS):
        product = lane_sum([(tile, tile[u : u + 1]) for tile in image])
        packed = jnp.where(lane == at + u, product, packed)
    at = at + VECS
    for b in range(basis):
        product = lane_sum([(tile, tile[b : b + 1]) for tile in window])
        for group in range(basis // VECS):
            rows = product[group * VECS : (group + 1) * VECS]
            packed = jnp.where(lane == at + group * basis + b, rows, packed)
    return packed


def couple_rows(rows, weights_ref):
    shape = (VECS, LANES)
    own = lanes_of(shape) // (LANES // VECS) == lax.broadcasted_iota(jnp.int32, shape, 0)
    parts = [
        jnp.concatenate(
            [jnp.where(own, part[at : at + 1], 0.0) for at in range(rows.shape[0])], axis=1
        )
        for part in (piece.astype(F32) for piece in three_parts(rows))
    ]
    return sum(row_groups(couple(jnp.concatenate(parts, axis=0), weights_ref)))


def one_row(values):
    width = LANES // VECS
    own = lanes_of(values.shape) // width == lax.broadcasted_iota(jnp.int32, values.shape, 0)
    return jnp.sum(jnp.where(own, values, 0.0), axis=0, keepdims=True)


def mapped(rows, maps_ref):
    products = sum(row_groups(rows_dot(rows, maps_ref[...])))
    rank = maps_ref.shape[0] // 4
    lane = lanes_of(products.shape) % rank
    spread = [
        jnp.take_along_axis(products, lane + part * rank, axis=1, mode="promise_in_bounds")
        for part in range(4)
    ]
    return spread[0], spread[1] + spread[2] + spread[3]


def first_kernel(
    trees,
    arrived_ref,
    basis_ref,
    weights_ref,
    near_ref,
    choice_ref,
    u_ref,
    maps_ref,
    image_ref,
    slots_ref,
    window_coupled_ref,
):
    own_tree = lax.axis_index("lvl")
    size = near_ref.shape[1]
    rank = u_ref.shape[0]
    leaves = arrived_ref.shape[0] // trees
    places = places_of(leaves, trees)
    first = [arrived_ref[place, :, size : size + LANES] for place in places]
    second = [arrived_ref[place, :, size + LANES :] for place in places]
    first = jnp.concatenate(first, axis=1).astype(F32)
    second = jnp.concatenate(second, axis=1).astype(F32)
    lane = lanes_of(first.shape) % LANES
    exact = jnp.where(lane < 3 * rank, first, 0.0)
    old = jnp.where(lane >= LANES - 2 * rank, second, 0.0)
    rows = couple(jnp.concatenate([exact, first, old], axis=0), weights_ref)
    linear = jnp.concatenate([rows[2 * VECS :], rows[VECS : 2 * VECS]], axis=0)
    blank = jnp.zeros((2 * VECS, LANES - rank), F32)
    window_coupled_ref[...] = jnp.concatenate([linear, blank], axis=1)
    image = jnp.dot(rows[:VECS].astype(BF16), u_ref[...], preferred_element_type=F32)
    blocks = [arrived_ref[place, :, :size] for place in near_places(leaves)]
    image = image + near_field(blocks, choice_ref, near_ref)
    image_ref[...] = image
    width = LANES // VECS
    packed = one_row(product_lanes(split_rows(basis_ref, window_coupled_ref.shape[0]), image, width))
    parts = [part.astype(F32) for part in three_parts(image)]
    skeleton, coarse = mapped(jnp.concatenate(parts, axis=0).astype(BF16), maps_ref)
    tree_row, level_row = one_row(skeleton), one_row(coarse)
    image_rows = jnp.concatenate(lane_tiles(image), axis=0)
    per_slot = image_rows.shape[0] + 3
    total = slots_ref.shape[0] // per_slot
    step = min(total, UNROLL)
    shape = (2 * VECS, LANES)
    lane = lanes_of(shape)
    row = lax.broadcasted_iota(jnp.int32, shape, 0)
    own = lane // PIECE % VECS == row % VECS

    def fill(part_ref, start):
        for inner in range(0, step, 2):
            sides = []
            for shift in (-1, 1):
                near = [start + inner + at + shift for at in range(2)]
                if isinstance(start, int):
                    near = [min(max(slot, 0), total - 1) for slot in near]
                else:
                    near = [jnp.clip(slot, 0, total - 1) for slot in near]
                near = [arrived_ref[slot, :, size + LANES :].astype(F32) for slot in near]
                sides.append(jnp.concatenate(near, axis=0))
            both = jnp.where(lane < LANES // 2, sides[0], pltpu.roll(sides[1], LANES // 2, 1))
            both = (
                both
                + pltpu.roll(both, LANES - PIECE, 1)
                + pltpu.roll(both, LANES - 2 * PIECE, 1)
            )
            both = jnp.where(own, pltpu.roll(both, 0, 1, stride=PIECE, stride_axis=0), 0.0)
            for at in range(2):
                relay = jnp.sum(both[at * VECS : (at + 1) * VECS], axis=0, keepdims=True)
                slot = jnp.int32(start + inner + at)
                same = lax.div(slot, jnp.int32(leaves)) == own_tree
                far = jnp.where(same, tree_row, level_row)
                first_row = (inner + at) * per_slot
                part_ref[first_row : first_row + per_slot] = jnp.concatenate(
                    [image_rows, far, relay, packed], axis=0
                )

    if total == step:
        fill(slots_ref, 0)
    else:

        def body(at, carry):
            start = pl.multiple_of(at * (step * per_slot), 8)
            fill(slots_ref.at[pl.ds(start, step * per_slot)], at * step)
            return carry

        lax.fori_loop(0, total // step, body, 0)


def orthogonalized(total, windows, images, more=()):
    basis = windows[0].shape[0]
    shape = (VECS, LANES)
    row, lane = lax.broadcasted_iota(jnp.int32, shape, 0), lanes_of(shape)
    total = jnp.broadcast_to(total, shape)

    def column_of(at):
        places = row * (LANES // VECS) + at
        return jnp.take_along_axis(total, places, axis=1, mode="promise_in_bounds")

    projection = [column_of(b) for b in range(basis)]
    square = [column_of(basis + u) for u in range(VECS)]
    start = basis + VECS
    inner = []
    for other in range(basis):
        value = -2.0 * projection[other]
        for group in range(basis // VECS):
            metric = column_of(start + group * basis + other)
            for v in range(VECS):
                value = value + projection[group * VECS + v] * metric[v : v + 1]
        inner.append(value)
    columns = []
    for u in range(VECS):
        value = square[u]
        for b in range(basis):
            value = value + inner[b] * projection[b][u : u + 1]
        columns.append(value)
    remainders = []
    for window, image in zip(windows, images):
        for b in range(basis):
            image = image - projection[b] * window[b : b + 1]
        remainders.append(image)
    remainders = [sum(pair) for pair in zip(remainders, more)] if more else remainders
    record = jnp.zeros(shape, F32)
    for b in range(basis):
        record = jnp.where(lane == b, projection[b], record)
    for j in range(VECS):
        pivot = columns[j][j : j + 1]
        scale = lax.rsqrt(pivot)
        lower = jnp.where(row > j, columns[j] * scale, 0.0)
        record = jnp.where(lane == basis + j, jnp.where(row == j, pivot * scale, lower), record)
        for u in range(j + 1, VECS):
            columns[u] = columns[u] - lower * lower[u : u + 1]
        for t, remainder in enumerate(remainders):
            solved = remainder[j : j + 1] * scale
            remainders[t] = jnp.where(row == j, solved, remainder - lower * solved)
    return remainders, record


def middle_kernel(
    trees,
    rows_all,
    arrived_ref,
    flat_ref,
    basis_ref,
    image_ref,
    window_coupled_ref,
    weights_ref,
    near_ref,
    choice_ref,
    u_ref,
    maps_ref,
    slots_ref,
    next_window_ref,
    near_part_ref,
    record_ref,
):
    own_tree = lax.axis_index("lvl")
    basis, size = next_window_ref.shape
    window = split_rows(basis_ref, basis)
    rank = u_ref.shape[0]
    lane = lanes_of((VECS, LANES))
    slots = arrived_ref.shape[0]
    leaves = slots // trees
    per_slot = flat_ref.shape[0] // slots
    per_row = size // LANES
    image_count = VECS * per_row
    rows = [
        flat_ref[pl.ds(per_slot * at + image_count + 2, 8, stride=per_slot), :]
        for at in range(0, slots, 8)
    ]
    total = jnp.sum(tree_sum(rows), axis=0, keepdims=True) * (1.0 / rows_all)
    first_tiles, other_tiles = [], []
    left = lanes_of((basis, LANES)) < LANES // 2
    for half in range(per_row):
        even, odd = (
            flat_ref[
                pl.ds(
                    per_slot * (2 * half + side) + image_count + 1,
                    basis,
                    stride=2 * per_row * per_slot,
                ),
                :,
            ]
            for side in range(2)
        )
        first_tiles.append(jnp.where(left, even, pltpu.roll(odd, LANES // 2, 1)))
        other_tiles.append(jnp.where(left, pltpu.roll(even, LANES // 2, 1), odd))
    own_slot = own_tree * leaves + lax.axis_index("clus")
    even_slot = lax.rem(own_slot, jnp.int32(2)) == 0
    low_tiles = [jnp.where(even_slot, a, b) for a, b in zip(first_tiles, other_tiles)]
    high_tiles = [jnp.where(even_slot, b, a) for a, b in zip(first_tiles, other_tiles)]

    def rows_of(place, start, count):
        at = [(start + row) * LANES for row in range(count)]
        return jnp.concatenate(
            [arrived_ref[place, 0:1, lane : lane + LANES] for lane in at], axis=0
        )

    low_place, _, high_place = near_places(leaves)
    coupled = couple_rows(
        jnp.concatenate(
            [rows_of(place, image_count, 1) for place in places_of(leaves, trees)], axis=0
        ),
        weights_ref,
    )
    images = [
        *row_groups(rows_of(low_place, 0, image_count)),
        *lane_tiles(image_ref[...]),
        *row_groups(rows_of(high_place, 0, image_count)),
        jnp.concatenate([coupled, jnp.zeros((VECS, LANES - rank), F32)], axis=1),
    ]
    windows = [
        *low_tiles,
        *lane_tiles(window),
        *high_tiles,
        window_coupled_ref[...],
    ]
    solved, record = orthogonalized(total, windows, images)
    record_ref[...] = record
    low_block, new_block, high_block = (
        jnp.concatenate(solved[at : at + per_row], axis=1)
        for at in range(0, 3 * per_row, per_row)
    )
    next_window = jnp.concatenate([window[VECS:], new_block], axis=0)
    next_window_ref[...] = next_window
    blocks = [block.astype(BF16) for block in (low_block, new_block, high_block)]
    near_part = near_field(blocks, choice_ref, near_ref)
    near_part_ref[...] = near_part
    far_part = jnp.dot(
        solved[-1][:, :rank].astype(BF16), u_ref[...], preferred_element_type=F32
    )
    skeleton, coarse = mapped(new_block.astype(BF16), maps_ref)
    width = LANES // VECS
    packed = one_row(product_lanes(next_window, near_part + far_part, width))
    tree_rows = jnp.concatenate([one_row(skeleton), packed], axis=0)
    level_rows = jnp.concatenate([one_row(coarse), packed], axis=0)

    def store(slot, at):
        slots_ref[slot] = level_rows

    over_slots(slots, store)

    def store_tree(leaf, at):
        slots_ref[own_tree * leaves + leaf] = tree_rows

    over_slots(leaves, store_tree)


def end_kernel(
    trees,
    rows_all,
    arrived_ref,
    flat_ref,
    window_ref,
    near_part_ref,
    weights_ref,
    u_ref,
    first_ref,
    block_ref,
    records_ref,
):
    leaves = arrived_ref.shape[0] // trees
    rows = jnp.concatenate(
        [arrived_ref[place, 0:1, :] for place in places_of(leaves, trees)], axis=0
    )
    coupled = couple_rows(rows, weights_ref)
    far_part = jnp.dot(coupled.astype(BF16), u_ref[...], preferred_element_type=F32)
    step = flat_ref.shape[0] // arrived_ref.shape[0] * VECS
    total = flat_ref[0:step]
    for at in range(step, flat_ref.shape[0], step):
        total = total + flat_ref[at : at + step]
    total = sum(total[at : at + 1] for at in range(1, step, step // VECS))
    total = total * (1.0 / rows_all)
    solved, record = orthogonalized(
        total,
        lane_tiles(window_ref[...]),
        lane_tiles(near_part_ref[...]),
        lane_tiles(far_part),
    )
    store_rows(block_ref, jnp.concatenate(solved, axis=1))
    used = records_ref.shape[2]
    records_ref[0] = first_ref[:, :used]
    records_ref[1] = record[:, :used]


def call(kernel, name, outs, ins, places, scratch=(), vmem=16 << 20, bytes_accessed=1 << 20):
    spaces = {"s": pltpu.SMEM, "v": pltpu.VMEM, "h": pltpu.HBM}
    return pl.pallas_call(
        kernel,
        name=name,
        out_shape=[jax.ShapeDtypeStruct(shape, dtype) for shape, dtype in outs],
        in_specs=[pl.BlockSpec(memory_space=spaces[place]) for place in places],
        out_specs=[pl.BlockSpec(memory_space=pltpu.VMEM)] * len(outs),
        scratch_shapes=list(scratch),
        cost_estimate=pl.CostEstimate(flops=0, bytes_accessed=bytes_accessed, transcendentals=0),
        compiler_params=pltpu.CompilerParams(vmem_limit_bytes=vmem),
    )(*ins)


def exchange(slots):
    return lax.all_to_all(slots, AXES, 0, 0, tiled=True)


def local(
    krylov_basis,
    near_block,
    near_col,
    near_count,
    far_col,
    v_basis,
    u_basis,
    far_coupling,
    transfer,
    top_coupling,
):
    basis, _, size = krylov_basis.shape
    trees = lax.axis_size("lvl")
    leaves = lax.axis_size("clus")
    devices = leaves * trees
    rows_all = float(devices * size)
    flat_basis = krylov_basis.reshape(-1, LANES)
    v_own, u_own, transfer_own = v_basis[0, 0], u_basis[0, 0], transfer[0, 0]
    rank = v_own.shape[0]
    far_own, top_own, near_own = far_coupling[0, 0], top_coupling[0, 0], near_block[0, 0]
    image_like = ((VECS, size), F32)
    window_like = ((basis, size), F32)
    per_slot = VECS * size // LANES + 3
    record_like = ((VECS, LANES), F32)
    maps_like = ((4 * rank, size), BF16)
    choice_like = ((-(-3 * near_own.shape[0] // 8) * 8, LANES), F32)
    weights_like = ((3, rank, (leaves + trees - 2) * LANES), BF16)
    (slots,) = call(
        functools.partial(begin_kernel, leaves),
        "begin",
        [((devices, VECS, size + 2 * LANES), BF16)],
        [flat_basis, v_own, transfer_own],
        "hhh",
        [
            pltpu.VMEM(flat_basis.shape, F32),
            pltpu.VMEM(v_own.shape, BF16),
            pltpu.VMEM(transfer_own.shape, F32),
            pltpu.SemaphoreType.DMA((3,)),
        ],
        vmem=None,
    )
    arrived = exchange(slots)
    weights, near_here, maps, choice = call(
        functools.partial(prepare_kernel, leaves),
        "prepare",
        [weights_like, (near_own.shape, BF16), maps_like, choice_like],
        [near_col, near_count, far_col, near_own, far_own, v_own, transfer_own, top_own],
        "ssshvvvv",
        [pltpu.SemaphoreType.DMA],
    )
    image, slots, window_coupled = call(
        functools.partial(first_kernel, trees),
        "first",
        [image_like, ((devices * per_slot, LANES), F32), ((basis, LANES), F32)],
        [
            arrived,
            flat_basis,
            weights,
            near_here,
            choice,
            u_own,
            maps,
        ],
        "v" * 7,
    )
    arrived = exchange(slots.reshape(devices, 1, per_slot * LANES))
    slots, window, near_part, record = call(
        functools.partial(middle_kernel, trees, rows_all),
        "middle",
        [((devices, 2, LANES), F32), window_like, image_like, record_like],
        [
            arrived,
            arrived.reshape(-1, LANES),
            flat_basis,
            image,
            window_coupled,
            weights,
            near_here,
            choice,
            u_own,
            maps,
        ],
        "v" * 10,
    )
    arrived = exchange(slots)
    block, records = call(
        functools.partial(end_kernel, trees, rows_all),
        "end",
        [((VECS * size // LANES, LANES), F32), ((STEPS, VECS, basis + VECS), F32)],
        [arrived, arrived.reshape(-1, LANES), window, near_part, weights, u_own, record],
        "v" * 7,
    )
    return (block.reshape(VECS, 1, size), jnp.transpose(records, (0, 2, 1)))


def solution(mesh):
    return jax.shard_map(
        local,
        mesh=mesh,
        in_specs=(
            P(None, "lvl", "clus"),
            P("lvl", "clus", None, None, None),
            P("lvl", "clus", None),
            P("lvl", "clus"),
            P("lvl", "clus", None),
            P("lvl", "clus", None, None),
            P("lvl", "clus", None, None),
            P("lvl", "clus", None, None, None),
            P("lvl", "clus", None, None),
            P("lvl", "clus", None, None, None),
        ),
        out_specs=(P(None, "lvl", "clus"), P()),
        check_vma=False,
    )
```

```python
import functools

import jax
import jax.numpy as jnp
from jax import lax
from jax.experimental import pallas as pl
from jax.experimental.pallas import tpu as pltpu
from jax.sharding import PartitionSpec as P

VECS = 4
STEPS = 2
LANES = 128
PIECE = 16
UNROLL = 32
AXES = ("lvl", "clus")

PRECISE = lax.Precision.HIGHEST
ROWS_DIMS = (((1,), (1,)), ((), ()))
F32, BF16 = jnp.float32, jnp.bfloat16


def rows_dot(left, right, precision=None):
    return lax.dot_general(
        left, right, ROWS_DIMS, precision=precision, preferred_element_type=F32
    )


def precise_dot(left, right):
    return jnp.dot(left, right, precision=PRECISE, preferred_element_type=F32)


def three_parts(values):
    high = values.astype(BF16)
    rest = values - high.astype(F32)
    middle = rest.astype(BF16)
    low = (rest - middle.astype(F32)).astype(BF16)
    return high, middle, low


def lane_parts(values, part):
    high = values.astype(BF16).astype(F32)
    rest = values - high
    middle = rest.astype(BF16).astype(F32)
    low = rest - middle
    return jnp.where(part == 0, high, jnp.where(part == 1, middle, jnp.where(part == 2, low, 0.0)))


def lanes_of(shape):
    return lax.broadcasted_iota(jnp.int32, shape, len(shape) - 1)


def over_slots(count, store):
    step = min(count, UNROLL)
    if count == step:
        for slot in range(count):
            store(slot, slot)
        return

    def body(at, carry):
        for inner in range(step):
            store(at * step + inner, inner)
        return carry

    lax.fori_loop(0, count // step, body, 0)


def split_rows(flat, rows):
    halves = flat.shape[0] // rows
    return jnp.concatenate(
        [flat[pl.ds(half, rows, stride=halves), :] for half in range(halves)], axis=1
    )


def store_rows(flat_ref, values):
    rows = values.shape[0]
    halves = flat_ref.shape[0] // rows
    for half in range(halves):
        flat_ref[pl.ds(half, rows, stride=halves), :] = values[:, half * LANES : (half + 1) * LANES]


def row_groups(rows):
    return [rows[at : at + VECS] for at in range(0, rows.shape[0], VECS)]


def lane_tiles(values):
    return [values[:, at : at + LANES] for at in range(0, values.shape[1], LANES)]


def replicated(column):
    return jnp.broadcast_to(column, (column.shape[0], LANES))


def lane_sum(pairs):
    return replicated(jnp.sum(sum(left * right for left, right in pairs), axis=1, keepdims=True))


def begin_kernel(leaves, basis_hbm, v_hbm, transfer_hbm, slots_ref, *scratch):
    basis_ref, v_ref, transfer_ref, sems = scratch
    copies = [
        pltpu.make_async_copy(source, target, sems.at[at])
        for at, (source, target) in enumerate(
            ((basis_hbm, basis_ref), (v_hbm, v_ref), (transfer_hbm, transfer_ref))
        )
    ]
    for copy in copies:
        copy.start()
    for copy in copies:
        copy.wait()
    rank, size = v_ref.shape
    basis = basis_ref.shape[0] * LANES // size
    window = split_rows(basis_ref, basis)
    current = window[basis - VECS :]
    lowered = current.astype(BF16)
    rest = current - lowered.astype(F32)
    parts = [lowered, *three_parts(window[: basis - VECS]), *three_parts(rest)[:2]]
    parts = jnp.concatenate([part.astype(F32) for part in parts], axis=0).astype(BF16)
    def summed(rows):
        rows = row_groups(rows)
        return jnp.concatenate(
            [rows[0], rows[1] + rows[2] + rows[3], rows[4] + rows[5]], axis=0
        )

    narrow = summed(rows_dot(parts, v_ref[...]))
    repeats = LANES // rank
    wide_basis = jnp.concatenate([v_ref[...]] * repeats, axis=0)
    skeletons = summed(rows_dot(parts, wide_basis))
    wide_transfer = jnp.concatenate([transfer_ref[...]] * repeats, axis=1)
    wide_transfer = jnp.concatenate(three_parts(wide_transfer), axis=1)
    narrow = jnp.concatenate([part.astype(F32) for part in three_parts(narrow)], axis=0)
    coarse = sum(lane_tiles(jnp.dot(narrow.astype(BF16), wide_transfer, preferred_element_type=F32)))
    count = skeletons.shape[0]
    coarse = coarse[:count] + coarse[count : 2 * count] + coarse[2 * count :]
    own_tree = lax.axis_index("lvl")

    def tails(values):
        exact, old, extra = row_groups(values)
        group = lanes_of((VECS, LANES)) // rank
        first = jnp.where(group < 3, lane_parts(exact, group), extra)
        return first.astype(BF16), lane_parts(old, group - (repeats - 2))

    tree_first, tree_second = tails(skeletons)
    level_first, level_second = tails(coarse)
    kept = lanes_of((VECS, LANES)) >= LANES - 2 * rank
    flat = basis_ref[...]
    turns = LANES // PIECE
    turned = [pltpu.roll(flat, LANES - PIECE * c, 1) if c else flat for c in range(turns)]
    part = lanes_of(flat.shape) // PIECE
    pieces = [
        lane_parts(
            jnp.where(
                part == 0, turned[c], jnp.where(part == 1, turned[c - 1], turned[c - 2])
            ),
            part,
        )
        for c in range(turns)
    ]

    def store(slot, at):
        row, side = at * VECS // turns % flat.shape[0], at * VECS % turns
        piece = [pieces[side + v][row : row + 1] for v in range(VECS)]
        same = lax.div(jnp.int32(slot), jnp.int32(leaves)) == own_tree
        second = jnp.where(same, tree_second, level_second)
        piece = jnp.where(kept, second, jnp.concatenate(piece, axis=0))
        slots_ref[slot, :, :size] = lowered
        slots_ref[slot, :, size : size + LANES] = level_first
        slots_ref[slot, :, size + LANES :] = piece.astype(BF16)

    over_slots(slots_ref.shape[0], store)

    def store_tree(leaf, at):
        slots_ref[own_tree * leaves + leaf, :, size : size + LANES] = tree_first

    over_slots(leaves, store_tree)


def prepare_kernel(
    leaves,
    near_col_ref,
    near_count_ref,
    far_col_ref,
    near_hbm,
    far_coupling_ref,
    v_ref,
    transfer_ref,
    top_ref,
    weights_ref,
    near_ref,
    maps_ref,
    choice_ref,
    sem,
):
    copy = pltpu.make_async_copy(near_hbm, near_ref, sem)
    copy.start()
    own_tree = lax.axis_index("lvl")
    far_slots = far_coupling_ref.shape[0]
    trees, rank = top_ref.shape[0], top_ref.shape[1]
    transfer = transfer_ref[...]
    own_leaf = lax.axis_index("clus")
    for slot in range(leaves + trees - 2):
        if slot < leaves - 1:
            leaf = lax.rem(own_leaf + 1 + slot, jnp.int32(leaves))
            block = jnp.zeros((rank, rank), F32)
            for at in range(far_slots):
                block = block + jnp.where(far_col_ref[0, 0, at] == leaf, far_coupling_ref[at], 0.0)
        else:
            tree = lax.rem(own_tree + 2 + slot - leaves, jnp.int32(trees))
            block = precise_dot(transfer, top_ref[tree])
        wide = jnp.concatenate([block] * (LANES // rank), axis=1)
        for part, piece in enumerate(three_parts(wide)):
            weights_ref[part, :, slot * LANES : (slot + 1) * LANES] = piece
    v_basis = v_ref[...]
    carried = precise_dot(transfer.T, v_basis.astype(F32))
    for part, piece in enumerate((v_basis, *three_parts(carried))):
        maps_ref[part * rank : (part + 1) * rank] = piece
    count = near_count_ref[0, 0]
    rows = lax.broadcasted_iota(jnp.int32, choice_ref.shape, 0)
    choice = jnp.zeros(choice_ref.shape, F32)
    for slot in range(near_ref.shape[0]):
        for side in range(3):
            wanted = (near_col_ref[0, 0, slot] == own_leaf + side - 1) & (slot < count)
            choice = jnp.where(rows == 3 * slot + side, jnp.where(wanted, 1.0, 0.0), choice)
    choice_ref[...] = choice
    copy.wait()


def places_of(leaves, trees):
    own_tree = lax.axis_index("lvl")
    own_leaf = lax.axis_index("clus")
    others = [lax.rem(own_leaf + 1 + at, jnp.int32(leaves)) for at in range(leaves - 1)]
    places = [own_tree * leaves + leaf for leaf in others]
    others = [lax.rem(own_tree + 1 + at, jnp.int32(trees)) for at in range(trees - 1)]
    return places + [tree * leaves + own_leaf for tree in others]


def near_places(leaves):
    start = lax.axis_index("lvl") * leaves
    own_leaf = lax.axis_index("clus")
    low = jnp.maximum(own_leaf - 1, 0)
    high = jnp.minimum(own_leaf + 1, leaves - 1)
    return [start + leaf for leaf in (low, own_leaf, high)]


def tree_sum(values):
    while len(values) > 1:
        values = [sum(values[at : at + 2]) for at in range(0, len(values), 2)]
    return values[0]


def near_field(blocks, choice_ref, near_ref):
    choice = choice_ref[...]
    blocks = [[tile.astype(F32) for tile in lane_tiles(block)] for block in blocks]
    parts = []
    for slot in range(near_ref.shape[0]):
        rows = [choice[3 * slot + side : 3 * slot + side + 1] for side in range(3)]
        tiles = [sum(tile * row for tile, row in zip(sides, rows)) for sides in zip(*blocks)]
        parts.append(rows_dot(jnp.concatenate(tiles, axis=1).astype(BF16), near_ref[slot]))
    return tree_sum(parts)


def couple(values, weights_ref):
    lowered = values.astype(BF16)
    return sum(rows_dot(lowered, weights_ref[part]) for part in range(3))


def product_lanes(window, image, period):
    basis = window.shape[0]
    window, image = lane_tiles(window), lane_tiles(image)
    lane = lanes_of((VECS, LANES)) % period
    packed = jnp.zeros((VECS, LANES), F32)
    for b in range(basis):
        product = lane_sum([(tile, other[b : b + 1]) for tile, other in zip(image, window)])
        packed = jnp.where(lane == b, product, packed)
    at = basis
    for u in range(VECS):
        product = lane_sum([(tile, tile[u : u + 1]) for tile in image])
        packed = jnp.where(lane == at + u, product, packed)
    at = at + VECS
    for b in range(basis):
        product = lane_sum([(tile, tile[b : b + 1]) for tile in window])
        for group in range(basis // VECS):
            rows = product[group * VECS : (group + 1) * VECS]
            packed = jnp.where(lane == at + group * basis + b, rows, packed)
    return packed


def couple_rows(rows, weights_ref):
    shape = (VECS, LANES)
    own = lanes_of(shape) // (LANES // VECS) == lax.broadcasted_iota(jnp.int32, shape, 0)
    parts = [
        jnp.concatenate(
            [jnp.where(own, part[at : at + 1], 0.0) for at in range(rows.shape[0])], axis=1
        )
        for part in (piece.astype(F32) for piece in three_parts(rows))
    ]
    return sum(row_groups(couple(jnp.concatenate(parts, axis=0), weights_ref)))


def one_row(values):
    width = LANES // VECS
    own = lanes_of(values.shape) // width == lax.broadcasted_iota(jnp.int32, values.shape, 0)
    return jnp.sum(jnp.where(own, values, 0.0), axis=0, keepdims=True)


def mapped(rows, maps_ref):
    products = sum(row_groups(rows_dot(rows, maps_ref[...])))
    rank = maps_ref.shape[0] // 4
    lane = lanes_of(products.shape) % rank
    spread = [
        jnp.take_along_axis(products, lane + part * rank, axis=1, mode="promise_in_bounds")
        for part in range(4)
    ]
    return spread[0], spread[1] + spread[2] + spread[3]


def first_kernel(
    trees,
    arrived_ref,
    basis_ref,
    weights_ref,
    near_ref,
    choice_ref,
    u_ref,
    maps_ref,
    image_ref,
    slots_ref,
    window_coupled_ref,
):
    own_tree = lax.axis_index("lvl")
    size = near_ref.shape[1]
    rank = u_ref.shape[0]
    leaves = arrived_ref.shape[0] // trees
    places = places_of(leaves, trees)
    first = [arrived_ref[place, :, size : size + LANES] for place in places]
    second = [arrived_ref[place, :, size + LANES :] for place in places]
    first = jnp.concatenate(first, axis=1).astype(F32)
    second = jnp.concatenate(second, axis=1).astype(F32)
    lane = lanes_of(first.shape) % LANES
    exact = jnp.where(lane < 3 * rank, first, 0.0)
    old = jnp.where(lane >= LANES - 2 * rank, second, 0.0)
    rows = couple(jnp.concatenate([exact, first, old], axis=0), weights_ref)
    linear = jnp.concatenate([rows[2 * VECS :], rows[VECS : 2 * VECS]], axis=0)
    blank = jnp.zeros((2 * VECS, LANES - rank), F32)
    window_coupled_ref[...] = jnp.concatenate([linear, blank], axis=1)
    image = jnp.dot(rows[:VECS].astype(BF16), u_ref[...], preferred_element_type=F32)
    blocks = [arrived_ref[place, :, :size] for place in near_places(leaves)]
    image = image + near_field(blocks, choice_ref, near_ref)
    image_ref[...] = image
    width = LANES // VECS
    packed = one_row(product_lanes(split_rows(basis_ref, window_coupled_ref.shape[0]), image, width))
    parts = [part.astype(F32) for part in three_parts(image)]
    skeleton, coarse = mapped(jnp.concatenate(parts, axis=0).astype(BF16), maps_ref)
    tree_row, level_row = one_row(skeleton), one_row(coarse)
    image_rows = jnp.concatenate(lane_tiles(image), axis=0)
    per_slot = image_rows.shape[0] + 3
    total = slots_ref.shape[0] // per_slot
    step = min(total, UNROLL)
    shape = (2 * VECS, LANES)
    lane = lanes_of(shape)
    row = lax.broadcasted_iota(jnp.int32, shape, 0)
    own = lane // PIECE % VECS == row % VECS

    def fill(part_ref, start):
        for inner in range(0, step, 2):
            sides = []
            for shift in (-1, 1):
                near = [start + inner + at + shift for at in range(2)]
                if isinstance(start, int):
                    near = [min(max(slot, 0), total - 1) for slot in near]
                else:
                    near = [jnp.clip(slot, 0, total - 1) for slot in near]
                near = [arrived_ref[slot, :, size + LANES :].astype(F32) for slot in near]
                sides.append(jnp.concatenate(near, axis=0))
            both = jnp.where(lane < LANES // 2, sides[0], pltpu.roll(sides[1], LANES // 2, 1))
            both = (
                both
                + pltpu.roll(both, LANES - PIECE, 1)
                + pltpu.roll(both, LANES - 2 * PIECE, 1)
            )
            both = jnp.where(own, pltpu.roll(both, 0, 1, stride=PIECE, stride_axis=0), 0.0)
            for at in range(2):
                relay = jnp.sum(both[at * VECS : (at + 1) * VECS], axis=0, keepdims=True)
                slot = jnp.int32(start + inner + at)
                same = lax.div(slot, jnp.int32(leaves)) == own_tree
                far = jnp.where(same, tree_row, level_row)
                first_row = (inner + at) * per_slot
                part_ref[first_row : first_row + per_slot] = jnp.concatenate(
                    [image_rows, far, relay, packed], axis=0
                )

    if total == step:
        fill(slots_ref, 0)
    else:

        def body(at, carry):
            start = pl.multiple_of(at * (step * per_slot), 8)
            fill(slots_ref.at[pl.ds(start, step * per_slot)], at * step)
            return carry

        lax.fori_loop(0, total // step, body, 0)


def orthogonalized(total, windows, images, more=()):
    basis = windows[0].shape[0]
    shape = (VECS, LANES)
    row, lane = lax.broadcasted_iota(jnp.int32, shape, 0), lanes_of(shape)
    total = jnp.broadcast_to(total, shape)

    def column_of(at):
        places = row * (LANES // VECS) + at
        return jnp.take_along_axis(total, places, axis=1, mode="promise_in_bounds")

    projection = [column_of(b) for b in range(basis)]
    square = [column_of(basis + u) for u in range(VECS)]
    start = basis + VECS
    inner = []
    for other in range(basis):
        value = -2.0 * projection[other]
        for group in range(basis // VECS):
            metric = column_of(start + group * basis + other)
            for v in range(VECS):
                value = value + projection[group * VECS + v] * metric[v : v + 1]
        inner.append(value)
    columns = []
    for u in range(VECS):
        value = square[u]
        for b in range(basis):
            value = value + inner[b] * projection[b][u : u + 1]
        columns.append(value)
    remainders = []
    for window, image in zip(windows, images):
        for b in range(basis):
            image = image - projection[b] * window[b : b + 1]
        remainders.append(image)
    remainders = [sum(pair) for pair in zip(remainders, more)] if more else remainders
    record = jnp.zeros(shape, F32)
    for b in range(basis):
        record = jnp.where(lane == b, projection[b], record)
    for j in range(VECS):
        pivot = columns[j][j : j + 1]
        scale = lax.rsqrt(pivot)
        lower = jnp.where(row > j, columns[j] * scale, 0.0)
        record = jnp.where(lane == basis + j, jnp.where(row == j, pivot * scale, lower), record)
        for u in range(j + 1, VECS):
            columns[u] = columns[u] - lower * lower[u : u + 1]
        for t, remainder in enumerate(remainders):
            solved = remainder[j : j + 1] * scale
            remainders[t] = jnp.where(row == j, solved, remainder - lower * solved)
    return remainders, record


def middle_kernel(
    trees,
    rows_all,
    arrived_ref,
    flat_ref,
    basis_ref,
    image_ref,
    window_coupled_ref,
    weights_ref,
    near_ref,
    choice_ref,
    u_ref,
    maps_ref,
    slots_ref,
    next_window_ref,
    near_part_ref,
    record_ref,
):
    own_tree = lax.axis_index("lvl")
    basis, size = next_window_ref.shape
    window = split_rows(basis_ref, basis)
    rank = u_ref.shape[0]
    lane = lanes_of((VECS, LANES))
    slots = arrived_ref.shape[0]
    leaves = slots // trees
    per_slot = flat_ref.shape[0] // slots
    per_row = size // LANES
    image_count = VECS * per_row
    rows = [
        flat_ref[pl.ds(per_slot * at + image_count + 2, 8, stride=per_slot), :]
        for at in range(0, slots, 8)
    ]
    total = jnp.sum(tree_sum(rows), axis=0, keepdims=True) * (1.0 / rows_all)
    first_tiles, other_tiles = [], []
    left = lanes_of((basis, LANES)) < LANES // 2
    for half in range(per_row):
        even, odd = (
            flat_ref[
                pl.ds(
                    per_slot * (2 * half + side) + image_count + 1,
                    basis,
                    stride=2 * per_row * per_slot,
                ),
                :,
            ]
            for side in range(2)
        )
        first_tiles.append(jnp.where(left, even, pltpu.roll(odd, LANES // 2, 1)))
        other_tiles.append(jnp.where(left, pltpu.roll(even, LANES // 2, 1), odd))
    own_slot = own_tree * leaves + lax.axis_index("clus")
    even_slot = lax.rem(own_slot, jnp.int32(2)) == 0
    low_tiles = [jnp.where(even_slot, a, b) for a, b in zip(first_tiles, other_tiles)]
    high_tiles = [jnp.where(even_slot, b, a) for a, b in zip(first_tiles, other_tiles)]

    def rows_of(place, start, count):
        at = [(start + row) * LANES for row in range(count)]
        return jnp.concatenate(
            [arrived_ref[place, 0:1, lane : lane + LANES] for lane in at], axis=0
        )

    low_place, _, high_place = near_places(leaves)
    coupled = couple_rows(
        jnp.concatenate(
            [rows_of(place, image_count, 1) for place in places_of(leaves, trees)], axis=0
        ),
        weights_ref,
    )
    images = [
        *row_groups(rows_of(low_place, 0, image_count)),
        *lane_tiles(image_ref[...]),
        *row_groups(rows_of(high_place, 0, image_count)),
        jnp.concatenate([coupled, jnp.zeros((VECS, LANES - rank), F32)], axis=1),
    ]
    windows = [
        *low_tiles,
        *lane_tiles(window),
        *high_tiles,
        window_coupled_ref[...],
    ]
    solved, record = orthogonalized(total, windows, images)
    record_ref[...] = record
    low_block, new_block, high_block = (
        jnp.concatenate(solved[at : at + per_row], axis=1)
        for at in range(0, 3 * per_row, per_row)
    )
    next_window = jnp.concatenate([window[VECS:], new_block], axis=0)
    next_window_ref[...] = next_window
    blocks = [block.astype(BF16) for block in (low_block, new_block, high_block)]
    near_part = near_field(blocks, choice_ref, near_ref)
    near_part_ref[...] = near_part
    far_part = jnp.dot(
        solved[-1][:, :rank].astype(BF16), u_ref[...], preferred_element_type=F32
    )
    skeleton, coarse = mapped(new_block.astype(BF16), maps_ref)
    width = LANES // VECS
    packed = one_row(product_lanes(next_window, near_part + far_part, width))
    tree_rows = jnp.concatenate([one_row(skeleton), packed], axis=0)
    level_rows = jnp.concatenate([one_row(coarse), packed], axis=0)

    def store(slot, at):
        slots_ref[slot] = level_rows

    over_slots(slots, store)

    def store_tree(leaf, at):
        slots_ref[own_tree * leaves + leaf] = tree_rows

    over_slots(leaves, store_tree)


def end_kernel(
    trees,
    rows_all,
    arrived_ref,
    flat_ref,
    window_ref,
    near_part_ref,
    weights_ref,
    u_ref,
    first_ref,
    block_ref,
    records_ref,
):
    leaves = arrived_ref.shape[0] // trees
    rows = jnp.concatenate(
        [arrived_ref[place, 0:1, :] for place in places_of(leaves, trees)], axis=0
    )
    coupled = couple_rows(rows, weights_ref)
    far_part = jnp.dot(coupled.astype(BF16), u_ref[...], preferred_element_type=F32)
    step = flat_ref.shape[0] // arrived_ref.shape[0] * VECS
    total = flat_ref[0:step]
    for at in range(step, flat_ref.shape[0], step):
        total = total + flat_ref[at : at + step]
    total = sum(total[at : at + 1] for at in range(1, step, step // VECS))
    total = total * (1.0 / rows_all)
    solved, record = orthogonalized(
        total,
        lane_tiles(window_ref[...]),
        lane_tiles(near_part_ref[...]),
        lane_tiles(far_part),
    )
    store_rows(block_ref, jnp.concatenate(solved, axis=1))
    used = records_ref.shape[2]
    records_ref[0] = first_ref[:, :used]
    records_ref[1] = record[:, :used]


def call(kernel, name, outs, ins, places, scratch=(), vmem=16 << 20, bytes_accessed=1 << 20):
    spaces = {"s": pltpu.SMEM, "v": pltpu.VMEM, "h": pltpu.HBM}
    return pl.pallas_call(
        kernel,
        name=name,
        out_shape=[jax.ShapeDtypeStruct(shape, dtype) for shape, dtype in outs],
        in_specs=[pl.BlockSpec(memory_space=spaces[place]) for place in places],
        out_specs=[pl.BlockSpec(memory_space=pltpu.VMEM)] * len(outs),
        scratch_shapes=list(scratch),
        cost_estimate=pl.CostEstimate(flops=0, bytes_accessed=bytes_accessed, transcendentals=0),
        compiler_params=pltpu.CompilerParams(vmem_limit_bytes=vmem),
    )(*ins)


def exchange(slots):
    return lax.all_to_all(slots, AXES, 0, 0, tiled=True)


def local(
    krylov_basis,
    near_block,
    near_col,
    near_count,
    far_col,
    v_basis,
    u_basis,
    far_coupling,
    transfer,
    top_coupling,
):
    basis, _, size = krylov_basis.shape
    trees = lax.axis_size("lvl")
    leaves = lax.axis_size("clus")
    devices = leaves * trees
    rows_all = float(devices * size)
    flat_basis = krylov_basis.reshape(-1, LANES)
    v_own, u_own, transfer_own = v_basis[0, 0], u_basis[0, 0], transfer[0, 0]
    rank = v_own.shape[0]
    far_own, top_own, near_own = far_coupling[0, 0], top_coupling[0, 0], near_block[0, 0]
    image_like = ((VECS, size), F32)
    window_like = ((basis, size), F32)
    per_slot = VECS * size // LANES + 3
    record_like = ((VECS, LANES), F32)
    maps_like = ((4 * rank, size), BF16)
    choice_like = ((-(-3 * near_own.shape[0] // 8) * 8, LANES), F32)
    weights_like = ((3, rank, (leaves + trees - 2) * LANES), BF16)
    (slots,) = call(
        functools.partial(begin_kernel, leaves),
        "begin",
        [((devices, VECS, size + 2 * LANES), BF16)],
        [flat_basis, v_own, transfer_own],
        "hhh",
        [
            pltpu.VMEM(flat_basis.shape, F32),
            pltpu.VMEM(v_own.shape, BF16),
            pltpu.VMEM(transfer_own.shape, F32),
            pltpu.SemaphoreType.DMA((3,)),
        ],
        vmem=None,
    )
    arrived = exchange(slots)
    weights, near_here, maps, choice = call(
        functools.partial(prepare_kernel, leaves),
        "prepare",
        [weights_like, (near_own.shape, BF16), maps_like, choice_like],
        [near_col, near_count, far_col, near_own, far_own, v_own, transfer_own, top_own],
        "ssshvvvv",
        [pltpu.SemaphoreType.DMA],
    )
    image, slots, window_coupled = call(
        functools.partial(first_kernel, trees),
        "first",
        [image_like, ((devices * per_slot, LANES), F32), ((basis, LANES), F32)],
        [
            arrived,
            flat_basis,
            weights,
            near_here,
            choice,
            u_own,
            maps,
        ],
        "v" * 7,
    )
    arrived = exchange(slots.reshape(devices, 1, per_slot * LANES))
    slots, window, near_part, record = call(
        functools.partial(middle_kernel, trees, rows_all),
        "middle",
        [((devices, 2, LANES), F32), window_like, image_like, record_like],
        [
            arrived,
            arrived.reshape(-1, LANES),
            flat_basis,
            image,
            window_coupled,
            weights,
            near_here,
            choice,
            u_own,
            maps,
        ],
        "v" * 10,
    )
    arrived = exchange(slots)
    block, records = call(
        functools.partial(end_kernel, trees, rows_all),
        "end",
        [((VECS * size // LANES, LANES), F32), ((STEPS, VECS, basis + VECS), F32)],
        [arrived, arrived.reshape(-1, LANES), window, near_part, weights, u_own, record],
        "v" * 7,
    )
    return (block.reshape(VECS, 1, size), jnp.transpose(records, (0, 2, 1)))


def solution(mesh):
    return jax.shard_map(
        local,
        mesh=mesh,
        in_specs=(
            P(None, "lvl", "clus"),
            P("lvl", "clus", None, None, None),
            P("lvl", "clus", None),
            P("lvl", "clus"),
            P("lvl", "clus", None),
            P("lvl", "clus", None, None),
            P("lvl", "clus", None, None),
            P("lvl", "clus", None, None, None),
            P("lvl", "clus", None, None),
            P("lvl", "clus", None, None, None),
        ),
        out_specs=(P(None, "lvl", "clus"), P()),
        check_vma=False,
    )
```

```python
import functools

import jax
import jax.numpy as jnp
from jax import lax
from jax.experimental import pallas as pl
from jax.experimental.pallas import tpu as pltpu
from jax.sharding import PartitionSpec as P

VECS = 4
STEPS = 2
LANES = 128
PIECE = 16
UNROLL = 32
AXES = ("lvl", "clus")

PRECISE = lax.Precision.HIGHEST
ROWS_DIMS = (((1,), (1,)), ((), ()))
F32, BF16 = jnp.float32, jnp.bfloat16


def rows_dot(left, right, precision=None):
    return lax.dot_general(
        left, right, ROWS_DIMS, precision=precision, preferred_element_type=F32
    )


def precise_dot(left, right):
    return jnp.dot(left, right, precision=PRECISE, preferred_element_type=F32)


def three_parts(values):
    high = values.astype(BF16)
    rest = values - high.astype(F32)
    middle = rest.astype(BF16)
    low = (rest - middle.astype(F32)).astype(BF16)
    return high, middle, low


def lane_parts(values, part):
    high = values.astype(BF16).astype(F32)
    rest = values - high
    middle = rest.astype(BF16).astype(F32)
    low = rest - middle
    return jnp.where(part == 0, high, jnp.where(part == 1, middle, jnp.where(part == 2, low, 0.0)))


def lanes_of(shape):
    return lax.broadcasted_iota(jnp.int32, shape, len(shape) - 1)


def over_slots(count, store):
    step = min(count, UNROLL)
    if count == step:
        for slot in range(count):
            store(slot, slot)
        return

    def body(at, carry):
        for inner in range(step):
            store(at * step + inner, inner)
        return carry

    lax.fori_loop(0, count // step, body, 0)


def split_rows(flat, rows):
    halves = flat.shape[0] // rows
    return jnp.concatenate(
        [flat[pl.ds(half, rows, stride=halves), :] for half in range(halves)], axis=1
    )


def store_rows(flat_ref, values):
    rows = values.shape[0]
    halves = flat_ref.shape[0] // rows
    for half in range(halves):
        flat_ref[pl.ds(half, rows, stride=halves), :] = values[:, half * LANES : (half + 1) * LANES]


def row_groups(rows):
    return [rows[at : at + VECS] for at in range(0, rows.shape[0], VECS)]


def lane_tiles(values):
    return [values[:, at : at + LANES] for at in range(0, values.shape[1], LANES)]


def replicated(column):
    return jnp.broadcast_to(column, (column.shape[0], LANES))


def lane_sum(pairs):
    return replicated(jnp.sum(sum(left * right for left, right in pairs), axis=1, keepdims=True))


def begin_kernel(leaves, basis_hbm, v_hbm, transfer_hbm, slots_ref, *scratch):
    basis_ref, v_ref, transfer_ref, sems = scratch
    copies = [
        pltpu.make_async_copy(source, target, sems.at[at])
        for at, (source, target) in enumerate(
            ((basis_hbm, basis_ref), (v_hbm, v_ref), (transfer_hbm, transfer_ref))
        )
    ]
    for copy in copies:
        copy.start()
    for copy in copies:
        copy.wait()
    rank, size = v_ref.shape
    basis = basis_ref.shape[0] * LANES // size
    window = split_rows(basis_ref, basis)
    current = window[basis - VECS :]
    lowered = current.astype(BF16)
    rest = current - lowered.astype(F32)
    parts = [lowered, *three_parts(window[: basis - VECS]), *three_parts(rest)[:2]]
    parts = jnp.concatenate([part.astype(F32) for part in parts], axis=0).astype(BF16)
    def summed(rows):
        rows = row_groups(rows)
        return jnp.concatenate(
            [rows[0], rows[1] + rows[2] + rows[3], rows[4] + rows[5]], axis=0
        )

    narrow = summed(rows_dot(parts, v_ref[...]))
    repeats = LANES // rank
    wide_basis = jnp.concatenate([v_ref[...]] * repeats, axis=0)
    skeletons = summed(rows_dot(parts, wide_basis))
    wide_transfer = jnp.concatenate([transfer_ref[...]] * repeats, axis=1)
    wide_transfer = jnp.concatenate(three_parts(wide_transfer), axis=1)
    narrow = jnp.concatenate([part.astype(F32) for part in three_parts(narrow)], axis=0)
    coarse = sum(lane_tiles(jnp.dot(narrow.astype(BF16), wide_transfer, preferred_element_type=F32)))
    count = skeletons.shape[0]
    coarse = coarse[:count] + coarse[count : 2 * count] + coarse[2 * count :]
    own_tree = lax.axis_index("lvl")

    def tails(values):
        exact, old, extra = row_groups(values)
        group = lanes_of((VECS, LANES)) // rank
        first = jnp.where(group < 3, lane_parts(exact, group), extra)
        return first.astype(BF16), lane_parts(old, group - (repeats - 2))

    tree_first, tree_second = tails(skeletons)
    level_first, level_second = tails(coarse)
    kept = lanes_of((VECS, LANES)) >= LANES - 2 * rank
    flat = basis_ref[...]
    turns = LANES // PIECE
    turned = [pltpu.roll(flat, LANES - PIECE * c, 1) if c else flat for c in range(turns)]
    part = lanes_of(flat.shape) // PIECE
    pieces = [
        lane_parts(
            jnp.where(
                part == 0, turned[c], jnp.where(part == 1, turned[c - 1], turned[c - 2])
            ),
            part,
        )
        for c in range(turns)
    ]

    def store(slot, at):
        row, side = at * VECS // turns % flat.shape[0], at * VECS % turns
        piece = [pieces[side + v][row : row + 1] for v in range(VECS)]
        same = lax.div(jnp.int32(slot), jnp.int32(leaves)) == own_tree
        second = jnp.where(same, tree_second, level_second)
        piece = jnp.where(kept, second, jnp.concatenate(piece, axis=0))
        slots_ref[slot, :, :size] = lowered
        slots_ref[slot, :, size : size + LANES] = level_first
        slots_ref[slot, :, size + LANES :] = piece.astype(BF16)

    over_slots(slots_ref.shape[0], store)

    def store_tree(leaf, at):
        slots_ref[own_tree * leaves + leaf, :, size : size + LANES] = tree_first

    over_slots(leaves, store_tree)


def prepare_kernel(
    leaves,
    near_col_ref,
    near_count_ref,
    far_col_ref,
    near_hbm,
    far_coupling_ref,
    v_ref,
    transfer_ref,
    top_ref,
    weights_ref,
    near_ref,
    maps_ref,
    choice_ref,
    sem,
):
    copy = pltpu.make_async_copy(near_hbm, near_ref, sem)
    copy.start()
    own_tree = lax.axis_index("lvl")
    far_slots = far_coupling_ref.shape[0]
    trees, rank = top_ref.shape[0], top_ref.shape[1]
    transfer = transfer_ref[...]
    own_leaf = lax.axis_index("clus")
    for slot in range(leaves + trees - 2):
        if slot < leaves - 1:
            leaf = lax.rem(own_leaf + 1 + slot, jnp.int32(leaves))
            block = jnp.zeros((rank, rank), F32)
            for at in range(far_slots):
                block = block + jnp.where(far_col_ref[0, 0, at] == leaf, far_coupling_ref[at], 0.0)
        else:
            tree = lax.rem(own_tree + 2 + slot - leaves, jnp.int32(trees))
            block = precise_dot(transfer, top_ref[tree])
        wide = jnp.concatenate([block] * (LANES // rank), axis=1)
        for part, piece in enumerate(three_parts(wide)):
            weights_ref[part, :, slot * LANES : (slot + 1) * LANES] = piece
    v_basis = v_ref[...]
    carried = precise_dot(transfer.T, v_basis.astype(F32))
    for part, piece in enumerate((v_basis, *three_parts(carried))):
        maps_ref[part * rank : (part + 1) * rank] = piece
    count = near_count_ref[0, 0]
    rows = lax.broadcasted_iota(jnp.int32, choice_ref.shape, 0)
    choice = jnp.zeros(choice_ref.shape, F32)
    for slot in range(near_ref.shape[0]):
        for side in range(3):
            wanted = (near_col_ref[0, 0, slot] == own_leaf + side - 1) & (slot < count)
            choice = jnp.where(rows == 3 * slot + side, jnp.where(wanted, 1.0, 0.0), choice)
    choice_ref[...] = choice
    copy.wait()


def places_of(leaves, trees):
    own_tree = lax.axis_index("lvl")
    own_leaf = lax.axis_index("clus")
    others = [lax.rem(own_leaf + 1 + at, jnp.int32(leaves)) for at in range(leaves - 1)]
    places = [own_tree * leaves + leaf for leaf in others]
    others = [lax.rem(own_tree + 1 + at, jnp.int32(trees)) for at in range(trees - 1)]
    return places + [tree * leaves + own_leaf for tree in others]


def near_places(leaves):
    start = lax.axis_index("lvl") * leaves
    own_leaf = lax.axis_index("clus")
    low = jnp.maximum(own_leaf - 1, 0)
    high = jnp.minimum(own_leaf + 1, leaves - 1)
    return [start + leaf for leaf in (low, own_leaf, high)]


def tree_sum(values):
    while len(values) > 1:
        values = [sum(values[at : at + 2]) for at in range(0, len(values), 2)]
    return values[0]


def near_field(blocks, choice_ref, near_ref):
    choice = choice_ref[...]
    low, own, high = blocks
    parts = [rows_dot(own, near_ref[0])]
    low, high = ([tile.astype(F32) for tile in lane_tiles(block)] for block in (low, high))
    for slot in range(1, near_ref.shape[0]):
        rows = [choice[3 * slot + side : 3 * slot + side + 1] for side in (0, 2)]
        tiles = [before * rows[0] + after * rows[1] for before, after in zip(low, high)]
        parts.append(rows_dot(jnp.concatenate(tiles, axis=1).astype(BF16), near_ref[slot]))
    return tree_sum(parts)


def couple(values, weights_ref):
    lowered = values.astype(BF16)
    return sum(rows_dot(lowered, weights_ref[part]) for part in range(3))


def product_lanes(window, image, period):
    basis = window.shape[0]
    window, image = lane_tiles(window), lane_tiles(image)
    lane = lanes_of((VECS, LANES)) % period
    packed = jnp.zeros((VECS, LANES), F32)
    for b in range(basis):
        product = lane_sum([(tile, other[b : b + 1]) for tile, other in zip(image, window)])
        packed = jnp.where(lane == b, product, packed)
    at = basis
    for u in range(VECS):
        product = lane_sum([(tile, tile[u : u + 1]) for tile in image])
        packed = jnp.where(lane == at + u, product, packed)
    at = at + VECS
    for b in range(basis):
        product = lane_sum([(tile, tile[b : b + 1]) for tile in window])
        for group in range(basis // VECS):
            rows = product[group * VECS : (group + 1) * VECS]
            packed = jnp.where(lane == at + group * basis + b, rows, packed)
    return packed


def couple_rows(rows, weights_ref):
    shape = (VECS, LANES)
    own = lanes_of(shape) // (LANES // VECS) == lax.broadcasted_iota(jnp.int32, shape, 0)
    parts = [
        jnp.concatenate(
            [jnp.where(own, part[at : at + 1], 0.0) for at in range(rows.shape[0])], axis=1
        )
        for part in (piece.astype(F32) for piece in three_parts(rows))
    ]
    return sum(row_groups(couple(jnp.concatenate(parts, axis=0), weights_ref)))


def one_row(values):
    width = LANES // VECS
    own = lanes_of(values.shape) // width == lax.broadcasted_iota(jnp.int32, values.shape, 0)
    return jnp.sum(jnp.where(own, values, 0.0), axis=0, keepdims=True)


def mapped(rows, maps_ref):
    products = sum(row_groups(rows_dot(rows, maps_ref[...])))
    rank = maps_ref.shape[0] // 4
    lane = lanes_of(products.shape) % rank
    spread = [
        jnp.take_along_axis(products, lane + part * rank, axis=1, mode="promise_in_bounds")
        for part in range(4)
    ]
    return spread[0], spread[1] + spread[2] + spread[3]


def first_kernel(
    trees,
    arrived_ref,
    basis_ref,
    weights_ref,
    near_ref,
    choice_ref,
    u_ref,
    maps_ref,
    image_ref,
    slots_ref,
    window_coupled_ref,
):
    own_tree = lax.axis_index("lvl")
    size = near_ref.shape[1]
    rank = u_ref.shape[0]
    leaves = arrived_ref.shape[0] // trees
    places = places_of(leaves, trees)
    first = [arrived_ref[place, :, size : size + LANES] for place in places]
    second = [arrived_ref[place, :, size + LANES :] for place in places]
    first = jnp.concatenate(first, axis=1).astype(F32)
    second = jnp.concatenate(second, axis=1).astype(F32)
    lane = lanes_of(first.shape) % LANES
    exact = jnp.where(lane < 3 * rank, first, 0.0)
    old = jnp.where(lane >= LANES - 2 * rank, second, 0.0)
    rows = couple(jnp.concatenate([exact, first, old], axis=0), weights_ref)
    linear = jnp.concatenate([rows[2 * VECS :], rows[VECS : 2 * VECS]], axis=0)
    blank = jnp.zeros((2 * VECS, LANES - rank), F32)
    window_coupled_ref[...] = jnp.concatenate([linear, blank], axis=1)
    image = jnp.dot(rows[:VECS].astype(BF16), u_ref[...], preferred_element_type=F32)
    blocks = [arrived_ref[place, :, :size] for place in near_places(leaves)]
    image = image + near_field(blocks, choice_ref, near_ref)
    image_ref[...] = image
    width = LANES // VECS
    packed = one_row(product_lanes(split_rows(basis_ref, window_coupled_ref.shape[0]), image, width))
    parts = [part.astype(F32) for part in three_parts(image)]
    skeleton, coarse = mapped(jnp.concatenate(parts, axis=0).astype(BF16), maps_ref)
    tree_row, level_row = one_row(skeleton), one_row(coarse)
    image_rows = jnp.concatenate(lane_tiles(image), axis=0)
    per_slot = image_rows.shape[0] + 3
    total = slots_ref.shape[0] // per_slot
    step = min(total, UNROLL)
    shape = (2 * VECS, LANES)
    lane = lanes_of(shape)
    row = lax.broadcasted_iota(jnp.int32, shape, 0)
    own = lane // PIECE % VECS == row % VECS

    def fill(part_ref, start):
        for inner in range(0, step, 2):
            sides = []
            for shift in (-1, 1):
                near = [start + inner + at + shift for at in range(2)]
                if isinstance(start, int):
                    near = [min(max(slot, 0), total - 1) for slot in near]
                else:
                    near = [jnp.clip(slot, 0, total - 1) for slot in near]
                near = [arrived_ref[slot, :, size + LANES :].astype(F32) for slot in near]
                sides.append(jnp.concatenate(near, axis=0))
            both = jnp.where(lane < LANES // 2, sides[0], pltpu.roll(sides[1], LANES // 2, 1))
            both = (
                both
                + pltpu.roll(both, LANES - PIECE, 1)
                + pltpu.roll(both, LANES - 2 * PIECE, 1)
            )
            both = jnp.where(own, pltpu.roll(both, 0, 1, stride=PIECE, stride_axis=0), 0.0)
            for at in range(2):
                relay = jnp.sum(both[at * VECS : (at + 1) * VECS], axis=0, keepdims=True)
                slot = jnp.int32(start + inner + at)
                same = lax.div(slot, jnp.int32(leaves)) == own_tree
                far = jnp.where(same, tree_row, level_row)
                first_row = (inner + at) * per_slot
                part_ref[first_row : first_row + per_slot] = jnp.concatenate(
                    [image_rows, far, relay, packed], axis=0
                )

    if total == step:
        fill(slots_ref, 0)
    else:

        def body(at, carry):
            start = pl.multiple_of(at * (step * per_slot), 8)
            fill(slots_ref.at[pl.ds(start, step * per_slot)], at * step)
            return carry

        lax.fori_loop(0, total // step, body, 0)


def orthogonalized(total, windows, images, more=()):
    basis = windows[0].shape[0]
    shape = (VECS, LANES)
    row, lane = lax.broadcasted_iota(jnp.int32, shape, 0), lanes_of(shape)
    total = jnp.broadcast_to(total, shape)

    def column_of(at):
        places = row * (LANES // VECS) + at
        return jnp.take_along_axis(total, places, axis=1, mode="promise_in_bounds")

    projection = [column_of(b) for b in range(basis)]
    square = [column_of(basis + u) for u in range(VECS)]
    start = basis + VECS
    inner = []
    for other in range(basis):
        value = -2.0 * projection[other]
        for group in range(basis // VECS):
            metric = column_of(start + group * basis + other)
            for v in range(VECS):
                value = value + projection[group * VECS + v] * metric[v : v + 1]
        inner.append(value)
    columns = []
    for u in range(VECS):
        value = square[u]
        for b in range(basis):
            value = value + inner[b] * projection[b][u : u + 1]
        columns.append(value)
    remainders = []
    for window, image in zip(windows, images):
        for b in range(basis):
            image = image - projection[b] * window[b : b + 1]
        remainders.append(image)
    remainders = [sum(pair) for pair in zip(remainders, more)] if more else remainders
    record = jnp.zeros(shape, F32)
    for b in range(basis):
        record = jnp.where(lane == b, projection[b], record)
    for j in range(VECS):
        pivot = columns[j][j : j + 1]
        scale = lax.rsqrt(pivot)
        lower = jnp.where(row > j, columns[j] * scale, 0.0)
        record = jnp.where(lane == basis + j, jnp.where(row == j, pivot * scale, lower), record)
        for u in range(j + 1, VECS):
            columns[u] = columns[u] - lower * lower[u : u + 1]
        for t, remainder in enumerate(remainders):
            solved = remainder[j : j + 1] * scale
            remainders[t] = jnp.where(row == j, solved, remainder - lower * solved)
    return remainders, record


def middle_kernel(
    trees,
    rows_all,
    arrived_ref,
    flat_ref,
    basis_ref,
    image_ref,
    window_coupled_ref,
    weights_ref,
    near_ref,
    choice_ref,
    u_ref,
    maps_ref,
    slots_ref,
    next_window_ref,
    near_part_ref,
    record_ref,
):
    own_tree = lax.axis_index("lvl")
    basis, size = next_window_ref.shape
    window = split_rows(basis_ref, basis)
    rank = u_ref.shape[0]
    lane = lanes_of((VECS, LANES))
    slots = arrived_ref.shape[0]
    leaves = slots // trees
    per_slot = flat_ref.shape[0] // slots
    per_row = size // LANES
    image_count = VECS * per_row
    rows = [
        flat_ref[pl.ds(per_slot * at + image_count + 2, 8, stride=per_slot), :]
        for at in range(0, slots, 8)
    ]
    total = jnp.sum(tree_sum(rows), axis=0, keepdims=True) * (1.0 / rows_all)
    first_tiles, other_tiles = [], []
    left = lanes_of((basis, LANES)) < LANES // 2
    for half in range(per_row):
        even, odd = (
            flat_ref[
                pl.ds(
                    per_slot * (2 * half + side) + image_count + 1,
                    basis,
                    stride=2 * per_row * per_slot,
                ),
                :,
            ]
            for side in range(2)
        )
        first_tiles.append(jnp.where(left, even, pltpu.roll(odd, LANES // 2, 1)))
        other_tiles.append(jnp.where(left, pltpu.roll(even, LANES // 2, 1), odd))
    own_slot = own_tree * leaves + lax.axis_index("clus")
    even_slot = lax.rem(own_slot, jnp.int32(2)) == 0
    low_tiles = [jnp.where(even_slot, a, b) for a, b in zip(first_tiles, other_tiles)]
    high_tiles = [jnp.where(even_slot, b, a) for a, b in zip(first_tiles, other_tiles)]

    def rows_of(place, start, count):
        at = [(start + row) * LANES for row in range(count)]
        return jnp.concatenate(
            [arrived_ref[place, 0:1, lane : lane + LANES] for lane in at], axis=0
        )

    low_place, _, high_place = near_places(leaves)
    coupled = couple_rows(
        jnp.concatenate(
            [rows_of(place, image_count, 1) for place in places_of(leaves, trees)], axis=0
        ),
        weights_ref,
    )
    images = [
        *row_groups(rows_of(low_place, 0, image_count)),
        *lane_tiles(image_ref[...]),
        *row_groups(rows_of(high_place, 0, image_count)),
        jnp.concatenate([coupled, jnp.zeros((VECS, LANES - rank), F32)], axis=1),
    ]
    windows = [
        *low_tiles,
        *lane_tiles(window),
        *high_tiles,
        window_coupled_ref[...],
    ]
    solved, record = orthogonalized(total, windows, images)
    record_ref[...] = record
    low_block, new_block, high_block = (
        jnp.concatenate(solved[at : at + per_row], axis=1)
        for at in range(0, 3 * per_row, per_row)
    )
    next_window = jnp.concatenate([window[VECS:], new_block], axis=0)
    next_window_ref[...] = next_window
    blocks = [block.astype(BF16) for block in (low_block, new_block, high_block)]
    near_part = near_field(blocks, choice_ref, near_ref)
    near_part_ref[...] = near_part
    far_part = jnp.dot(
        solved[-1][:, :rank].astype(BF16), u_ref[...], preferred_element_type=F32
    )
    skeleton, coarse = mapped(new_block.astype(BF16), maps_ref)
    width = LANES // VECS
    packed = one_row(product_lanes(next_window, near_part + far_part, width))
    tree_rows = jnp.concatenate([one_row(skeleton), packed], axis=0)
    level_rows = jnp.concatenate([one_row(coarse), packed], axis=0)

    def store(slot, at):
        slots_ref[slot] = level_rows

    over_slots(slots, store)

    def store_tree(leaf, at):
        slots_ref[own_tree * leaves + leaf] = tree_rows

    over_slots(leaves, store_tree)


def end_kernel(
    trees,
    rows_all,
    arrived_ref,
    flat_ref,
    window_ref,
    near_part_ref,
    weights_ref,
    u_ref,
    first_ref,
    block_ref,
    records_ref,
):
    leaves = arrived_ref.shape[0] // trees
    rows = jnp.concatenate(
        [arrived_ref[place, 0:1, :] for place in places_of(leaves, trees)], axis=0
    )
    coupled = couple_rows(rows, weights_ref)
    far_part = jnp.dot(coupled.astype(BF16), u_ref[...], preferred_element_type=F32)
    step = flat_ref.shape[0] // arrived_ref.shape[0] * VECS
    total = flat_ref[0:step]
    for at in range(step, flat_ref.shape[0], step):
        total = total + flat_ref[at : at + step]
    total = sum(total[at : at + 1] for at in range(1, step, step // VECS))
    total = total * (1.0 / rows_all)
    solved, record = orthogonalized(
        total,
        lane_tiles(window_ref[...]),
        lane_tiles(near_part_ref[...]),
        lane_tiles(far_part),
    )
    store_rows(block_ref, jnp.concatenate(solved, axis=1))
    used = records_ref.shape[2]
    records_ref[0] = first_ref[:, :used]
    records_ref[1] = record[:, :used]


def call(kernel, name, outs, ins, places, scratch=(), vmem=16 << 20, bytes_accessed=1 << 20):
    spaces = {"s": pltpu.SMEM, "v": pltpu.VMEM, "h": pltpu.HBM}
    return pl.pallas_call(
        kernel,
        name=name,
        out_shape=[jax.ShapeDtypeStruct(shape, dtype) for shape, dtype in outs],
        in_specs=[pl.BlockSpec(memory_space=spaces[place]) for place in places],
        out_specs=[pl.BlockSpec(memory_space=pltpu.VMEM)] * len(outs),
        scratch_shapes=list(scratch),
        cost_estimate=pl.CostEstimate(flops=0, bytes_accessed=bytes_accessed, transcendentals=0),
        compiler_params=pltpu.CompilerParams(vmem_limit_bytes=vmem),
    )(*ins)


def exchange(slots):
    return lax.all_to_all(slots, AXES, 0, 0, tiled=True)


def local(
    krylov_basis,
    near_block,
    near_col,
    near_count,
    far_col,
    v_basis,
    u_basis,
    far_coupling,
    transfer,
    top_coupling,
):
    basis, _, size = krylov_basis.shape
    trees = lax.axis_size("lvl")
    leaves = lax.axis_size("clus")
    devices = leaves * trees
    rows_all = float(devices * size)
    flat_basis = krylov_basis.reshape(-1, LANES)
    v_own, u_own, transfer_own = v_basis[0, 0], u_basis[0, 0], transfer[0, 0]
    rank = v_own.shape[0]
    far_own, top_own, near_own = far_coupling[0, 0], top_coupling[0, 0], near_block[0, 0]
    image_like = ((VECS, size), F32)
    window_like = ((basis, size), F32)
    per_slot = VECS * size // LANES + 3
    record_like = ((VECS, LANES), F32)
    maps_like = ((4 * rank, size), BF16)
    choice_like = ((-(-3 * near_own.shape[0] // 8) * 8, LANES), F32)
    weights_like = ((3, rank, (leaves + trees - 2) * LANES), BF16)
    (slots,) = call(
        functools.partial(begin_kernel, leaves),
        "begin",
        [((devices, VECS, size + 2 * LANES), BF16)],
        [flat_basis, v_own, transfer_own],
        "hhh",
        [
            pltpu.VMEM(flat_basis.shape, F32),
            pltpu.VMEM(v_own.shape, BF16),
            pltpu.VMEM(transfer_own.shape, F32),
            pltpu.SemaphoreType.DMA((3,)),
        ],
        vmem=None,
    )
    arrived = exchange(slots)
    weights, near_here, maps, choice = call(
        functools.partial(prepare_kernel, leaves),
        "prepare",
        [weights_like, (near_own.shape, BF16), maps_like, choice_like],
        [near_col, near_count, far_col, near_own, far_own, v_own, transfer_own, top_own],
        "ssshvvvv",
        [pltpu.SemaphoreType.DMA],
    )
    image, slots, window_coupled = call(
        functools.partial(first_kernel, trees),
        "first",
        [image_like, ((devices * per_slot, LANES), F32), ((basis, LANES), F32)],
        [
            arrived,
            flat_basis,
            weights,
            near_here,
            choice,
            u_own,
            maps,
        ],
        "v" * 7,
    )
    arrived = exchange(slots.reshape(devices, 1, per_slot * LANES))
    slots, window, near_part, record = call(
        functools.partial(middle_kernel, trees, rows_all),
        "middle",
        [((devices, 2, LANES), F32), window_like, image_like, record_like],
        [
            arrived,
            arrived.reshape(-1, LANES),
            flat_basis,
            image,
            window_coupled,
            weights,
            near_here,
            choice,
            u_own,
            maps,
        ],
        "v" * 10,
    )
    arrived = exchange(slots)
    block, records = call(
        functools.partial(end_kernel, trees, rows_all),
        "end",
        [((VECS * size // LANES, LANES), F32), ((STEPS, VECS, basis + VECS), F32)],
        [arrived, arrived.reshape(-1, LANES), window, near_part, weights, u_own, record],
        "v" * 7,
    )
    return (block.reshape(VECS, 1, size), jnp.transpose(records, (0, 2, 1)))


def solution(mesh):
    return jax.shard_map(
        local,
        mesh=mesh,
        in_specs=(
            P(None, "lvl", "clus"),
            P("lvl", "clus", None, None, None),
            P("lvl", "clus", None),
            P("lvl", "clus"),
            P("lvl", "clus", None),
            P("lvl", "clus", None, None),
            P("lvl", "clus", None, None),
            P("lvl", "clus", None, None, None),
            P("lvl", "clus", None, None),
            P("lvl", "clus", None, None, None),
        ),
        out_specs=(P(None, "lvl", "clus"), P()),
        check_vma=False,
    )
```
